256 devices in a mesh: gx: 8 (over z), yz: 32 (over x, y, core).
Axes of the slice: x: 4, y: 4, z: 8, core: 2. Of those that a mesh axis runs over, the one named last changes fastest.
Arguments:
- camera_accel: float32 [8, 2048, 3, 16, 128], P('gx', 'yz'), may hold values from -8 to 8
- camera_weight: float32 [8, 2048, 16, 128], P('gx', 'yz'), may hold values from 0.25 to 4
- brick_slot: int32 [8, 2048], P('gx', 'yz'), may hold values from 0 to 2047, as said below
- brick_solid: int32 [8, 2048], P('gx', 'yz'), may hold values from 0 to 1, as said below
Outputs:
- solution: float32 [32, 1024, 1024], P('yz', 'gx')
- residual: float32 [32, 1024, 1024], P('yz', 'gx')
The draws below stay inside these ranges and needn't reach their ends.
Inputs may be any that keep to these rules, and one draw needn't show every extreme that they name: `brick_slot`: row g lists each in-slab brick number of slab g once; entries j * 64 to (j + 1) * 64 - 1 are the bricks that camera owner j holds; brick number i belongs to solver owner i // 64. One camera owner holds at most 3 bricks of one solver owner, and exactly 3 of some in every slab. `brick_solid`: 1 marks a solid brick, numbered as in brick_slot; every slab has solid and fluid bricks.
All inputs are finite; a program needn't handle non-finite values.
Results may differ from the reference program's by a relative error of at most 0.00024.
Values sent between devices are 32-bit elements; how exact they have to be, the bound alone decides.
No kernel may reach another device: no remote copies, remote signals or barrier semaphores. Data moves between devices by JAX's collectives and lax.ppermute only.
A program may use at most 128 MiB of HBM per device.

```python
import math
import jax
import jax.numpy as jnp
from jax import lax

NX = 1024
NY = 1024
ZL = 1
BR = 16
B = 128
ITERS = 2
XL = 128
NZ = 32
BPD = 64
N_GX = 8
N_YZ = 32


def draw_camera_accel(key, part):
    shape = (N_GX, N_YZ * BPD, 3, ZL * BR, B)
    values = jax.random.normal(key, shape, jnp.float32)
    return jnp.clip(values, -8.0, 8.0)


def draw_brick_slot(key, part):
    owner_count = N_YZ
    slot_count = BPD
    base_load = slot_count // owner_count
    swing = base_load // 2

    def shuffle_slots(owner_key):
        return jax.random.permutation(owner_key, slot_count).astype(jnp.int32)

    def one_slab(slab_key):
        split_keys = jax.random.split(slab_key, 3)
        raised = jax.random.permutation(split_keys[0], owner_count).astype(jnp.int32)
        lowered = jnp.roll(raised, -1)
        owner_ids = jnp.arange(owner_count, dtype=jnp.int32)
        counts = base_load + swing * (raised[:, None] == owner_ids[None, :]).astype(jnp.int32)
        counts = counts - swing * (lowered[:, None] == owner_ids[None, :]).astype(jnp.int32)
        start_owner = jnp.cumsum(counts, axis=0) - counts
        end_camera = jnp.cumsum(counts, axis=1)
        start_camera = end_camera - counts
        local_order = jax.vmap(shuffle_slots)(jax.random.split(split_keys[1], owner_count))
        slot_ids = jnp.arange(slot_count, dtype=jnp.int32)
        owner_of = jnp.sum((end_camera[:, None, :] <= slot_ids[None, :, None]).astype(jnp.int32), axis=2)
        within = slot_ids[None, :] - jnp.take_along_axis(start_camera, owner_of, axis=1)
        offset = jnp.take_along_axis(start_owner, owner_of, axis=1) + within
        local_ids = local_order[owner_of, offset]
        brick_ids = owner_of * slot_count + local_ids
        camera_perm = jax.vmap(shuffle_slots)(jax.random.split(split_keys[2], owner_count))
        brick_ids = jnp.take_along_axis(brick_ids, camera_perm, axis=1)
        return brick_ids.reshape(owner_count * slot_count).astype(jnp.int32)
    return jax.vmap(one_slab)(jax.random.split(key, N_GX))


def draw_brick_solid(key, part):
    x_bricks = NX // N_GX // BR
    y_bricks = NY // B
    z_span = max(1, N_YZ // 2)
    x_span = max(1, x_bricks // 2)
    y_span = max(1, y_bricks // 2)

    def one_slab(slab_key):
        split_keys = jax.random.split(slab_key, 3)
        z_first = jax.random.randint(split_keys[0], (), 0, N_YZ - z_span + 1)
        x_first = jax.random.randint(split_keys[1], (), 0, x_bricks - x_span + 1)
        y_first = jax.random.randint(split_keys[2], (), 0, y_bricks - y_span + 1)
        brick_ids = jnp.arange(N_YZ * BPD, dtype=jnp.int32)
        z_brick = brick_ids // BPD
        x_brick = brick_ids % BPD // y_bricks
        y_brick = brick_ids % y_bricks
        inside = (z_brick >= z_first) & (z_brick < z_first + z_span)
        inside = inside & (x_brick >= x_first) & (x_brick < x_first + x_span)
        inside = inside & (y_brick >= y_first) & (y_brick < y_first + y_span)
        return inside.astype(jnp.int32)
    return jax.vmap(one_slab)(jax.random.split(key, N_GX))


def block_scale(stream_key, dims, cuts, low, high):
    loudness, own = 1.0, jax.random.fold_in(stream_key, 6)
    for dim, shards_of in cuts:
        heights = jnp.exp(jax.random.uniform(jax.random.fold_in(own, dim), (shards_of,), jnp.float32, low / len(cuts), high / len(cuts)))
        loudness = loudness * jnp.repeat(heights, dims[dim] // shards_of).reshape([-1 if axis == dim else 1 for axis in range(len(dims))])
    return loudness


def setup_inputs(seed: int = 0) -> dict:
    seeds = jax.random.split(jax.random.key(seed), 5)
    return {
        "camera_accel": draw_camera_accel(jax.random.fold_in(seeds[4], 71), 0),
        "camera_weight": jnp.clip(jnp.exp(math.log(4.0) - 2.7725887 * jax.random.uniform(seeds[1], (N_GX, N_YZ * BPD, ZL * BR, B), jnp.float32) ** block_scale(seeds[1], (N_GX, N_YZ * BPD, ZL * BR, B), ((0, 8), (1, 32)), -0.2, 0.2)), 0.25, 4.0),
        "brick_slot": draw_brick_slot(jax.random.fold_in(seeds[4], 71), 0),
        "brick_solid": draw_brick_solid(jax.random.fold_in(seeds[4], 71), 0),
    }


shift_rate = 0.05
spectral_gain = 1.0
spectral_floor = 2.0
highest = lax.Precision.HIGHEST

def cosine_table(length, row_start, row_count, col_start, col_count):
    row_ids = row_start + jnp.arange(row_count, dtype=jnp.int32)
    col_ids = col_start + jnp.arange(col_count, dtype=jnp.int32)
    phases = jnp.remainder(row_ids[:, None] * (2 * col_ids[None, :] + 1), 4 * length).astype(jnp.float32)
    angles = phases * (jnp.pi / (2.0 * length))
    norm_scale = jnp.where(row_ids == 0, 1.0 / length, 2.0 / length).astype(jnp.float32)
    return jnp.sqrt(norm_scale)[:, None] * jnp.cos(angles)

def eigen_values(length, first_mode, mode_count):
    modes = (first_mode + jnp.arange(mode_count, dtype=jnp.int32)).astype(jnp.float32)
    return 2.0 - 2.0 * jnp.cos(modes * (jnp.pi / length))

def to_grid(bricks):
    channels = bricks.shape[2]
    shaped = bricks.reshape(N_GX, N_YZ, XL // BR, NY // B, channels, ZL, BR, B)
    shaped = jnp.transpose(shaped, (4, 1, 5, 0, 2, 6, 3, 7))
    return shaped.reshape(channels, NZ, NX, NY)

def next_cell(values_in, axis_index):
    padding = [(0, 0), (0, 0), (0, 0)]
    padding[axis_index] = (0, 1)
    return lax.slice_in_dim(jnp.pad(values_in, padding), 1, values_in.shape[axis_index] + 1, axis=axis_index)

def prev_cell(values_in, axis_index):
    padding = [(0, 0), (0, 0), (0, 0)]
    padding[axis_index] = (1, 0)
    return lax.slice_in_dim(jnp.pad(values_in, padding), 0, values_in.shape[axis_index], axis=axis_index)

def reference(camera_accel, camera_weight, brick_slot, brick_solid):
    fluid_bricks = (1 - brick_solid).astype(jnp.float32)

    def place(values_in, brick_ids):
        return jnp.zeros_like(values_in).at[brick_ids].set(values_in)
    brick_mask = fluid_bricks[:, :, None, None, None]
    accel = to_grid(jax.vmap(place)(camera_accel, brick_slot) * brick_mask)
    weight = to_grid(jax.vmap(place)(camera_weight[:, :, None], brick_slot) * brick_mask)[0]
    fluid = to_grid(jnp.broadcast_to(brick_mask, (N_GX, N_YZ * BPD, 1, ZL * BR, B)))[0]
    face_list = []
    for axis_index in range(3):
        face_list.append(jnp.sqrt(weight * next_cell(weight, axis_index)))
    diagonal = shift_rate * weight + (1.0 - fluid)
    source_term = jnp.zeros_like(weight)
    for axis_index in range(3):
        face_flux = face_list[axis_index] * (accel[axis_index] + next_cell(accel[axis_index], axis_index)) * 0.5
        source_term = source_term + prev_cell(face_flux, axis_index) - face_flux
        diagonal = diagonal + face_list[axis_index] + prev_cell(face_list[axis_index], axis_index)

    def operate(values_in):
        result = diagonal * values_in
        for axis_index in range(3):
            result = result - face_list[axis_index] * next_cell(values_in, axis_index)
            result = result - prev_cell(face_list[axis_index], axis_index) * prev_cell(values_in, axis_index)
        return result
    table_x = cosine_table(NX, 0, NX, 0, NX)
    table_y = cosine_table(NY, 0, NY, 0, NY)
    denom = spectral_gain * (eigen_values(NX, 0, NX)[:, None] + eigen_values(NY, 0, NY)[None, :]) + spectral_floor

    def precondition(values_in):
        spectrum = jnp.einsum('zxy,ky->zxk', values_in, table_y, precision=highest)
        spectrum = jnp.einsum('kx,zxy->zky', table_x, spectrum, precision=highest)
        spectrum = spectrum / denom[None]
        spatial = jnp.einsum('kx,zky->zxy', table_x, spectrum, precision=highest)
        spatial = jnp.einsum('zxk,ky->zxy', spatial, table_y, precision=highest)
        return fluid * spatial
    solution = jnp.zeros_like(source_term)
    residual = source_term
    update = precondition(residual)
    energy_now = jnp.sum(residual * update)
    direction = update
    for step_index in range(ITERS):
        image_of = operate(direction)
        step_size = energy_now / jnp.sum(direction * image_of)
        solution = solution + step_size * direction
        residual = residual - step_size * image_of
        if step_index + 1 < ITERS:
            update = precondition(residual)
            energy_next = jnp.sum(residual * update)
            direction = update + energy_next / energy_now * direction
            energy_now = energy_next
    return (solution, residual)
```

```python
import functools

import jax
import jax.numpy as jnp
import ml_dtypes
import numpy as np
from jax import lax
from jax.experimental import pallas as pl
from jax.experimental.pallas import tpu as pltpu
from jax.sharding import Mesh
from jax.sharding import PartitionSpec as P

N = 1024
H = N // 2
XL = 128
SLABS = 8
BR = 16
B = 128
PLANE_BRICKS = 64
OWNERS = 32
PER_PAIR = 3
BRICK_ROWS = 4 * BR
PAIR_ROWS = PER_PAIR * BRICK_ROWS
SEND_ROWS = PAIR_ROWS + 8
YZ = ("yz_0", "yz_1", "yz_2")
SHIFT_RATE = 0.05
FLOOR = 2.0
F32 = jnp.float32
BF16 = jnp.bfloat16
VMEM = pl.BlockSpec(memory_space=pltpu.VMEM)
SMEM = pl.BlockSpec(memory_space=pltpu.SMEM)
ANY = pl.BlockSpec(memory_space=pl.ANY)


def cosine_rows(length):
    k = np.arange(length, dtype=np.int64)[:, None]
    i = np.arange(length, dtype=np.int64)[None, :]
    m = (k * (2 * i + 1)) % (4 * length)
    scale = np.sqrt(np.where(k == 0, 1.0, 2.0) / length)
    return scale * np.cos(np.pi * m / (2.0 * length))


def two_bf16(table):
    high = table.astype(np.float32).astype(ml_dtypes.bfloat16)
    low = (table - high.astype(np.float64)).astype(np.float32).astype(ml_dtypes.bfloat16)
    return high, low


@functools.lru_cache(None)
def tables():
    out = {}
    big = cosine_rows(N)
    out["even"] = np.stack(two_bf16(big[0::2, :H]))
    out["odd"] = np.stack(two_bf16(big[1::2, :H]))
    small = cosine_rows(XL)
    out["small"] = np.concatenate(two_bf16(small), axis=0)
    out["small_t"] = np.concatenate(two_bf16(small.T.copy()), axis=0)
    lam_x = 2.0 - 2.0 * np.cos(np.pi * np.arange(XL) / XL)
    ky = np.concatenate([np.arange(0, N, 2), np.arange(1, N, 2)])
    lam_y = 2.0 - 2.0 * np.cos(np.pi * ky / N)
    column = np.zeros((XL, 128), np.float32)
    column[:, 0] = lam_x + FLOOR
    column[:, 1] = small[:, 0]
    column[:, 2] = small[:, XL - 1]
    out["column"] = column
    out["lam_y"] = lam_y.astype(np.float32)[None]
    denom = lam_x[:, None] + lam_y[None] + FLOOR
    near = np.sum(small[:, :1] ** 2 / denom, axis=0)
    far = np.sum(small[:, :1] * small[:, XL - 1 :] / denom, axis=0)
    cuts = SLABS - 1
    system = np.zeros((N, cuts, cuts))
    for j in range(cuts):
        system[:, j, j] = 1.0 + 2.0 * near
    for j in range(cuts - 1):
        system[:, j, j + 1] = -far
        system[:, j + 1, j] = -far
    inverse = np.linalg.inv(system)
    joined = np.zeros((SLABS + 3, SLABS, 2, N))
    for i in range(cuts):
        for j in range(cuts):
            joined[i + 2, j, 1] += inverse[:, i, j]
            joined[i + 2, j + 1, 0] -= inverse[:, i, j]
    out["cut"] = joined.astype(np.float32).reshape(SLABS + 3, SLABS, 16, 128)
    out["ends"] = np.stack([near, far]).astype(np.float32).reshape(2, 8, 128)
    return out


def split(value):
    high = value.astype(BF16)
    return high, (value - high.astype(F32)).astype(BF16)


def product(a, b, transposed=False):
    dims = (((1,), (1 if transposed else 0,)), ((), ()))
    return lax.dot_general(a, b, dims, preferred_element_type=F32)


def by_table(data, table_ref, transposed):
    high, low = split(data)
    rows = data.shape[0]
    both = product(jnp.concatenate([high, low], axis=0), table_ref[0], transposed)
    return both[:rows] + both[rows:] + product(high, table_ref[1], transposed)


def of_table(table_ref, data):
    high, low = split(data)
    both = product(table_ref[...], high)
    return both[:XL] + both[XL:] + product(table_ref[:XL], low)


def mirrored(value):
    rows, width = value.shape
    index = 127 - lax.broadcasted_iota(jnp.int32, (rows, 128), 1)
    tiles = [
        jnp.take_along_axis(value[:, t * 128 : (t + 1) * 128], index, axis=1)
        for t in range(width // 128)
    ]
    return jnp.concatenate(tiles[::-1], axis=1)


def as_tile(row):
    return jnp.concatenate([row[:, t * 128 : (t + 1) * 128] for t in range(8)], axis=0)


def as_row(tile):
    return jnp.concatenate([tile[t : t + 1] for t in range(8)], axis=1)


def to_modes(field_ref, even_ref, odd_ref, small_ref, column_ref, lam_ref, fold_ref, modes_ref, ends_ref):
    for i in range(XL // 8):
        rows = pl.ds(8 * i, 8)
        low = field_ref[rows, :H]
        high = mirrored(field_ref[rows, H:])
        fold_ref[rows, :H] = low + high
        fold_ref[rows, H:] = low - high
    spectrum = jnp.concatenate(
        [
            by_table(fold_ref[:, :H], even_ref, True),
            by_table(fold_ref[:, H:], odd_ref, True),
        ],
        axis=1,
    )
    modes_ref[...] = of_table(small_ref, spectrum)
    first = jnp.zeros((8, N), F32)
    last = jnp.zeros((8, N), F32)
    for i in range(XL // 8):
        rows = pl.ds(8 * i, 8)
        modes = modes_ref[rows, :] / (column_ref[rows, 0:1] + lam_ref[...])
        modes_ref[rows, :] = modes
        first = first + modes * column_ref[rows, 1:2]
        last = last + modes * column_ref[rows, 2:3]
    first = as_tile(jnp.sum(first, axis=0, keepdims=True))
    last = as_tile(jnp.sum(last, axis=0, keepdims=True))
    for j in range(SLABS):
        ends_ref[j, 0:8] = first
        ends_ref[j, 8:16] = last


def pack_kernel(slot_ref, accel_ref, weight_ref, out_ref, count_ref, sem):
    for o in range(OWNERS):
        count_ref[o] = 0
    out_ref[:, PAIR_ROWS:] = jnp.full((OWNERS, 8, 128), -1.0, F32)

    def one(s, carry):
        brick = slot_ref[s]
        owner = brick // PLANE_BRICKS
        place = count_ref[owner]
        count_ref[owner] = place + 1
        number = jnp.full((1, 128), brick - owner * PLANE_BRICKS, jnp.int32)
        out_ref[owner, pl.ds(PAIR_ROWS + place, 1), :] = number.astype(F32)
        at = pl.multiple_of(place * BRICK_ROWS, 16)
        pltpu.make_async_copy(accel_ref.at[s], out_ref.at[owner, pl.ds(at, 3 * BR)], sem).start()
        pltpu.make_async_copy(weight_ref.at[s], out_ref.at[owner, pl.ds(at + 3 * BR, BR)], sem).start()
        return carry

    lax.fori_loop(0, PLANE_BRICKS, one, 0)
    sent = out_ref.at[:, pl.ds(0, PLANE_BRICKS * BRICK_ROWS // OWNERS)]
    pltpu.make_async_copy(sent, sent, sem).wait()


def place_kernel(ids_ref, solid_ref, got_ref, fields_ref, first_ref, last_ref, sem):
    def one(s, carry):
        brick = ids_ref[s]

        @pl.when(brick >= 0)
        def _():
            x_at = pl.multiple_of((brick // 8) * BR, BR)
            y_at = pl.multiple_of((brick % 8) * B, B)
            source = s // PER_PAIR
            row = (s % PER_PAIR) * BRICK_ROWS
            for channel in range(4):
                at = pl.multiple_of(row + channel * BR, BR)
                pltpu.make_async_copy(
                    got_ref.at[source, pl.ds(at, BR)],
                    fields_ref.at[channel, pl.ds(x_at, BR), pl.ds(y_at, B)],
                    sem,
                ).start()

        return carry

    lax.fori_loop(0, OWNERS * PER_PAIR, one, 0)
    pltpu.make_async_copy(fields_ref, fields_ref, sem).wait()
    for i in range(PLANE_BRICKS):
        fluid = (1 - solid_ref[i]).astype(F32)
        rows = pl.ds((i // 8) * BR, BR)
        cols = pl.ds((i % 8) * B, B)
        for channel in range(4):
            fields_ref[channel, rows, cols] = fields_ref[channel, rows, cols] * fluid
    for ref, row in ((first_ref, 0), (last_ref, XL - 1)):
        ref[0:1] = fields_ref[3, row : row + 1]
        ref[1:2] = fields_ref[1, row : row + 1]


def setup_kernel(
    fields_ref, above_ref, below_ref, xlo_ref, xhi_ref, even_ref, odd_ref, small_ref, column_ref, lam_ref,
    faces_ref, source_ref, modes_ref, ends_ref, wext_ref, aext_ref, fold_ref,
):
    for ref, channel, row in ((wext_ref, 3, 0), (aext_ref, 1, 1)):
        ref[7:8] = xlo_ref[row : row + 1]
        ref[XL + 8 : XL + 9] = xhi_ref[row : row + 1]
        ref[8 : XL + 8] = fields_ref[channel]
    inner = lax.broadcasted_iota(jnp.int32, (8, N), 1) < N - 1
    for i in range(XL // 8):
        rows = pl.ds(8 * i, 8)
        weight = fields_ref[3, rows]
        accel_z = fields_ref[0, rows]
        accel_x = fields_ref[1, rows]
        accel_y = fields_ref[2, rows]
        face_zp = jnp.sqrt(weight * above_ref[1, rows])
        face_zm = jnp.sqrt(weight * below_ref[1, rows])
        face_xp = jnp.sqrt(weight * wext_ref[pl.ds(8 * i + 9, 8)])
        face_xm = jnp.sqrt(weight * wext_ref[pl.ds(8 * i + 7, 8)])
        face_yp = jnp.where(inner, jnp.sqrt(weight * pltpu.roll(weight, N - 1, 1)), 0.0)
        face_ym = pltpu.roll(face_yp, 1, 1)
        diagonal = SHIFT_RATE * weight + jnp.where(weight > 0.0, 0.0, 1.0)
        diagonal = diagonal + face_zp + face_zm + face_xp + face_xm + face_yp + face_ym
        flux = face_zm * (below_ref[0, rows] + accel_z) - face_zp * (accel_z + above_ref[0, rows])
        flux = flux + face_xm * (aext_ref[pl.ds(8 * i + 7, 8)] + accel_x)
        flux = flux - face_xp * (accel_x + aext_ref[pl.ds(8 * i + 9, 8)])
        flux_y = face_yp * (accel_y + pltpu.roll(accel_y, N - 1, 1))
        flux = flux + pltpu.roll(flux_y, 1, 1) - flux_y
        source_ref[rows] = 0.5 * flux
        for k, face in enumerate((face_zp, face_zm, face_xp, face_xm, face_yp, face_ym, diagonal)):
            faces_ref[k, rows] = face
    to_modes(source_ref, even_ref, odd_ref, small_ref, column_ref, lam_ref, fold_ref, modes_ref, ends_ref)


def update_kernel(
    slab_ref, modes_ref, all_ends_ref, fields_ref, cut_ref, near_far_ref, even_ref, odd_ref, small_t_ref,
    column_ref, lam_ref, update_ref, rim_ref, work_ref,
):
    slab = slab_ref[0]

    def jump(m):
        total = jnp.zeros((16, 128), F32)
        for j in range(SLABS):
            total = total + cut_ref[slab + m, j] * all_ends_ref[j]
        return total[:8] + total[8:]

    farther_low, low, high, farther_high = (jump(m) for m in range(4))
    near, far = near_far_ref[0], near_far_ref[1]
    before = all_ends_ref[jnp.maximum(slab - 1, 0), 8:16] - (near * low - far * farther_low)
    after = all_ends_ref[jnp.minimum(slab + 1, SLABS - 1), 0:8] - (far * farther_high - near * high)
    low_row, high_row = as_row(low), as_row(high)
    for i in range(XL // 8):
        rows = pl.ds(8 * i, 8)
        change = column_ref[rows, 2:3] * high_row - column_ref[rows, 1:2] * low_row
        work_ref[rows] = modes_ref[rows] - change / (column_ref[rows, 0:1] + lam_ref[...])
    work_ref[0:XL] = of_table(small_t_ref, work_ref[0:XL])
    work_ref[XL : XL + 8] = jnp.concatenate([as_row(before), as_row(after), jnp.zeros((6, N), F32)], axis=0)
    even = by_table(work_ref[:, :H], even_ref, False)
    odd = by_table(work_ref[:, H:], odd_ref, False)
    work_ref[:, :H] = even
    work_ref[:, H:] = odd
    for i in range(XL // 8 + 1):
        rows = pl.ds(8 * i, 8)
        even = work_ref[rows, :H]
        odd = work_ref[rows, H:]
        value = jnp.concatenate([even + odd, mirrored(even - odd)], axis=1)
        if i < XL // 8:
            update_ref[rows] = jnp.where(fields_ref[3, rows] > 0.0, value, 0.0)
        else:
            rim_ref[...] = value


def image_rows(i, value_ref, above_ref, below_ref, faces_ref, ext_ref):
    rows = pl.ds(8 * i, 8)
    value = value_ref[rows]
    image = faces_ref[6, rows] * value
    image = image - (faces_ref[0, rows] * above_ref[rows] + faces_ref[1, rows] * below_ref[rows])
    image = image - (faces_ref[2, rows] * ext_ref[pl.ds(8 * i + 9, 8)] + faces_ref[3, rows] * ext_ref[pl.ds(8 * i + 7, 8)])
    image = image - (faces_ref[4, rows] * pltpu.roll(value, N - 1, 1) + faces_ref[5, rows] * pltpu.roll(value, 1, 1))
    return value, image


def extend(value_ref, rim_ref, ext_ref):
    ext_ref[7:8] = rim_ref[0:1]
    ext_ref[XL + 8 : XL + 9] = rim_ref[1:2]
    ext_ref[8 : XL + 8] = value_ref[...]


def image_kernel(
    value_ref, rim_ref, above_ref, below_ref, faces_ref, even_ref, odd_ref, small_ref, column_ref, lam_ref,
    image_ref, modes_ref, ends_ref, ext_ref, fold_ref,
):
    extend(value_ref, rim_ref, ext_ref)
    for i in range(XL // 8):
        image_ref[pl.ds(8 * i, 8)] = image_rows(i, value_ref, above_ref, below_ref, faces_ref, ext_ref)[1]
    to_modes(image_ref, even_ref, odd_ref, small_ref, column_ref, lam_ref, fold_ref, modes_ref, ends_ref)


def sums_kernel(
    value_ref, rim_ref, above_ref, below_ref, faces_ref, source_ref, update_ref, first_image_ref,
    image_ref, sums_ref, ext_ref,
):
    extend(value_ref, rim_ref, ext_ref)
    totals = [jnp.zeros((8, N), F32) for _ in range(6)]
    for i in range(XL // 8):
        rows = pl.ds(8 * i, 8)
        v, t = image_rows(i, value_ref, above_ref, below_ref, faces_ref, ext_ref)
        image_ref[rows] = t
        r, u, q = source_ref[rows], update_ref[rows], first_image_ref[rows]
        for k, (a, b) in enumerate(((r, u), (u, q), (r, v), (q, v), (u, t), (v, t))):
            totals[k] = totals[k] + a * b
    lines = []
    for total in totals:
        line = jnp.sum(total, axis=0, keepdims=True)
        lines.append(sum(line[:, t * 128 : (t + 1) * 128] for t in range(8)))
    lines = jnp.concatenate(lines + [jnp.zeros((2, 128), F32)], axis=0)
    for j in range(OWNERS):
        sums_ref[j] = lines


def final_kernel(sums_ref, source_ref, u_ref, q_ref, v_ref, t_ref, solution_ref, residual_ref):
    total = sums_ref[0]
    for j in range(1, SLABS):
        total = total + sums_ref[j]
    total = jnp.sum(total, axis=1, keepdims=True)
    ru, uq, rv, qv, ut, vt = (total[k : k + 1] for k in range(6))
    step = ru / uq
    energy = ru - step * (rv + uq) + step * step * qv
    beta = energy / ru
    cross = uq - step * ut
    curve = cross - step * qv + step * step * vt
    curve = curve + beta * (cross + uq - step * qv) + beta * beta * uq
    second = energy / curve
    spread = lambda s: jnp.broadcast_to(s, (8, N))
    step, beta, second = spread(step), spread(beta), spread(second)
    for i in range(XL // 8):
        rows = pl.ds(8 * i, 8)
        u, q = u_ref[rows], q_ref[rows]
        direction = u - step * v_ref[rows] + beta * u
        along = q - step * t_ref[rows] + beta * q
        solution_ref[rows] = step * u + second * direction
        residual_ref[rows] = source_ref[rows] - step * q - second * along


def shape(*dims):
    return jax.ShapeDtypeStruct(dims, F32)


def call(kernel, out_shape, in_specs, out_specs, scratch=(), name=None):
    return pl.pallas_call(
        kernel, out_shape=out_shape, in_specs=in_specs, out_specs=out_specs, scratch_shapes=list(scratch), name=name
    )


PLANE = (XL, N)
EXT = pltpu.VMEM((XL + 16, N), F32)
FOLD = pltpu.VMEM(PLANE, F32)


def on_device(camera_accel, camera_weight, brick_slot, brick_solid):
    constant = {name: jnp.asarray(value) for name, value in tables().items()}
    dct = (constant["even"], constant["odd"])
    slab_tables = (constant["column"], constant["lam_y"])
    forward = dct + (constant["small"],) + slab_tables
    slab = lax.axis_index("gx")
    slabs, owners = lax.axis_size("gx"), lax.axis_size(YZ)
    up_z = [(i, i + 1) for i in range(owners - 1)]
    down_z = [(b, a) for a, b in up_z]
    up_x = [(i, i + 1) for i in range(slabs - 1)]
    down_x = [(b, a) for a, b in up_x]

    send = call(
        pack_kernel,
        shape(OWNERS, SEND_ROWS, 128),
        [SMEM, ANY, ANY],
        VMEM,
        [pltpu.SMEM((OWNERS,), jnp.int32), pltpu.SemaphoreType.DMA],
        name="pack",
    )(brick_slot[0], camera_accel[0].reshape(PLANE_BRICKS, 3 * BR, B), camera_weight[0])
    got = lax.all_to_all(send, YZ, split_axis=0, concat_axis=0, tiled=True)
    ids = got[:, PAIR_ROWS : PAIR_ROWS + PER_PAIR, 0].astype(jnp.int32).reshape(-1)
    fields, first, last = call(
        place_kernel,
        (shape(4, *PLANE), shape(2, N), shape(2, N)),
        [SMEM, SMEM, ANY],
        (VMEM, VMEM, VMEM),
        [pltpu.SemaphoreType.DMA],
        name="place",
    )(ids, brick_solid[0], got)
    beside = fields[jnp.array([0, 3])]
    above = lax.ppermute(beside, YZ, down_z)
    below = lax.ppermute(beside, YZ, up_z)
    xlo = lax.ppermute(last, "gx", up_x)
    xhi = lax.ppermute(first, "gx", down_x)
    faces, source, modes, ends = call(
        setup_kernel,
        (shape(7, *PLANE), shape(*PLANE), shape(*PLANE), shape(SLABS, 16, 128)),
        [VMEM] * 10,
        (VMEM,) * 4,
        [EXT, EXT, FOLD],
        name="setup",
    )(fields, above, below, xlo, xhi, *forward)

    def updated(modes, ends):
        all_ends = lax.all_to_all(ends, "gx", split_axis=0, concat_axis=0, tiled=True)
        return call(
            update_kernel,
            (shape(*PLANE), shape(8, N)),
            [SMEM] + [VMEM] * 10,
            (VMEM, VMEM),
            [pltpu.VMEM((XL + 8, N), F32)],
            name="update",
        )(
            slab.reshape(1), modes, all_ends, fields, constant["cut"], constant["ends"],
            *dct, constant["small_t"], *slab_tables,
        )

    def neighbours(value):
        return lax.ppermute(value, YZ, down_z), lax.ppermute(value, YZ, up_z)

    u, rim = updated(modes, ends)
    q, modes, ends = call(
        image_kernel,
        (shape(*PLANE), shape(*PLANE), shape(SLABS, 16, 128)),
        [VMEM] * 10,
        (VMEM,) * 3,
        [EXT, FOLD],
        name="image",
    )(u, rim, *neighbours(u), faces, *forward)
    v, rim = updated(modes, ends)
    t, sums = call(
        sums_kernel,
        (shape(*PLANE), shape(OWNERS, 8, 128)),
        [VMEM] * 8,
        (VMEM, VMEM),
        [EXT],
        name="sums",
    )(v, rim, *neighbours(v), faces, source, u, q)
    sums = lax.all_to_all(sums, YZ, split_axis=0, concat_axis=0, tiled=True)
    sums = jnp.broadcast_to(jnp.sum(sums, axis=0)[None], (SLABS, 8, 128))
    sums = lax.all_to_all(sums, "gx", split_axis=0, concat_axis=0, tiled=True)
    result, residual = call(
        final_kernel, (shape(*PLANE), shape(*PLANE)), [VMEM] * 6, (VMEM, VMEM), name="final"
    )(sums, source, u, q, v, t)
    return result[None], residual[None]


def solution(mesh):
    finer = Mesh(mesh.devices.reshape(mesh.shape["gx"], 4, 4, 2), ("gx", "yz_0", "yz_1", "yz_2"))
    in_specs = (P("gx", YZ, None, None, None), P("gx", YZ, None, None), P("gx", YZ), P("gx", YZ))
    out_specs = (P(YZ, "gx", None), P(YZ, "gx", None))
    return jax.shard_map(
        on_device, mesh=finer, in_specs=in_specs, out_specs=out_specs, check_vma=False
    )
```

```python
import functools

import jax
import jax.numpy as jnp
import ml_dtypes
import numpy as np
from jax import lax
from jax.experimental import pallas as pl
from jax.experimental.pallas import tpu as pltpu
from jax.sharding import Mesh
from jax.sharding import PartitionSpec as P

N = 1024
H = N // 2
XL = 128
SLABS = 8
BR = 16
B = 128
PLANE_BRICKS = 64
OWNERS = 32
PER_PAIR = 3
BRICK_ROWS = 4 * BR
PAIR_ROWS = PER_PAIR * BRICK_ROWS
SEND_ROWS = PAIR_ROWS + 8
YZ = ("yz_0", "yz_1", "yz_2")
SHIFT_RATE = 0.05
FLOOR = 2.0
F32 = jnp.float32
BF16 = jnp.bfloat16
VMEM = pl.BlockSpec(memory_space=pltpu.VMEM)
SMEM = pl.BlockSpec(memory_space=pltpu.SMEM)
HBM = pl.BlockSpec(memory_space=pltpu.HBM)


def cosine_rows(length):
    k = np.arange(length, dtype=np.int64)[:, None]
    i = np.arange(length, dtype=np.int64)[None, :]
    m = (k * (2 * i + 1)) % (4 * length)
    scale = np.sqrt(np.where(k == 0, 1.0, 2.0) / length)
    return scale * np.cos(np.pi * m / (2.0 * length))


def two_bf16(table):
    high = table.astype(np.float32).astype(ml_dtypes.bfloat16)
    low = (table - high.astype(np.float64)).astype(np.float32).astype(ml_dtypes.bfloat16)
    return high, low


@functools.lru_cache(None)
def tables():
    out = {}
    big = cosine_rows(N)
    out["even"] = np.stack(two_bf16(big[0::2, :H]))
    out["odd"] = np.stack(two_bf16(big[1::2, :H]))
    small = cosine_rows(XL)
    out["small"] = np.concatenate(two_bf16(small), axis=0)
    out["small_t"] = np.concatenate(two_bf16(small.T.copy()), axis=0)
    lam_x = 2.0 - 2.0 * np.cos(np.pi * np.arange(XL) / XL)
    ky = np.concatenate([np.arange(0, N, 2), np.arange(1, N, 2)])
    lam_y = 2.0 - 2.0 * np.cos(np.pi * ky / N)
    column = np.zeros((XL, 128), np.float32)
    column[:, 0] = lam_x + FLOOR
    column[:, 1] = small[:, 0]
    column[:, 2] = small[:, XL - 1]
    out["column"] = column
    out["lam_y"] = lam_y.astype(np.float32)[None]
    denom = lam_x[:, None] + lam_y[None] + FLOOR
    near = np.sum(small[:, :1] ** 2 / denom, axis=0)
    far = np.sum(small[:, :1] * small[:, XL - 1 :] / denom, axis=0)
    cuts = SLABS - 1
    system = np.zeros((N, cuts, cuts))
    for j in range(cuts):
        system[:, j, j] = 1.0 + 2.0 * near
    for j in range(cuts - 1):
        system[:, j, j + 1] = -far
        system[:, j + 1, j] = -far
    inverse = np.linalg.inv(system)
    joined = np.zeros((SLABS + 3, SLABS, 2, N))
    for i in range(cuts):
        for j in range(cuts):
            joined[i + 2, j, 1] += inverse[:, i, j]
            joined[i + 2, j + 1, 0] -= inverse[:, i, j]
    out["cut"] = joined.astype(np.float32).reshape(SLABS + 3, SLABS, 16, 128)
    out["ends"] = np.stack([near, far]).astype(np.float32).reshape(2, 8, 128)
    return out


def split(value):
    high = value.astype(BF16)
    return high, (value - high.astype(F32)).astype(BF16)


def product(a, b, transposed=False):
    dims = (((1,), (1 if transposed else 0,)), ((), ()))
    return lax.dot_general(a, b, dims, preferred_element_type=F32)


def by_table(data, table_ref, transposed):
    high, low = split(data)
    rows = data.shape[0]
    both = product(jnp.concatenate([high, low], axis=0), table_ref[0], transposed)
    return both[:rows] + both[rows:] + product(high, table_ref[1], transposed)


def of_table(table_ref, data):
    high, low = split(data)
    both = product(table_ref[...], high)
    return both[:XL] + both[XL:] + product(table_ref[:XL], low)


def mirrored(value):
    rows, width = value.shape
    index = 127 - lax.broadcasted_iota(jnp.int32, (rows, 128), 1)
    tiles = [
        jnp.take_along_axis(value[:, t * 128 : (t + 1) * 128], index, axis=1)
        for t in range(width // 128)
    ]
    return jnp.concatenate(tiles[::-1], axis=1)


def as_tile(row):
    return jnp.concatenate([row[:, t * 128 : (t + 1) * 128] for t in range(8)], axis=0)


def as_row(tile):
    return jnp.concatenate([tile[t : t + 1] for t in range(8)], axis=1)


def to_modes(field_ref, even_ref, odd_ref, small_ref, column_ref, lam_ref, fold_ref, modes_ref, ends_ref):
    for i in range(XL // 8):
        rows = pl.ds(8 * i, 8)
        low = field_ref[rows, :H]
        high = mirrored(field_ref[rows, H:])
        fold_ref[rows, :H] = low + high
        fold_ref[rows, H:] = low - high
    spectrum = jnp.concatenate(
        [
            by_table(fold_ref[:, :H], even_ref, True),
            by_table(fold_ref[:, H:], odd_ref, True),
        ],
        axis=1,
    )
    modes_ref[...] = of_table(small_ref, spectrum)
    first = jnp.zeros((8, N), F32)
    last = jnp.zeros((8, N), F32)
    for i in range(XL // 8):
        rows = pl.ds(8 * i, 8)
        modes = modes_ref[rows, :] / (column_ref[rows, 0:1] + lam_ref[...])
        modes_ref[rows, :] = modes
        first = first + modes * column_ref[rows, 1:2]
        last = last + modes * column_ref[rows, 2:3]
    first = as_tile(jnp.sum(first, axis=0, keepdims=True))
    last = as_tile(jnp.sum(last, axis=0, keepdims=True))
    for j in range(SLABS):
        ends_ref[j, 0:8] = first
        ends_ref[j, 8:16] = last


def pack_kernel(place_ref, slot_ref, accel_ref, weight_ref, out_ref, count_ref, sem):
    del place_ref
    for o in range(OWNERS):
        count_ref[o] = 0
    out_ref[:, PAIR_ROWS:] = jnp.full((OWNERS, 8, 128), -1.0, F32)
    lane = lax.broadcasted_iota(jnp.int32, (1, 128), 1)

    def one(s, carry):
        brick = slot_ref[s]
        owner = brick // PLANE_BRICKS
        place = count_ref[owner]
        count_ref[owner] = place + 1
        number = (brick - owner * PLANE_BRICKS).astype(F32)
        line = out_ref[owner, PAIR_ROWS : PAIR_ROWS + 1, :]
        out_ref[owner, PAIR_ROWS : PAIR_ROWS + 1, :] = jnp.where(lane == place, number, line)
        at = pl.multiple_of(place * BRICK_ROWS, BRICK_ROWS)
        pltpu.make_async_copy(accel_ref.at[s], out_ref.at[owner, pl.ds(at, 3 * BR)], sem).start()
        pltpu.make_async_copy(weight_ref.at[s], out_ref.at[owner, pl.ds(at + 3 * BR, BR)], sem).start()
        return carry

    lax.fori_loop(0, PLANE_BRICKS, one, 0)
    sent = out_ref.at[:, pl.ds(0, PLANE_BRICKS * BRICK_ROWS // OWNERS)]
    pltpu.make_async_copy(sent, sent, sem).wait()


def place_kernel(solid_ref, got_ref, z_ref, xy_ref, first_ref, last_ref, ids_ref, sem):
    ids_copy = pltpu.make_async_copy(got_ref.at[:, pl.ds(PAIR_ROWS, 1)], ids_ref, sem)
    ids_copy.start()
    ids_copy.wait()

    def one(source, carry):
        for place in range(PER_PAIR):
            brick = ids_ref[source, 0, place].astype(jnp.int32)

            @pl.when(brick >= 0)
            def _():
                fluid = (1 - solid_ref[brick]).astype(F32)
                x_at = pl.multiple_of((brick // 8) * BR, BR)
                y_at = pl.multiple_of((brick % 8) * B, B)
                for channel, (ref, at) in enumerate(((z_ref, 0), (xy_ref, 0), (xy_ref, 1), (z_ref, 1))):
                    row = place * BRICK_ROWS + channel * BR
                    ref[at, pl.ds(x_at, BR), pl.ds(y_at, B)] = got_ref[source, row : row + BR] * fluid

        return carry

    lax.fori_loop(0, OWNERS, one, 0)
    for ref, row in ((first_ref, 0), (last_ref, XL - 1)):
        ref[0:1] = z_ref[1, row : row + 1]
        ref[1:2] = xy_ref[0, row : row + 1]


def setup_kernel(
    place_ref, z_ref, xy_ref, partner_ref, outer_ref, xlo_ref, xhi_ref, even_ref, odd_ref, small_ref, column_ref,
    lam_ref, faces_ref, source_ref, modes_ref, ends_ref, wext_ref, aext_ref, fold_ref,
):
    for ref, field, row in ((wext_ref, z_ref[1], 0), (aext_ref, xy_ref[0], 1)):
        ref[7:8] = xlo_ref[row : row + 1]
        ref[XL + 8 : XL + 9] = xhi_ref[row : row + 1]
        ref[8 : XL + 8] = field
    inner = lax.broadcasted_iota(jnp.int32, (8, N), 1) < N - 1
    sign = (2 * place_ref[1] - 1).astype(F32)
    for i in range(XL // 8):
        rows = pl.ds(8 * i, 8)
        accel_z = z_ref[0, rows]
        weight = z_ref[1, rows]
        accel_x = xy_ref[0, rows]
        accel_y = xy_ref[1, rows]
        face_p = jnp.sqrt(weight * partner_ref[1, rows])
        face_o = jnp.sqrt(weight * outer_ref[1, rows])
        face_xp = jnp.sqrt(weight * wext_ref[pl.ds(8 * i + 9, 8)])
        face_xm = jnp.sqrt(weight * wext_ref[pl.ds(8 * i + 7, 8)])
        face_yp = jnp.where(inner, jnp.sqrt(weight * pltpu.roll(weight, N - 1, 1)), 0.0)
        face_ym = pltpu.roll(face_yp, 1, 1)
        diagonal = SHIFT_RATE * weight + jnp.where(weight > 0.0, 0.0, 1.0)
        diagonal = diagonal + face_p + face_o + face_xp + face_xm + face_yp + face_ym
        flux = face_p * (partner_ref[0, rows] + accel_z) - face_o * (accel_z + outer_ref[0, rows])
        flux = sign * flux + face_xm * (aext_ref[pl.ds(8 * i + 7, 8)] + accel_x)
        flux = flux - face_xp * (accel_x + aext_ref[pl.ds(8 * i + 9, 8)])
        flux_y = face_yp * (accel_y + pltpu.roll(accel_y, N - 1, 1))
        flux = flux + pltpu.roll(flux_y, 1, 1) - flux_y
        source_ref[rows] = 0.5 * flux
        for k, face in enumerate((face_p, face_o, face_xp, face_xm, face_yp, face_ym, diagonal)):
            faces_ref[k, rows] = face
    to_modes(source_ref, even_ref, odd_ref, small_ref, column_ref, lam_ref, fold_ref, modes_ref, ends_ref)


def update_kernel(
    place_ref, modes_ref, all_ends_ref, z_ref, cut_ref, near_far_ref, even_ref, odd_ref, small_t_ref,
    column_ref, lam_ref, update_ref, rim_ref, work_ref,
):
    slab = place_ref[0]

    def jump(m):
        total = jnp.zeros((16, 128), F32)
        for j in range(SLABS):
            total = total + cut_ref[slab + m, j] * all_ends_ref[j]
        return total[:8] + total[8:]

    farther_low, low, high, farther_high = (jump(m) for m in range(4))
    near, far = near_far_ref[0], near_far_ref[1]
    before = all_ends_ref[jnp.maximum(slab - 1, 0), 8:16] - (near * low - far * farther_low)
    after = all_ends_ref[jnp.minimum(slab + 1, SLABS - 1), 0:8] - (far * farther_high - near * high)
    low_row, high_row = as_row(low), as_row(high)
    for i in range(XL // 8):
        rows = pl.ds(8 * i, 8)
        change = column_ref[rows, 2:3] * high_row - column_ref[rows, 1:2] * low_row
        work_ref[rows] = modes_ref[rows] - change / (column_ref[rows, 0:1] + lam_ref[...])
    work_ref[0:XL] = of_table(small_t_ref, work_ref[0:XL])
    work_ref[XL : XL + 8] = jnp.concatenate([as_row(before), as_row(after), jnp.zeros((6, N), F32)], axis=0)
    even = by_table(work_ref[:, :H], even_ref, False)
    odd = by_table(work_ref[:, H:], odd_ref, False)
    work_ref[:, :H] = even
    work_ref[:, H:] = odd
    for i in range(XL // 8 + 1):
        rows = pl.ds(8 * i, 8)
        even = work_ref[rows, :H]
        odd = work_ref[rows, H:]
        value = jnp.concatenate([even + odd, mirrored(even - odd)], axis=1)
        if i < XL // 8:
            update_ref[rows] = jnp.where(z_ref[1, rows] > 0.0, value, 0.0)
        else:
            rim_ref[...] = value


def image_rows(i, value_ref, partner_ref, outer_ref, faces_ref, ext_ref):
    rows = pl.ds(8 * i, 8)
    value = value_ref[rows]
    image = faces_ref[6, rows] * value
    image = image - (faces_ref[0, rows] * partner_ref[rows] + faces_ref[1, rows] * outer_ref[rows])
    image = image - (faces_ref[2, rows] * ext_ref[pl.ds(8 * i + 9, 8)] + faces_ref[3, rows] * ext_ref[pl.ds(8 * i + 7, 8)])
    image = image - (faces_ref[4, rows] * pltpu.roll(value, N - 1, 1) + faces_ref[5, rows] * pltpu.roll(value, 1, 1))
    return value, image


def extend(value_ref, rim_ref, ext_ref):
    ext_ref[7:8] = rim_ref[0:1]
    ext_ref[XL + 8 : XL + 9] = rim_ref[1:2]
    ext_ref[8 : XL + 8] = value_ref[...]


def image_kernel(
    value_ref, rim_ref, partner_ref, outer_ref, faces_ref, even_ref, odd_ref, small_ref, column_ref, lam_ref,
    image_ref, modes_ref, ends_ref, ext_ref, fold_ref,
):
    extend(value_ref, rim_ref, ext_ref)
    for i in range(XL // 8):
        image_ref[pl.ds(8 * i, 8)] = image_rows(i, value_ref, partner_ref, outer_ref, faces_ref, ext_ref)[1]
    to_modes(image_ref, even_ref, odd_ref, small_ref, column_ref, lam_ref, fold_ref, modes_ref, ends_ref)


def sums_kernel(
    value_ref, rim_ref, partner_ref, outer_ref, faces_ref, source_ref, update_ref, first_image_ref,
    image_ref, sums_ref, ext_ref,
):
    extend(value_ref, rim_ref, ext_ref)
    totals = [jnp.zeros((8, N), F32) for _ in range(6)]
    for i in range(XL // 8):
        rows = pl.ds(8 * i, 8)
        v, t = image_rows(i, value_ref, partner_ref, outer_ref, faces_ref, ext_ref)
        image_ref[rows] = t
        r, u, q = source_ref[rows], update_ref[rows], first_image_ref[rows]
        for k, (a, b) in enumerate(((r, u), (u, q), (r, v), (q, v), (u, t), (v, t))):
            totals[k] = totals[k] + a * b
    lines = []
    for total in totals:
        line = jnp.sum(total, axis=0, keepdims=True)
        lines.append(sum(line[:, t * 128 : (t + 1) * 128] for t in range(8)))
    lines = jnp.concatenate(lines + [jnp.zeros((2, 128), F32)], axis=0)
    for j in range(OWNERS):
        sums_ref[j] = lines


def add_kernel(sums_ref, out_ref):
    total = sums_ref[0]
    for j in range(1, OWNERS):
        total = total + sums_ref[j]
    for j in range(SLABS):
        out_ref[j] = total


def final_kernel(sums_ref, source_ref, u_ref, q_ref, v_ref, t_ref, solution_ref, residual_ref):
    total = sums_ref[0]
    for j in range(1, SLABS):
        total = total + sums_ref[j]
    total = jnp.sum(total, axis=1, keepdims=True)
    ru, uq, rv, qv, ut, vt = (total[k : k + 1] for k in range(6))
    step = ru / uq
    energy = ru - step * (rv + uq) + step * step * qv
    beta = energy / ru
    cross = uq - step * ut
    curve = cross - step * qv + step * step * vt
    curve = curve + beta * (cross + uq - step * qv) + beta * beta * uq
    second = energy / curve
    spread = lambda s: jnp.broadcast_to(s, (8, N))
    step, beta, second = spread(step), spread(beta), spread(second)
    for i in range(XL // 8):
        rows = pl.ds(8 * i, 8)
        u, q = u_ref[rows], q_ref[rows]
        direction = u - step * v_ref[rows] + beta * u
        along = q - step * t_ref[rows] + beta * q
        solution_ref[rows] = step * u + second * direction
        residual_ref[rows] = source_ref[rows] - step * q - second * along


def shape(*dims):
    return pltpu.VMEM(dims, F32)


def call(kernel, out_shape, in_specs, out_specs, scratch=(), name=None):
    run = pl.pallas_call(
        kernel, out_shape=out_shape, in_specs=in_specs, out_specs=out_specs, scratch_shapes=list(scratch), name=name,
        compiler_params=pltpu.CompilerParams(vmem_limit_bytes=16 * 2**20),
    )

    def with_spaces(*operands):
        assert len(operands) == len(in_specs)
        return run(
            *(
                x if spec is SMEM else pltpu.with_memory_space_constraint(x, spec.memory_space)
                for x, spec in zip(operands, in_specs)
            )
        )

    return with_spaces


PLANE = (XL, N)
EXT = pltpu.VMEM((XL + 16, N), F32)
FOLD = pltpu.VMEM(PLANE, F32)


def on_device(camera_accel, camera_weight, brick_slot, brick_solid):
    constant = {name: jnp.asarray(value) for name, value in tables().items()}
    dct = (constant["even"], constant["odd"])
    slab_tables = (constant["column"], constant["lam_y"])
    forward = dct + (constant["small"],) + slab_tables
    place = jnp.stack([lax.axis_index("gx"), lax.axis_index("yz_2")])
    slabs, owners = lax.axis_size("gx"), lax.axis_size(YZ)
    up_x = [(i, i + 1) for i in range(slabs - 1)]
    down_x = [(b, a) for a, b in up_x]
    on_chip = [(0, 1), (1, 0)]
    off_chip = [pair for i in range(1, owners - 1, 2) for pair in ((i, i + 1), (i + 1, i))]

    def neighbours(value):
        outer = lax.ppermute(value, YZ, off_chip)
        return lax.ppermute(value, "yz_2", on_chip), outer

    send = call(
        pack_kernel,
        shape(OWNERS, SEND_ROWS, 128),
        [SMEM, SMEM, HBM, HBM],
        VMEM,
        [pltpu.SMEM((OWNERS,), jnp.int32), pltpu.SemaphoreType.DMA],
        name="pack",
    )(place, brick_slot[0], camera_accel[0].reshape(PLANE_BRICKS, 3 * BR, B), camera_weight[0])
    got = lax.all_to_all(send, YZ, split_axis=0, concat_axis=0, tiled=True)
    z_fields, xy_fields, first, last = call(
        place_kernel,
        (shape(2, *PLANE), shape(2, *PLANE), shape(2, N), shape(2, N)),
        [SMEM, VMEM],
        (VMEM,) * 4,
        [pltpu.SMEM((OWNERS, 1, 128), F32), pltpu.SemaphoreType.DMA],
        name="place",
    )(brick_solid[0], got)
    partner, outer = neighbours(z_fields)
    xlo = lax.ppermute(last, "gx", up_x)
    xhi = lax.ppermute(first, "gx", down_x)
    faces, source, modes, ends = call(
        setup_kernel,
        (shape(7, *PLANE), shape(*PLANE), shape(*PLANE), shape(SLABS, 16, 128)),
        [SMEM] + [VMEM] * 11,
        (VMEM,) * 4,
        [EXT, EXT, FOLD],
        name="setup",
    )(place, z_fields, xy_fields, partner, outer, xlo, xhi, *forward)

    def updated(modes, ends):
        all_ends = lax.all_to_all(ends, "gx", split_axis=0, concat_axis=0, tiled=True)
        return call(
            update_kernel,
            (shape(*PLANE), shape(8, N)),
            [SMEM] + [VMEM] * 10,
            (VMEM, VMEM),
            [pltpu.VMEM((XL + 8, N), F32)],
            name="update",
        )(
            place, modes, all_ends, z_fields, constant["cut"], constant["ends"],
            *dct, constant["small_t"], *slab_tables,
        )

    u, rim = updated(modes, ends)
    q, modes, ends = call(
        image_kernel,
        (shape(*PLANE), shape(*PLANE), shape(SLABS, 16, 128)),
        [VMEM] * 10,
        (VMEM,) * 3,
        [EXT, FOLD],
        name="image",
    )(u, rim, *neighbours(u), faces, *forward)
    v, rim = updated(modes, ends)
    t, sums = call(
        sums_kernel,
        (shape(*PLANE), shape(OWNERS, 8, 128)),
        [VMEM] * 8,
        (VMEM, VMEM),
        [EXT],
        name="sums",
    )(v, rim, *neighbours(v), faces, source, u, q)
    sums = lax.all_to_all(sums, YZ, split_axis=0, concat_axis=0, tiled=True)
    sums = call(add_kernel, shape(SLABS, 8, 128), [VMEM], VMEM, name="add")(sums)
    sums = lax.all_to_all(sums, "gx", split_axis=0, concat_axis=0, tiled=True)
    result, residual = call(
        final_kernel, (jax.ShapeDtypeStruct(PLANE, F32),) * 2, [VMEM] * 6, (VMEM, VMEM), name="final"
    )(sums, source, u, q, v, t)
    return result[None], residual[None]


def solution(mesh):
    finer = Mesh(mesh.devices.reshape(mesh.shape["gx"], 4, 4, 2), ("gx", "yz_0", "yz_1", "yz_2"))
    in_specs = (P("gx", YZ, None, None, None), P("gx", YZ, None, None), P("gx", YZ), P("gx", YZ))
    out_specs = (P(YZ, "gx", None), P(YZ, "gx", None))
    return jax.shard_map(
        on_device, mesh=finer, in_specs=in_specs, out_specs=out_specs, check_vma=False
    )
```

```python
import functools

import jax
import jax.numpy as jnp
import ml_dtypes
import numpy as np
from jax import lax
from jax.experimental import pallas as pl
from jax.experimental.pallas import tpu as pltpu
from jax.sharding import Mesh
from jax.sharding import PartitionSpec as P

N = 1024
H = N // 2
XL = 128
SLABS = 8
BR = 16
B = 128
PLANE_BRICKS = 64
OWNERS = 32
PER_PAIR = 3
BRICK_ROWS = 3 * BR
SIDE_ROW = PER_PAIR * BRICK_ROWS
END_ROW = SIDE_ROW + BR
SEND_ROWS = END_ROW + 8
ID_LANE = 64
CHUNKS = 4
GROUP = 4
YZ = ("yz_0", "yz_1", "yz_2")
SHIFT_RATE = 0.05
FLOOR = 2.0
F32 = jnp.float32
BF16 = jnp.bfloat16
VMEM = pl.BlockSpec(memory_space=pltpu.VMEM)
SMEM = pl.BlockSpec(memory_space=pltpu.SMEM)
HBM = pl.BlockSpec(memory_space=pltpu.HBM)


def cosine_rows(length):
    k = np.arange(length, dtype=np.int64)[:, None]
    i = np.arange(length, dtype=np.int64)[None, :]
    m = (k * (2 * i + 1)) % (4 * length)
    scale = np.sqrt(np.where(k == 0, 1.0, 2.0) / length)
    return scale * np.cos(np.pi * m / (2.0 * length))


def two_bf16(table):
    high = table.astype(np.float32).astype(ml_dtypes.bfloat16)
    low = (table - high.astype(np.float64)).astype(np.float32).astype(ml_dtypes.bfloat16)
    return high, low


@functools.lru_cache(None)
def tables():
    out = {}
    big = cosine_rows(N)
    out["even"] = np.stack(two_bf16(big[0::2, :H]))
    out["odd"] = np.stack(two_bf16(big[1::2, :H]))
    small = cosine_rows(XL)
    out["small"] = np.concatenate(two_bf16(small), axis=0)
    out["small_t"] = np.concatenate(two_bf16(small.T.copy()), axis=0)
    lam_x = 2.0 - 2.0 * np.cos(np.pi * np.arange(XL) / XL)
    ky = np.concatenate([np.arange(0, N, 2), np.arange(1, N, 2)])
    lam_y = 2.0 - 2.0 * np.cos(np.pi * ky / N)
    column = np.zeros((XL, 128), np.float32)
    column[:, 0] = lam_x + FLOOR
    column[:, 1] = small[:, 0]
    column[:, 2] = small[:, XL - 1]
    out["column"] = column
    out["lam_y"] = lam_y.astype(np.float32)[None]
    denom = lam_x[:, None] + lam_y[None] + FLOOR
    near = np.sum(small[:, :1] ** 2 / denom, axis=0)
    far = np.sum(small[:, :1] * small[:, XL - 1 :] / denom, axis=0)
    cuts = SLABS - 1
    system = np.zeros((N, cuts, cuts))
    for j in range(cuts):
        system[:, j, j] = 1.0 + 2.0 * near
    for j in range(cuts - 1):
        system[:, j, j + 1] = -far
        system[:, j + 1, j] = -far
    inverse = np.linalg.inv(system)
    out["cut"] = inverse.transpose(1, 2, 0).astype(np.float32).reshape(cuts, cuts, 8, 128)
    out["ends"] = np.stack([near, far]).astype(np.float32).reshape(2, 8, 128)
    return out


def split(value):
    high = value.astype(BF16)
    return high, (value - high.astype(F32)).astype(BF16)


def product(a, b, transposed=False):
    dims = (((1,), (1 if transposed else 0,)), ((), ()))
    return lax.dot_general(a, b, dims, preferred_element_type=F32)


def by_table(data, table_ref, transposed):
    high, low = split(data)
    rows = data.shape[0]
    both = product(jnp.concatenate([high, low], axis=0), table_ref[0], transposed)
    return both[:rows] + both[rows:] + product(high, table_ref[1], transposed)


def of_table(table_ref, data):
    high, low = split(data)
    both = product(table_ref[...], high)
    return both[:XL] + both[XL:] + product(table_ref[:XL], low)


def mirrored(value):
    rows, width = value.shape
    index = 127 - lax.broadcasted_iota(jnp.int32, (rows, 128), 1)
    tiles = [
        jnp.take_along_axis(value[:, t * 128 : (t + 1) * 128], index, axis=1)
        for t in range(width // 128)
    ]
    return jnp.concatenate(tiles[::-1], axis=1)


def as_tile(row):
    return jnp.concatenate([row[:, t * 128 : (t + 1) * 128] for t in range(8)], axis=0)


def as_row(tile):
    return jnp.concatenate([tile[t : t + 1] for t in range(8)], axis=1)


def to_modes(field_ref, even_ref, odd_ref, small_ref, column_ref, lam_ref, fold_ref, modes_ref, ends_ref):
    for i in range(XL // 8):
        rows = pl.ds(8 * i, 8)
        low = field_ref[rows, :H]
        high = mirrored(field_ref[rows, H:])
        fold_ref[rows, :H] = low + high
        fold_ref[rows, H:] = low - high
    spectrum = jnp.concatenate(
        [
            by_table(fold_ref[:, :H], even_ref, True),
            by_table(fold_ref[:, H:], odd_ref, True),
        ],
        axis=1,
    )
    modes_ref[...] = of_table(small_ref, spectrum)
    first = jnp.zeros((8, N), F32)
    last = jnp.zeros((8, N), F32)
    for i in range(XL // 8):
        rows = pl.ds(8 * i, 8)
        modes = modes_ref[rows, :] / (column_ref[rows, 0:1] + lam_ref[...])
        modes_ref[rows, :] = modes
        first = first + modes * column_ref[rows, 1:2]
        last = last + modes * column_ref[rows, 2:3]
    first = as_tile(jnp.sum(first, axis=0, keepdims=True))
    last = as_tile(jnp.sum(last, axis=0, keepdims=True))
    for j in range(SLABS):
        ends_ref[j, 0:8] = first
        ends_ref[j, 8:16] = last


def pack_kernel(
    place_ref, slot_ref, accel_hbm, weight_hbm, out_ref,
    count_ref, held_ref, number_ref, accel_ref, weight_ref, inner_ref, side_ref, sem,
):
    del place_ref
    size = PLANE_BRICKS // CHUNKS
    copies = []
    for chunk in range(CHUNKS):
        bricks = pl.ds(chunk * size, size)
        copies.append(
            (
                pltpu.make_async_copy(accel_hbm.at[bricks], accel_ref.at[bricks], sem.at[0, chunk]),
                pltpu.make_async_copy(weight_hbm.at[bricks], weight_ref.at[bricks], sem.at[1, chunk]),
            )
        )
        for copy in copies[-1]:
            copy.start()
    for o in range(OWNERS):
        count_ref[o] = 0
    for k in range(OWNERS * PER_PAIR):
        held_ref[k] = 0
        number_ref[k] = -1

    def assign(s, carry):
        brick = slot_ref[s]
        owner = brick // PLANE_BRICKS
        place = count_ref[owner]
        count_ref[owner] = place + 1
        held_ref[owner * PER_PAIR + place] = s
        number_ref[owner * PER_PAIR + place] = brick - owner * PLANE_BRICKS
        return carry

    lax.fori_loop(0, PLANE_BRICKS, assign, 0, unroll=4)
    dims = (GROUP, BR, B)
    lane = lax.broadcasted_iota(jnp.int32, dims, 2)
    row = lax.broadcasted_iota(jnp.int32, dims, 1)

    def inside(group, carry):
        bricks = pl.ds(group * GROUP, GROUP)
        accel_x, accel_y = accel_ref[bricks, BR : 2 * BR], accel_ref[bricks, 2 * BR :]
        weight = weight_ref[bricks]
        flux_x = jnp.sqrt(weight * pltpu.roll(weight, BR - 1, 1)) * (accel_x + pltpu.roll(accel_x, BR - 1, 1))
        flux_y = jnp.sqrt(weight * pltpu.roll(weight, B - 1, 2)) * (accel_y + pltpu.roll(accel_y, B - 1, 2))
        flux_x = jnp.where(row < BR - 1, flux_x, 0.0)
        flux_y = jnp.where(lane < B - 1, flux_y, 0.0)
        inner_ref[bricks] = 0.5 * (pltpu.roll(flux_x, 1, 1) - flux_x + pltpu.roll(flux_y, 1, 2) - flux_y)
        low = jnp.broadcast_to(accel_y[:, :, :1], dims)
        high = jnp.broadcast_to(accel_y[:, :, B - 1 :], dims)
        side_ref[bricks] = jnp.where(lane < ID_LANE, low, high)
        return carry

    for chunk in range(CHUNKS):
        for copy in copies[chunk]:
            copy.wait()
        lax.fori_loop(chunk * size // GROUP, (chunk + 1) * size // GROUP, inside, 0)
    lane, row = lane[0], row[0, :8]

    def fill(owner, carry):
        sides = jnp.zeros((BR, B), F32)
        ends = jnp.zeros((8, B), F32)
        for place in range(PER_PAIR):
            s = held_ref[owner * PER_PAIR + place]
            number = number_ref[owner * PER_PAIR + place].astype(F32)
            at = place * BRICK_ROWS
            out_ref[owner, at : at + BR] = accel_ref[s, :BR]
            out_ref[owner, at + BR : at + 2 * BR] = inner_ref[s]
            out_ref[owner, at + 2 * BR : at + 3 * BR] = weight_ref[s]
            sides = jnp.where((lane == place) | (lane == B - 1 - place), side_ref[s], sides)
            sides = jnp.where(lane == ID_LANE + place, number, sides)
            ends = jnp.where(row == 2 * place, accel_ref[s, BR : BR + 1], ends)
            ends = jnp.where(row == 2 * place + 1, accel_ref[s, 2 * BR - 1 : 2 * BR], ends)
        out_ref[owner, SIDE_ROW:END_ROW] = sides
        out_ref[owner, END_ROW:] = ends
        return carry

    lax.fori_loop(0, OWNERS, fill, 0, unroll=2)


def place_kernel(
    solid_ref, got_ref, z_ref, source_ref, ends_ref, sides_ref, first_ref, last_ref, ids_ref, from_ref, sem
):
    ids_copy = pltpu.make_async_copy(got_ref.at[:, pl.ds(SIDE_ROW, 1)], ids_ref, sem)
    ids_copy.start()
    ids_copy.wait()
    first_lane = lax.broadcasted_iota(jnp.int32, (BR, B), 1) == 0
    upper_half = lax.broadcasted_iota(jnp.int32, (BR, B), 0) < BR // 2

    def find(source, carry):
        for place in range(PER_PAIR):
            brick = ids_ref[source, 0, ID_LANE + place].astype(jnp.int32)
            from_ref[jnp.where(brick < 0, PLANE_BRICKS, brick)] = source * 4 + place
        return carry

    lax.fori_loop(0, OWNERS, find, 0, unroll=2)

    def line(x, carry):
        rows = pl.ds(pl.multiple_of(x * BR, BR), BR)
        for y in range(N // B):
            cols = pl.ds(y * B, B)
            source, place = from_ref[x * (N // B) + y] // 4, from_ref[x * (N // B) + y] % 4
            fluid = (1 - solid_ref[x * (N // B) + y]).astype(F32)
            at = pl.multiple_of(place * BRICK_ROWS, BR)
            z_ref[0, rows, cols] = got_ref[source, pl.ds(at, BR)]
            source_ref[rows, cols] = got_ref[source, pl.ds(at + BR, BR)] * fluid
            z_ref[1, rows, cols] = got_ref[source, pl.ds(at + 2 * BR, BR)] * fluid
            sides = got_ref[source, SIDE_ROW:END_ROW]
            low = pltpu.roll(sides, (B - place) % B, 1)
            high = pltpu.roll(sides, place, 1)
            sides_ref[rows, cols] = jnp.where(first_lane, low, high)
            first = got_ref[source, pl.ds(END_ROW + 2 * place, 1)]
            last = got_ref[source, pl.ds(END_ROW + 1 + 2 * place, 1)]
            ends_ref[rows, cols] = jnp.where(upper_half, first, last)
        return carry

    lax.fori_loop(0, XL // BR, line, 0)
    for ref, row in ((first_ref, 0), (last_ref, XL - 1)):
        ref[0:1] = z_ref[1, row : row + 1]
        ref[1:2] = ends_ref[row : row + 1]


def setup_kernel(
    place_ref, z_ref, inner_ref, x_ends_ref, sides_ref, partner_ref, outer_ref, xlo_ref, xhi_ref,
    even_ref, odd_ref, small_ref, column_ref, lam_ref,
    faces_ref, source_ref, modes_ref, ends_ref, wext_ref, fold_ref,
):
    wext_ref[7:8] = xlo_ref[0:1]
    wext_ref[XL + 8 : XL + 9] = xhi_ref[0:1]
    wext_ref[8 : XL + 8] = z_ref[1]
    lane = lax.broadcasted_iota(jnp.int32, (8, N), 1)
    inside = lane < N - 1
    brick_end = lane % B == B - 1
    sign = (2 * place_ref[1] - 1).astype(F32)
    for i in range(XL // 8):
        rows = pl.ds(8 * i, 8)
        accel_z = z_ref[0, rows]
        weight = z_ref[1, rows]
        side = sides_ref[rows]
        face_p = jnp.sqrt(weight * partner_ref[1, rows])
        face_o = jnp.sqrt(weight * outer_ref[1, rows])
        face_xp = jnp.sqrt(weight * wext_ref[pl.ds(8 * i + 9, 8)])
        face_xm = jnp.sqrt(weight * wext_ref[pl.ds(8 * i + 7, 8)])
        face_yp = jnp.where(inside, jnp.sqrt(weight * pltpu.roll(weight, N - 1, 1)), 0.0)
        face_ym = pltpu.roll(face_yp, 1, 1)
        diagonal = SHIFT_RATE * weight + jnp.where(weight > 0.0, 0.0, 1.0)
        diagonal = diagonal + face_p + face_o + face_xp + face_xm + face_yp + face_ym
        flux = face_p * (partner_ref[0, rows] + accel_z) - face_o * (accel_z + outer_ref[0, rows])
        flux_y = jnp.where(brick_end, face_yp * (side + pltpu.roll(side, N - 1, 1)), 0.0)
        flux = sign * flux + pltpu.roll(flux_y, 1, 1) - flux_y
        source_ref[rows] = inner_ref[rows] + 0.5 * flux
        for k, face in enumerate((face_p, face_o, face_xp, face_xm, face_yp, face_ym, diagonal)):
            faces_ref[k, rows] = face
    for x in range(0, XL + 1, BR):
        face = faces_ref[3, x : x + 1] if x < XL else faces_ref[2, x - 1 : x]
        before = x_ends_ref[x - 1 : x] if x > 0 else xlo_ref[1:2]
        after = x_ends_ref[x : x + 1] if x < XL else xhi_ref[1:2]
        flux = 0.5 * face * (before + after)
        if x > 0:
            source_ref[x - 1 : x] = source_ref[x - 1 : x] - flux
        if x < XL:
            source_ref[x : x + 1] = source_ref[x : x + 1] + flux
    to_modes(source_ref, even_ref, odd_ref, small_ref, column_ref, lam_ref, fold_ref, modes_ref, ends_ref)


def update_kernel(
    place_ref, modes_ref, all_ends_ref, z_ref, cut_ref, near_far_ref, even_ref, odd_ref, small_t_ref,
    column_ref, lam_ref, update_ref, rim_ref, work_ref,
):
    slab = place_ref[0]

    steps = [all_ends_ref[j, 8:16] - all_ends_ref[j + 1, 0:8] for j in range(SLABS - 1)]

    def jump(cut):
        at = jnp.clip(cut, 0, SLABS - 2)
        total = jnp.zeros((8, 128), F32)
        for j, step in enumerate(steps):
            total = total + cut_ref[at, j] * step
        return jnp.where(at == cut, total, 0.0)

    farther_low, low, high, farther_high = (jump(slab + m) for m in (-2, -1, 0, 1))
    near, far = near_far_ref[0], near_far_ref[1]
    before = all_ends_ref[jnp.maximum(slab - 1, 0), 8:16] - (near * low - far * farther_low)
    after = all_ends_ref[jnp.minimum(slab + 1, SLABS - 1), 0:8] - (far * farther_high - near * high)
    low_row, high_row = as_row(low), as_row(high)
    for i in range(XL // 8):
        rows = pl.ds(8 * i, 8)
        change = column_ref[rows, 2:3] * high_row - column_ref[rows, 1:2] * low_row
        work_ref[rows] = modes_ref[rows] - change / (column_ref[rows, 0:1] + lam_ref[...])
    work_ref[0:XL] = of_table(small_t_ref, work_ref[0:XL])
    work_ref[XL : XL + 8] = jnp.concatenate([as_row(before), as_row(after), jnp.zeros((6, N), F32)], axis=0)
    even = by_table(work_ref[:, :H], even_ref, False)
    odd = by_table(work_ref[:, H:], odd_ref, False)
    work_ref[:, :H] = even
    work_ref[:, H:] = odd
    for i in range(XL // 8 + 1):
        rows = pl.ds(8 * i, 8)
        even = work_ref[rows, :H]
        odd = work_ref[rows, H:]
        value = jnp.concatenate([even + odd, mirrored(even - odd)], axis=1)
        if i < XL // 8:
            update_ref[rows] = jnp.where(z_ref[1, rows] > 0.0, value, 0.0)
        else:
            rim_ref[...] = value


def image_rows(i, value_ref, partner_ref, outer_ref, faces_ref, ext_ref):
    rows = pl.ds(8 * i, 8)
    value = value_ref[rows]
    image = faces_ref[6, rows] * value
    image = image - (faces_ref[0, rows] * partner_ref[rows] + faces_ref[1, rows] * outer_ref[rows])
    image = image - (faces_ref[2, rows] * ext_ref[pl.ds(8 * i + 9, 8)] + faces_ref[3, rows] * ext_ref[pl.ds(8 * i + 7, 8)])
    image = image - (faces_ref[4, rows] * pltpu.roll(value, N - 1, 1) + faces_ref[5, rows] * pltpu.roll(value, 1, 1))
    return value, image


def extend(value_ref, rim_ref, ext_ref):
    ext_ref[7:8] = rim_ref[0:1]
    ext_ref[XL + 8 : XL + 9] = rim_ref[1:2]
    ext_ref[8 : XL + 8] = value_ref[...]


def image_kernel(
    value_ref, rim_ref, partner_ref, outer_ref, faces_ref, even_ref, odd_ref, small_ref, column_ref, lam_ref,
    image_ref, modes_ref, ends_ref, ext_ref, fold_ref,
):
    extend(value_ref, rim_ref, ext_ref)
    for i in range(XL // 8):
        image_ref[pl.ds(8 * i, 8)] = image_rows(i, value_ref, partner_ref, outer_ref, faces_ref, ext_ref)[1]
    to_modes(image_ref, even_ref, odd_ref, small_ref, column_ref, lam_ref, fold_ref, modes_ref, ends_ref)


def sums_kernel(
    value_ref, rim_ref, partner_ref, outer_ref, faces_ref, source_ref, update_ref, first_image_ref,
    image_ref, sums_ref, ext_ref,
):
    extend(value_ref, rim_ref, ext_ref)
    totals = [jnp.zeros((8, N), F32) for _ in range(6)]
    for i in range(XL // 8):
        rows = pl.ds(8 * i, 8)
        v, t = image_rows(i, value_ref, partner_ref, outer_ref, faces_ref, ext_ref)
        image_ref[rows] = t
        r, u, q = source_ref[rows], update_ref[rows], first_image_ref[rows]
        for k, (a, b) in enumerate(((r, u), (u, q), (r, v), (q, v), (u, t), (v, t))):
            totals[k] = totals[k] + a * b
    lines = []
    for total in totals:
        line = jnp.sum(total, axis=0, keepdims=True)
        lines.append(sum(line[:, t * 128 : (t + 1) * 128] for t in range(8)))
    lines = jnp.concatenate(lines + [jnp.zeros((2, 128), F32)], axis=0)
    for j in range(OWNERS):
        sums_ref[j] = lines


def add_kernel(sums_ref, out_ref):
    total = sums_ref[0]
    for j in range(1, OWNERS):
        total = total + sums_ref[j]
    for j in range(SLABS):
        out_ref[j] = total


def final_kernel(sums_ref, source_ref, u_ref, q_ref, v_ref, t_ref, solution_ref, residual_ref):
    total = sums_ref[0]
    for j in range(1, SLABS):
        total = total + sums_ref[j]
    total = jnp.sum(total, axis=1, keepdims=True)
    ru, uq, rv, qv, ut, vt = (total[k : k + 1] for k in range(6))
    step = ru / uq
    energy = ru - step * (rv + uq) + step * step * qv
    beta = energy / ru
    cross = uq - step * ut
    curve = cross - step * qv + step * step * vt
    curve = curve + beta * (cross + uq - step * qv) + beta * beta * uq
    second = energy / curve
    spread = lambda s: jnp.broadcast_to(s, (8, N))
    step, beta, second = spread(step), spread(beta), spread(second)
    for i in range(XL // 8):
        rows = pl.ds(8 * i, 8)
        u, q = u_ref[rows], q_ref[rows]
        direction = u - step * v_ref[rows] + beta * u
        along = q - step * t_ref[rows] + beta * q
        solution_ref[rows] = step * u + second * direction
        residual_ref[rows] = source_ref[rows] - step * q - second * along


def shape(*dims):
    return pltpu.VMEM(dims, F32)


def call(kernel, out_shape, in_specs, out_specs, scratch=(), name=None):
    run = pl.pallas_call(
        kernel, out_shape=out_shape, in_specs=in_specs, out_specs=out_specs, scratch_shapes=list(scratch), name=name,
        compiler_params=pltpu.CompilerParams(vmem_limit_bytes=16 * 2**20),
    )

    def with_spaces(*operands):
        assert len(operands) == len(in_specs)
        return run(
            *(
                x if spec is SMEM else pltpu.with_memory_space_constraint(x, spec.memory_space)
                for x, spec in zip(operands, in_specs)
            )
        )

    return with_spaces


PLANE = (XL, N)
EXT = pltpu.VMEM((XL + 16, N), F32)
FOLD = pltpu.VMEM(PLANE, F32)


def on_device(camera_accel, camera_weight, brick_slot, brick_solid):
    constant = {name: jnp.asarray(value) for name, value in tables().items()}
    dct = (constant["even"], constant["odd"])
    slab_tables = (constant["column"], constant["lam_y"])
    forward = dct + (constant["small"],) + slab_tables
    place = jnp.stack([lax.axis_index("gx"), lax.axis_index("yz_2")])
    slabs, owners = lax.axis_size("gx"), lax.axis_size(YZ)
    up_x = [(i, i + 1) for i in range(slabs - 1)]
    down_x = [(b, a) for a, b in up_x]
    on_chip = [(0, 1), (1, 0)]
    off_chip = [pair for i in range(1, owners - 1, 2) for pair in ((i, i + 1), (i + 1, i))]

    def neighbours(value):
        outer = lax.ppermute(value, YZ, off_chip)
        return lax.ppermute(value, "yz_2", on_chip), outer

    send = call(
        pack_kernel,
        shape(OWNERS, SEND_ROWS, 128),
        [SMEM, SMEM, HBM, HBM],
        VMEM,
        [
            pltpu.SMEM((OWNERS,), jnp.int32),
            pltpu.SMEM((OWNERS * PER_PAIR,), jnp.int32),
            pltpu.SMEM((OWNERS * PER_PAIR,), jnp.int32),
            pltpu.VMEM((PLANE_BRICKS, 3 * BR, B), F32),
            pltpu.VMEM((PLANE_BRICKS, BR, B), F32),
            pltpu.VMEM((PLANE_BRICKS, BR, B), F32),
            pltpu.VMEM((PLANE_BRICKS, BR, B), F32),
            pltpu.SemaphoreType.DMA((2, CHUNKS)),
        ],
        name="pack",
    )(place, brick_slot[0], camera_accel[0].reshape(PLANE_BRICKS, 3 * BR, B), camera_weight[0])
    got = lax.all_to_all(send, YZ, split_axis=0, concat_axis=0, tiled=True)
    z_fields, inner, x_ends, sides, first, last = call(
        place_kernel,
        (shape(2, *PLANE), shape(*PLANE), shape(*PLANE), shape(*PLANE), shape(2, N), shape(2, N)),
        [SMEM, VMEM],
        (VMEM,) * 6,
        [
            pltpu.SMEM((OWNERS, 1, B), F32),
            pltpu.SMEM((PLANE_BRICKS + 1,), jnp.int32),
            pltpu.SemaphoreType.DMA,
        ],
        name="place",
    )(brick_solid[0], got)
    partner, outer = neighbours(z_fields)
    xlo = lax.ppermute(last, "gx", up_x)
    xhi = lax.ppermute(first, "gx", down_x)
    faces, source, modes, ends = call(
        setup_kernel,
        (shape(7, *PLANE), shape(*PLANE), shape(*PLANE), shape(SLABS, 16, 128)),
        [SMEM] + [VMEM] * 13,
        (VMEM,) * 4,
        [EXT, FOLD],
        name="setup",
    )(place, z_fields, inner, x_ends, sides, partner, outer, xlo, xhi, *forward)

    def updated(modes, ends):
        all_ends = lax.all_to_all(ends, "gx", split_axis=0, concat_axis=0, tiled=True)
        return call(
            update_kernel,
            (shape(*PLANE), shape(8, N)),
            [SMEM] + [VMEM] * 10,
            (VMEM, VMEM),
            [pltpu.VMEM((XL + 8, N), F32)],
            name="update",
        )(
            place, modes, all_ends, z_fields, constant["cut"], constant["ends"],
            *dct, constant["small_t"], *slab_tables,
        )

    u, rim = updated(modes, ends)
    q, modes, ends = call(
        image_kernel,
        (shape(*PLANE), shape(*PLANE), shape(SLABS, 16, 128)),
        [VMEM] * 10,
        (VMEM,) * 3,
        [EXT, FOLD],
        name="image",
    )(u, rim, *neighbours(u), faces, *forward)
    v, rim = updated(modes, ends)
    t, sums = call(
        sums_kernel,
        (shape(*PLANE), shape(OWNERS, 8, 128)),
        [VMEM] * 8,
        (VMEM, VMEM),
        [EXT],
        name="sums",
    )(v, rim, *neighbours(v), faces, source, u, q)
    sums = lax.all_to_all(sums, YZ, split_axis=0, concat_axis=0, tiled=True)
    sums = call(add_kernel, shape(SLABS, 8, 128), [VMEM], VMEM, name="add")(sums)
    sums = lax.all_to_all(sums, "gx", split_axis=0, concat_axis=0, tiled=True)
    result, residual = call(
        final_kernel, (jax.ShapeDtypeStruct(PLANE, F32),) * 2, [VMEM] * 6, (VMEM, VMEM), name="final"
    )(sums, source, u, q, v, t)
    return result[None], residual[None]


def solution(mesh):
    finer = Mesh(mesh.devices.reshape(mesh.shape["gx"], 4, 4, 2), ("gx", "yz_0", "yz_1", "yz_2"))
    in_specs = (P("gx", YZ, None, None, None), P("gx", YZ, None, None), P("gx", YZ), P("gx", YZ))
    out_specs = (P(YZ, "gx", None), P(YZ, "gx", None))
    return jax.shard_map(
        on_device, mesh=finer, in_specs=in_specs, out_specs=out_specs, check_vma=False
    )
```

```python
import functools

import jax
import jax.numpy as jnp
import ml_dtypes
import numpy as np
from jax import lax
from jax.experimental import pallas as pl
from jax.experimental.pallas import tpu as pltpu
from jax.sharding import Mesh
from jax.sharding import PartitionSpec as P

N = 1024
H = N // 2
XL = 128
SLABS = 8
BR = 16
B = 128
PLANE_BRICKS = 64
OWNERS = 32
PER_PAIR = 3
BRICK_ROWS = 3 * BR
END_ROW = PER_PAIR * BRICK_ROWS
SIDE_ROW = END_ROW + 2 * PER_PAIR
ID_ROW = SIDE_ROW + 1
SEND_ROWS = END_ROW + 8
CHUNKS = 4
GROUP = 8
YZ = ("yz_0", "yz_1", "yz_2")
SHIFT_RATE = 0.05
FLOOR = 2.0
F32 = jnp.float32
BF16 = jnp.bfloat16
VMEM = pl.BlockSpec(memory_space=pltpu.VMEM)
SMEM = pl.BlockSpec(memory_space=pltpu.SMEM)
HBM = pl.BlockSpec(memory_space=pltpu.HBM)


def cosine_rows(length):
    k = np.arange(length, dtype=np.int64)[:, None]
    i = np.arange(length, dtype=np.int64)[None, :]
    m = (k * (2 * i + 1)) % (4 * length)
    scale = np.sqrt(np.where(k == 0, 1.0, 2.0) / length)
    return scale * np.cos(np.pi * m / (2.0 * length))


def two_bf16(table):
    high = table.astype(np.float32).astype(ml_dtypes.bfloat16)
    low = (table - high.astype(np.float64)).astype(np.float32).astype(ml_dtypes.bfloat16)
    return high, low


@functools.lru_cache(None)
def tables():
    out = {}
    big = cosine_rows(N)
    out["even"] = np.stack(two_bf16(big[0::2, :H]))
    out["odd"] = np.stack(two_bf16(big[1::2, :H]))
    small = cosine_rows(XL)
    out["small"] = np.concatenate(two_bf16(small), axis=0)
    out["small_t"] = np.concatenate(two_bf16(small.T.copy()), axis=0)
    lam_x = 2.0 - 2.0 * np.cos(np.pi * np.arange(XL) / XL)
    ky = np.concatenate([np.arange(0, N, 2), np.arange(1, N, 2)])
    lam_y = 2.0 - 2.0 * np.cos(np.pi * ky / N)
    column = np.zeros((XL, 128), np.float32)
    column[:, 0] = lam_x + FLOOR
    column[:, 1] = small[:, 0]
    column[:, 2] = small[:, XL - 1]
    out["column"] = column
    out["lam_y"] = lam_y.astype(np.float32)[None]
    denom = lam_x[:, None] + lam_y[None] + FLOOR
    near = np.sum(small[:, :1] ** 2 / denom, axis=0)
    far = np.sum(small[:, :1] * small[:, XL - 1 :] / denom, axis=0)
    cuts = SLABS - 1
    system = np.zeros((N, cuts, cuts))
    for j in range(cuts):
        system[:, j, j] = 1.0 + 2.0 * near
    for j in range(cuts - 1):
        system[:, j, j + 1] = -far
        system[:, j + 1, j] = -far
    inverse = np.linalg.inv(system)
    out["cut"] = inverse.transpose(1, 2, 0).astype(np.float32).reshape(cuts, cuts, 8, 128)
    out["ends"] = np.stack([near, far]).astype(np.float32).reshape(2, 8, 128)
    return out


def split(value):
    high = value.astype(BF16)
    return high, (value - high.astype(F32)).astype(BF16)


def product(a, b, transposed=False):
    dims = (((1,), (1 if transposed else 0,)), ((), ()))
    return lax.dot_general(a, b, dims, preferred_element_type=F32)


def by_table(data, table_ref, transposed):
    high, low = split(data)
    rows = data.shape[0]
    both = product(jnp.concatenate([high, low], axis=0), table_ref[0], transposed)
    return both[:rows] + both[rows:] + product(high, table_ref[1], transposed)


def of_table(table_ref, data):
    high, low = split(data)
    both = product(table_ref[...], high)
    return both[:XL] + both[XL:] + product(table_ref[:XL], low)


def mirrored(value):
    rows, width = value.shape
    index = 127 - lax.broadcasted_iota(jnp.int32, (rows, 128), 1)
    tiles = [
        jnp.take_along_axis(value[:, t * 128 : (t + 1) * 128], index, axis=1)
        for t in range(width // 128)
    ]
    return jnp.concatenate(tiles[::-1], axis=1)


def as_tile(row):
    return jnp.concatenate([row[:, t * 128 : (t + 1) * 128] for t in range(8)], axis=0)


def as_row(tile):
    return jnp.concatenate([tile[t : t + 1] for t in range(8)], axis=1)


def to_modes(field_ref, even_ref, odd_ref, small_ref, column_ref, lam_ref, fold_ref, modes_ref, ends_ref):
    for i in range(XL // 8):
        rows = pl.ds(8 * i, 8)
        low = field_ref[rows, :H]
        high = mirrored(field_ref[rows, H:])
        fold_ref[rows, :H] = low + high
        fold_ref[rows, H:] = low - high
    spectrum = jnp.concatenate(
        [
            by_table(fold_ref[:, :H], even_ref, True),
            by_table(fold_ref[:, H:], odd_ref, True),
        ],
        axis=1,
    )
    modes_ref[...] = of_table(small_ref, spectrum)
    first = jnp.zeros((8, N), F32)
    last = jnp.zeros((8, N), F32)
    for i in range(XL // 8):
        rows = pl.ds(8 * i, 8)
        modes = modes_ref[rows, :] / (column_ref[rows, 0:1] + lam_ref[...])
        modes_ref[rows, :] = modes
        first = first + modes * column_ref[rows, 1:2]
        last = last + modes * column_ref[rows, 2:3]
    first = as_tile(jnp.sum(first, axis=0, keepdims=True))
    last = as_tile(jnp.sum(last, axis=0, keepdims=True))
    for j in range(SLABS):
        ends_ref[j, 0:8] = first
        ends_ref[j, 8:16] = last


def pack_kernel(
    place_ref, slot_hbm, accel_hbm, weight_hbm, out_ref,
    slot_ref, count_ref, held_ref, number_ref, accel_ref, weight_ref, inner_ref, side_ref, sem, slot_sem,
):
    del place_ref
    slot_copy = pltpu.make_async_copy(slot_hbm, slot_ref, slot_sem)
    slot_copy.start()
    size = PLANE_BRICKS // CHUNKS
    copies = []
    for chunk in range(CHUNKS):
        bricks = pl.ds(chunk * size, size)
        copies.append(
            (
                pltpu.make_async_copy(accel_hbm.at[bricks], accel_ref.at[bricks], sem.at[0, chunk]),
                pltpu.make_async_copy(weight_hbm.at[bricks], weight_ref.at[bricks], sem.at[1, chunk]),
            )
        )
        for copy in copies[-1]:
            copy.start()
    for o in range(OWNERS):
        count_ref[o] = 0
    for k in range(OWNERS * PER_PAIR):
        held_ref[k] = 0
        number_ref[k] = -1
    slot_copy.wait()

    def assign(s, carry):
        brick = slot_ref[0, s]
        owner = brick // PLANE_BRICKS
        place = count_ref[owner]
        count_ref[owner] = place + 1
        held_ref[owner * PER_PAIR + place] = s
        number_ref[owner * PER_PAIR + place] = brick - owner * PLANE_BRICKS
        return carry

    lax.fori_loop(0, PLANE_BRICKS, assign, 0, unroll=8)
    dims = (GROUP, BR, B)
    lane = lax.broadcasted_iota(jnp.int32, dims, 2)
    row = lax.broadcasted_iota(jnp.int32, dims, 1)
    few_lanes, few_rows = lane[0, :8], row[0, :8]
    edge = jnp.where((few_rows == 0) & (few_lanes == 0), 1.0, 0.0)
    edge = jnp.where((few_rows == 1) & (few_lanes == B - 1), 1.0, edge)

    def inside(group, carry):
        bricks = pl.ds(group * GROUP, GROUP)
        root = jnp.sqrt(weight_ref[bricks])
        weight_ref[bricks] = root
        accel_x = accel_ref[bricks, BR : 2 * BR]
        flux_x = root * pltpu.roll(root, BR - 1, 1) * (accel_x + pltpu.roll(accel_x, BR - 1, 1))
        flux_x = jnp.where(row < BR - 1, flux_x, 0.0)
        inner = pltpu.roll(flux_x, 1, 1) - flux_x
        accel_y = accel_ref[bricks, 2 * BR :]
        flux_y = root * pltpu.roll(root, B - 1, 2) * (accel_y + pltpu.roll(accel_y, B - 1, 2))
        flux_y = jnp.where(lane < B - 1, flux_y, 0.0)
        inner_ref[bricks] = 0.5 * (inner + pltpu.roll(flux_y, 1, 2) - flux_y)
        sides = lax.dot_general(
            edge, accel_y.reshape(GROUP * BR, B), (((1,), (1,)), ((), ())),
            precision=lax.Precision.HIGHEST, preferred_element_type=F32,
        )
        side_ref[group] = jnp.where(few_rows == 1, pltpu.roll(sides, BR, 1), sides)
        return carry

    for chunk in range(CHUNKS):
        for copy in copies[chunk]:
            copy.wait()
        lax.fori_loop(chunk * size // GROUP, (chunk + 1) * size // GROUP, inside, 0, unroll=2)

    def fill(owner, carry):
        ends = jnp.zeros((8, B), F32)
        for place in range(PER_PAIR):
            s = held_ref[owner * PER_PAIR + place]
            number = number_ref[owner * PER_PAIR + place].astype(F32)
            at = place * BRICK_ROWS
            out_ref[owner, at : at + BR] = accel_ref[s, :BR]
            out_ref[owner, at + BR : at + 2 * BR] = inner_ref[s]
            out_ref[owner, at + 2 * BR : at + 3 * BR] = weight_ref[s]
            ends = jnp.where(few_rows == 2 * place, accel_ref[s, BR : BR + 1], ends)
            ends = jnp.where(few_rows == 2 * place + 1, accel_ref[s, 2 * BR - 1 : 2 * BR], ends)
            sides = pltpu.roll(side_ref[s // GROUP], (B + 2 * BR * place - BR * (s % GROUP)) % B, 1)
            sides = jnp.where(few_lanes < 2 * BR * place + BR, sides[0:1], sides[1:2])
            ends = jnp.where((few_rows == SIDE_ROW - END_ROW) & (few_lanes >= 2 * BR * place), sides, ends)
            ends = jnp.where((few_rows == ID_ROW - END_ROW) & (few_lanes == place), number, ends)
        out_ref[owner, END_ROW:] = ends
        return carry

    lax.fori_loop(0, OWNERS, fill, 0, unroll=4)


def place_kernel(
    solid_ref, got_ref, z_ref, source_ref, ends_ref, sides_ref, first_ref, last_ref, ids_ref, from_ref, sem
):
    ids_copy = pltpu.make_async_copy(got_ref.at[:, pl.ds(ID_ROW, 1)], ids_ref, sem)
    ids_copy.start()
    ids_copy.wait()
    lane = lax.broadcasted_iota(jnp.int32, (BR, B), 1)
    row = lax.broadcasted_iota(jnp.int32, (BR, B), 0)

    def find(source, carry):
        for place in range(PER_PAIR):
            brick = ids_ref[source, 0, place].astype(jnp.int32)
            from_ref[jnp.where(brick < 0, PLANE_BRICKS, brick)] = source * 4 + place
        return carry

    lax.fori_loop(0, OWNERS, find, 0, unroll=4)

    def line(x, carry):
        rows = pl.ds(pl.multiple_of(x * BR, BR), BR)
        for y in range(N // B):
            cols = pl.ds(y * B, B)
            source, place = from_ref[x * (N // B) + y] // 4, from_ref[x * (N // B) + y] % 4
            fluid = (1 - solid_ref[x * (N // B) + y]).astype(F32)
            at = pl.multiple_of(place * BRICK_ROWS, BR)
            z_ref[0, rows, cols] = got_ref[source, pl.ds(at, BR)]
            source_ref[rows, cols] = got_ref[source, pl.ds(at + BR, BR)] * fluid
            z_ref[1, rows, cols] = got_ref[source, pl.ds(at + 2 * BR, BR)] * fluid
            sides = jnp.broadcast_to(got_ref[source, SIDE_ROW : SIDE_ROW + 1], (BR, B))
            own = lane - row - 2 * BR * place
            low = jnp.sum(jnp.where(own == 0, sides, 0.0), axis=1, keepdims=True)
            high = jnp.sum(jnp.where(own == BR, sides, 0.0), axis=1, keepdims=True)
            sides_ref[rows, cols] = jnp.where(lane == 0, low, high)
            first = got_ref[source, pl.ds(END_ROW + 2 * place, 1)]
            last = got_ref[source, pl.ds(END_ROW + 1 + 2 * place, 1)]
            ends_ref[rows, cols] = jnp.where(row < BR // 2, first, last)
        return carry

    lax.fori_loop(0, XL // BR, line, 0)
    for ref, row in ((first_ref, 0), (last_ref, XL - 1)):
        ref[0:1] = z_ref[1, row : row + 1]
        ref[1:2] = ends_ref[row : row + 1]


def setup_kernel(
    place_ref, z_ref, inner_ref, x_ends_ref, sides_ref, partner_ref, outer_ref, xlo_ref, xhi_ref,
    even_ref, odd_ref, small_ref, column_ref, lam_ref,
    diagonal_ref, source_ref, modes_ref, ends_ref, ext_ref, fold_ref,
):
    ext_ref[7:8] = xlo_ref[0:1]
    ext_ref[XL + 8 : XL + 9] = xhi_ref[0:1]
    ext_ref[8 : XL + 8] = z_ref[1]
    lane = lax.broadcasted_iota(jnp.int32, (8, N), 1)
    brick_end = (lane % B == B - 1) & (lane < N - 1)
    sign = (2 * place_ref[1] - 1).astype(F32)
    for i in range(XL // 8):
        rows = pl.ds(8 * i, 8)
        accel_z, root, side = z_ref[0, rows], z_ref[1, rows], sides_ref[rows]
        root_p, root_o = partner_ref[1, rows], outer_ref[1, rows]
        after = pltpu.roll(root, N - 1, 1)
        beside = root_p + root_o + ext_ref[pl.ds(8 * i + 9, 8)] + ext_ref[pl.ds(8 * i + 7, 8)]
        beside = beside + jnp.where(lane < N - 1, after, 0.0) + jnp.where(lane > 0, pltpu.roll(root, 1, 1), 0.0)
        diagonal_ref[rows] = root * (SHIFT_RATE * root + beside) + jnp.where(root > 0.0, 0.0, 1.0)
        flux = sign * (root_p * (partner_ref[0, rows] + accel_z) - root_o * (accel_z + outer_ref[0, rows]))
        flux_y = jnp.where(brick_end, root * after * (side + pltpu.roll(side, N - 1, 1)), 0.0)
        source_ref[rows] = inner_ref[rows] + 0.5 * (root * flux + pltpu.roll(flux_y, 1, 1) - flux_y)
    for x in range(0, XL + 1, BR):
        before = x_ends_ref[x - 1 : x] if x > 0 else xlo_ref[1:2]
        after = x_ends_ref[x : x + 1] if x < XL else xhi_ref[1:2]
        flux = 0.5 * ext_ref[x + 7 : x + 8] * ext_ref[x + 8 : x + 9] * (before + after)
        if x > 0:
            source_ref[x - 1 : x] = source_ref[x - 1 : x] - flux
        if x < XL:
            source_ref[x : x + 1] = source_ref[x : x + 1] + flux
    to_modes(source_ref, even_ref, odd_ref, small_ref, column_ref, lam_ref, fold_ref, modes_ref, ends_ref)


def update_kernel(
    place_ref, modes_ref, all_ends_ref, z_ref, xlo_ref, xhi_ref, cut_ref, near_far_ref, even_ref, odd_ref,
    small_t_ref, column_ref, lam_ref, update_ref, scaled_ref, rim_ref, work_ref,
):
    slab = place_ref[0]

    steps = [all_ends_ref[j, 8:16] - all_ends_ref[j + 1, 0:8] for j in range(SLABS - 1)]

    def jump(cut):
        at = jnp.clip(cut, 0, SLABS - 2)
        total = jnp.zeros((8, 128), F32)
        for j, step in enumerate(steps):
            total = total + cut_ref[at, j] * step
        return jnp.where(at == cut, total, 0.0)

    farther_low, low, high, farther_high = (jump(slab + m) for m in (-2, -1, 0, 1))
    near, far = near_far_ref[0], near_far_ref[1]
    before = all_ends_ref[jnp.maximum(slab - 1, 0), 8:16] - (near * low - far * farther_low)
    after = all_ends_ref[jnp.minimum(slab + 1, SLABS - 1), 0:8] - (far * farther_high - near * high)
    low_row, high_row = as_row(low), as_row(high)
    for i in range(XL // 8):
        rows = pl.ds(8 * i, 8)
        change = column_ref[rows, 2:3] * high_row - column_ref[rows, 1:2] * low_row
        work_ref[rows] = modes_ref[rows] - change / (column_ref[rows, 0:1] + lam_ref[...])
    work_ref[0:XL] = of_table(small_t_ref, work_ref[0:XL])
    work_ref[XL : XL + 8] = jnp.concatenate([as_row(before), as_row(after), jnp.zeros((6, N), F32)], axis=0)
    even = by_table(work_ref[:, :H], even_ref, False)
    odd = by_table(work_ref[:, H:], odd_ref, False)
    work_ref[:, :H] = even
    work_ref[:, H:] = odd
    for i in range(XL // 8 + 1):
        rows = pl.ds(8 * i, 8)
        even = work_ref[rows, :H]
        odd = work_ref[rows, H:]
        value = jnp.concatenate([even + odd, mirrored(even - odd)], axis=1)
        if i < XL // 8:
            root = z_ref[1, rows]
            update_ref[rows] = jnp.where(root > 0.0, value, 0.0)
            scaled_ref[rows] = root * value
        else:
            rim_ref[0:1] = value[0:1] * xlo_ref[0:1]
            rim_ref[1:2] = value[1:2] * xhi_ref[0:1]


def image_rows(i, value_ref, scaled_ref, partner_ref, outer_ref, z_ref, diagonal_ref, ext_ref):
    rows = pl.ds(8 * i, 8)
    value, scaled = value_ref[rows], scaled_ref[rows]
    lane = lax.broadcasted_iota(jnp.int32, (8, N), 1)
    beside = partner_ref[rows] + outer_ref[rows] + ext_ref[pl.ds(8 * i + 9, 8)] + ext_ref[pl.ds(8 * i + 7, 8)]
    beside = beside + jnp.where(lane < N - 1, pltpu.roll(scaled, N - 1, 1), 0.0)
    beside = beside + jnp.where(lane > 0, pltpu.roll(scaled, 1, 1), 0.0)
    return value, diagonal_ref[rows] * value - z_ref[1, rows] * beside


def extend(scaled_ref, rim_ref, ext_ref):
    ext_ref[7:8] = rim_ref[0:1]
    ext_ref[XL + 8 : XL + 9] = rim_ref[1:2]
    ext_ref[8 : XL + 8] = scaled_ref[...]


def image_kernel(
    value_ref, scaled_ref, rim_ref, partner_ref, outer_ref, z_ref, diagonal_ref,
    even_ref, odd_ref, small_ref, column_ref, lam_ref,
    image_ref, modes_ref, ends_ref, ext_ref, fold_ref,
):
    extend(scaled_ref, rim_ref, ext_ref)
    for i in range(XL // 8):
        _, image = image_rows(i, value_ref, scaled_ref, partner_ref, outer_ref, z_ref, diagonal_ref, ext_ref)
        image_ref[pl.ds(8 * i, 8)] = image
    to_modes(image_ref, even_ref, odd_ref, small_ref, column_ref, lam_ref, fold_ref, modes_ref, ends_ref)


def sums_kernel(
    value_ref, scaled_ref, rim_ref, partner_ref, outer_ref, z_ref, diagonal_ref, source_ref, update_ref,
    first_image_ref, image_ref, sums_ref, ext_ref,
):
    extend(scaled_ref, rim_ref, ext_ref)
    totals = [jnp.zeros((8, N), F32) for _ in range(6)]
    for i in range(XL // 8):
        rows = pl.ds(8 * i, 8)
        v, t = image_rows(i, value_ref, scaled_ref, partner_ref, outer_ref, z_ref, diagonal_ref, ext_ref)
        image_ref[rows] = t
        r, u, q = source_ref[rows], update_ref[rows], first_image_ref[rows]
        for k, (a, b) in enumerate(((r, u), (u, q), (r, v), (q, v), (u, t), (v, t))):
            totals[k] = totals[k] + a * b
    lines = []
    for total in totals:
        line = jnp.sum(total, axis=0, keepdims=True)
        lines.append(sum(line[:, t * 128 : (t + 1) * 128] for t in range(8)))
    lines = jnp.concatenate(lines + [jnp.zeros((2, 128), F32)], axis=0)
    for j in range(OWNERS):
        sums_ref[j] = lines


def add_kernel(sums_ref, out_ref):
    total = sums_ref[0]
    for j in range(1, OWNERS):
        total = total + sums_ref[j]
    for j in range(SLABS):
        out_ref[j] = total


def final_kernel(sums_ref, source_ref, u_ref, q_ref, v_ref, t_ref, solution_ref, residual_ref):
    total = sums_ref[0]
    for j in range(1, SLABS):
        total = total + sums_ref[j]
    total = jnp.sum(total, axis=1, keepdims=True)
    ru, uq, rv, qv, ut, vt = (total[k : k + 1] for k in range(6))
    step = ru / uq
    energy = ru - step * (rv + uq) + step * step * qv
    beta = energy / ru
    cross = uq - step * ut
    curve = cross - step * qv + step * step * vt
    curve = curve + beta * (cross + uq - step * qv) + beta * beta * uq
    second = energy / curve
    spread = lambda s: jnp.broadcast_to(s, (8, N))
    step, beta, second = spread(step), spread(beta), spread(second)
    for i in range(XL // 8):
        rows = pl.ds(8 * i, 8)
        u, q = u_ref[rows], q_ref[rows]
        direction = u - step * v_ref[rows] + beta * u
        along = q - step * t_ref[rows] + beta * q
        solution_ref[rows] = step * u + second * direction
        residual_ref[rows] = source_ref[rows] - step * q - second * along


def shape(*dims):
    return pltpu.VMEM(dims, F32)


def call(kernel, out_shape, in_specs, out_specs, scratch=(), name=None):
    run = pl.pallas_call(
        kernel, out_shape=out_shape, in_specs=in_specs, out_specs=out_specs, scratch_shapes=list(scratch), name=name,
        compiler_params=pltpu.CompilerParams(vmem_limit_bytes=16 * 2**20),
    )

    def with_spaces(*operands):
        assert len(operands) == len(in_specs)
        return run(
            *(
                x if spec is SMEM else pltpu.with_memory_space_constraint(x, spec.memory_space)
                for x, spec in zip(operands, in_specs)
            )
        )

    return with_spaces


PLANE = (XL, N)
EXT = pltpu.VMEM((XL + 16, N), F32)
FOLD = pltpu.VMEM(PLANE, F32)


def on_device(camera_accel, camera_weight, brick_slot, brick_solid):
    constant = {name: jnp.asarray(value) for name, value in tables().items()}
    dct = (constant["even"], constant["odd"])
    slab_tables = (constant["column"], constant["lam_y"])
    forward = dct + (constant["small"],) + slab_tables
    place = jnp.stack([lax.axis_index("gx"), lax.axis_index("yz_2")])
    slabs, owners = lax.axis_size("gx"), lax.axis_size(YZ)
    up_x = [(i, i + 1) for i in range(slabs - 1)]
    down_x = [(b, a) for a, b in up_x]
    on_chip = [(0, 1), (1, 0)]
    off_chip = [pair for i in range(1, owners - 1, 2) for pair in ((i, i + 1), (i + 1, i))]

    def neighbours(value):
        outer = lax.ppermute(value, YZ, off_chip)
        return lax.ppermute(value, "yz_2", on_chip), outer

    send = call(
        pack_kernel,
        shape(OWNERS, SEND_ROWS, 128),
        [SMEM, HBM, HBM, HBM],
        VMEM,
        [
            pltpu.SMEM((1, PLANE_BRICKS), jnp.int32),
            pltpu.SMEM((OWNERS,), jnp.int32),
            pltpu.SMEM((OWNERS * PER_PAIR,), jnp.int32),
            pltpu.SMEM((OWNERS * PER_PAIR,), jnp.int32),
            pltpu.VMEM((PLANE_BRICKS, 3 * BR, B), F32),
            pltpu.VMEM((PLANE_BRICKS, BR, B), F32),
            pltpu.VMEM((PLANE_BRICKS, BR, B), F32),
            pltpu.VMEM((PLANE_BRICKS // GROUP, 8, B), F32),
            pltpu.SemaphoreType.DMA((2, CHUNKS)),
            pltpu.SemaphoreType.DMA,
        ],
        name="pack",
    )(place, brick_slot, camera_accel[0].reshape(PLANE_BRICKS, 3 * BR, B), camera_weight[0])
    got = lax.all_to_all(send, YZ, split_axis=0, concat_axis=0, tiled=True)
    z_fields, inner, x_ends, sides, first, last = call(
        place_kernel,
        (shape(2, *PLANE), shape(*PLANE), shape(*PLANE), shape(*PLANE), shape(2, N), shape(2, N)),
        [SMEM, VMEM],
        (VMEM,) * 6,
        [
            pltpu.SMEM((OWNERS, 1, B), F32),
            pltpu.SMEM((PLANE_BRICKS + 1,), jnp.int32),
            pltpu.SemaphoreType.DMA,
        ],
        name="place",
    )(brick_solid[0], got)
    partner, outer = neighbours(z_fields)
    xlo = lax.ppermute(last, "gx", up_x)
    xhi = lax.ppermute(first, "gx", down_x)
    diagonal, source, modes, ends = call(
        setup_kernel,
        (shape(*PLANE), shape(*PLANE), shape(*PLANE), shape(SLABS, 16, 128)),
        [SMEM] + [VMEM] * 13,
        (VMEM,) * 4,
        [EXT, FOLD],
        name="setup",
    )(place, z_fields, inner, x_ends, sides, partner, outer, xlo, xhi, *forward)

    def updated(modes, ends):
        all_ends = lax.all_to_all(ends, "gx", split_axis=0, concat_axis=0, tiled=True)
        return call(
            update_kernel,
            (shape(*PLANE), shape(*PLANE), shape(2, N)),
            [SMEM] + [VMEM] * 12,
            (VMEM,) * 3,
            [pltpu.VMEM((XL + 8, N), F32)],
            name="update",
        )(
            place, modes, all_ends, z_fields, xlo, xhi, constant["cut"], constant["ends"],
            *dct, constant["small_t"], *slab_tables,
        )

    u, scaled, rim = updated(modes, ends)
    q, modes, ends = call(
        image_kernel,
        (shape(*PLANE), shape(*PLANE), shape(SLABS, 16, 128)),
        [VMEM] * 12,
        (VMEM,) * 3,
        [EXT, FOLD],
        name="image",
    )(u, scaled, rim, *neighbours(scaled), z_fields, diagonal, *forward)
    v, scaled, rim = updated(modes, ends)
    t, sums = call(
        sums_kernel,
        (shape(*PLANE), shape(OWNERS, 8, 128)),
        [VMEM] * 10,
        (VMEM, VMEM),
        [EXT],
        name="sums",
    )(v, scaled, rim, *neighbours(scaled), z_fields, diagonal, source, u, q)
    sums = lax.all_to_all(sums, YZ, split_axis=0, concat_axis=0, tiled=True)
    sums = call(add_kernel, shape(SLABS, 8, 128), [VMEM], VMEM, name="add")(sums)
    sums = lax.all_to_all(sums, "gx", split_axis=0, concat_axis=0, tiled=True)
    result, residual = call(
        final_kernel, (jax.ShapeDtypeStruct(PLANE, F32),) * 2, [VMEM] * 6, (VMEM, VMEM), name="final"
    )(sums, source, u, q, v, t)
    return result[None], residual[None]


def solution(mesh):
    finer = Mesh(mesh.devices.reshape(mesh.shape["gx"], 4, 4, 2), ("gx", "yz_0", "yz_1", "yz_2"))
    in_specs = (P("gx", YZ, None, None, None), P("gx", YZ, None, None), P("gx", YZ), P("gx", YZ))
    out_specs = (P(YZ, "gx", None), P(YZ, "gx", None))
    return jax.shard_map(
        on_device, mesh=finer, in_specs=in_specs, out_specs=out_specs, check_vma=False
    )
```

```python
import functools

import jax
import jax.numpy as jnp
import ml_dtypes
import numpy as np
from jax import lax
from jax.experimental import pallas as pl
from jax.experimental.pallas import tpu as pltpu
from jax.sharding import Mesh
from jax.sharding import PartitionSpec as P

N = 1024
H = N // 2
XL = 128
SLABS = 8
BR = 16
B = 128
PLANE_SHIFT = 6
PLANE_BRICKS = 1 << PLANE_SHIFT
OWNERS = 32
PER_PAIR = 3
BRICK_ROWS = 3 * BR
END_ROW = PER_PAIR * BRICK_ROWS
SIDE_ROW = END_ROW + 2 * PER_PAIR
ID_ROW = SIDE_ROW + 1
SEND_ROWS = END_ROW + 8
CHUNKS = 4
GROUP_SHIFT = 3
GROUP = 1 << GROUP_SHIFT
YZ = ("yz_0", "yz_1", "yz_2")
SHIFT_RATE = 0.05
FLOOR = 2.0
F32 = jnp.float32
BF16 = jnp.bfloat16
VMEM = pl.BlockSpec(memory_space=pltpu.VMEM)
SMEM = pl.BlockSpec(memory_space=pltpu.SMEM)
HBM = pl.BlockSpec(memory_space=pltpu.HBM)


def cosine_rows(length):
    k = np.arange(length, dtype=np.int64)[:, None]
    i = np.arange(length, dtype=np.int64)[None, :]
    m = (k * (2 * i + 1)) % (4 * length)
    scale = np.sqrt(np.where(k == 0, 1.0, 2.0) / length)
    return scale * np.cos(np.pi * m / (2.0 * length))


def two_bf16(table):
    high = table.astype(np.float32).astype(ml_dtypes.bfloat16)
    low = (table - high.astype(np.float64)).astype(np.float32).astype(ml_dtypes.bfloat16)
    return high, low


@functools.lru_cache(None)
def tables():
    out = {}
    big = cosine_rows(N)
    out["even"] = np.stack(two_bf16(big[0::2, :H]))
    out["odd"] = np.stack(two_bf16(big[1::2, :H]))
    small = cosine_rows(XL)
    out["small"] = np.concatenate(two_bf16(small), axis=0)
    out["small_t"] = np.concatenate(two_bf16(small.T.copy()), axis=0)
    lam_x = 2.0 - 2.0 * np.cos(np.pi * np.arange(XL) / XL)
    ky = np.concatenate([np.arange(0, N, 2), np.arange(1, N, 2)])
    lam_y = 2.0 - 2.0 * np.cos(np.pi * ky / N)
    column = np.zeros((XL, 128), np.float32)
    column[:, 0] = lam_x + FLOOR
    column[:, 1] = small[:, 0]
    column[:, 2] = small[:, XL - 1]
    out["column"] = column
    out["lam_y"] = lam_y.astype(np.float32)[None]
    denom = lam_x[:, None] + lam_y[None] + FLOOR
    near = np.sum(small[:, :1] ** 2 / denom, axis=0)
    far = np.sum(small[:, :1] * small[:, XL - 1 :] / denom, axis=0)
    cuts = SLABS - 1
    system = np.zeros((N, cuts, cuts))
    for j in range(cuts):
        system[:, j, j] = 1.0 + 2.0 * near
    for j in range(cuts - 1):
        system[:, j, j + 1] = -far
        system[:, j + 1, j] = -far
    inverse = np.linalg.inv(system)
    out["cut"] = inverse.transpose(1, 2, 0).astype(np.float32).reshape(cuts, cuts, 8, 128)
    out["ends"] = np.stack([near, far]).astype(np.float32).reshape(2, 8, 128)
    return out


def split(value):
    high = value.astype(BF16)
    return high, (value - high.astype(F32)).astype(BF16)


def product(a, b, transposed=False):
    dims = (((1,), (1 if transposed else 0,)), ((), ()))
    return lax.dot_general(a, b, dims, preferred_element_type=F32)


def by_table(data, table_ref, transposed):
    high, low = split(data)
    rows = data.shape[0]
    both = product(jnp.concatenate([high, low], axis=0), table_ref[0], transposed)
    return both[:rows] + both[rows:] + product(high, table_ref[1], transposed)


def of_table(table_ref, data):
    high, low = split(data)
    both = product(table_ref[...], high)
    return both[:XL] + both[XL:] + product(table_ref[:XL], low)


def mirrored(value):
    rows, width = value.shape
    index = 127 - lax.broadcasted_iota(jnp.int32, (rows, 128), 1)
    tiles = [
        jnp.take_along_axis(value[:, t * 128 : (t + 1) * 128], index, axis=1)
        for t in range(width // 128)
    ]
    return jnp.concatenate(tiles[::-1], axis=1)


def as_tile(row):
    return jnp.concatenate([row[:, t * 128 : (t + 1) * 128] for t in range(8)], axis=0)


def as_row(tile):
    return jnp.concatenate([tile[t : t + 1] for t in range(8)], axis=1)


def to_modes(field_ref, even_ref, odd_ref, small_ref, column_ref, inverse_ref, fold_ref, modes_ref, ends_ref):
    for i in range(XL // 8):
        rows = pl.ds(8 * i, 8)
        low = field_ref[rows, :H]
        high = mirrored(field_ref[rows, H:])
        fold_ref[rows, :H] = low + high
        fold_ref[rows, H:] = low - high
    spectrum = jnp.concatenate(
        [
            by_table(fold_ref[:, :H], even_ref, True),
            by_table(fold_ref[:, H:], odd_ref, True),
        ],
        axis=1,
    )
    modes_ref[...] = of_table(small_ref, spectrum)
    first = jnp.zeros((8, N), F32)
    last = jnp.zeros((8, N), F32)
    for i in range(XL // 8):
        rows = pl.ds(8 * i, 8)
        modes = modes_ref[rows, :] * inverse_ref[rows]
        modes_ref[rows, :] = modes
        first = first + modes * column_ref[rows, 1:2]
        last = last + modes * column_ref[rows, 2:3]
    first = as_tile(jnp.sum(first, axis=0, keepdims=True))
    last = as_tile(jnp.sum(last, axis=0, keepdims=True))
    for j in range(SLABS):
        ends_ref[j, 0:8] = first
        ends_ref[j, 8:16] = last


def pack_kernel(
    place_ref, slot_hbm, accel_hbm, weight_hbm, out_ref,
    slot_ref, count_ref, held_ref, number_ref, accel_ref, weight_ref, inner_ref, side_ref, sem, slot_sem,
):
    del place_ref
    slot_copy = pltpu.make_async_copy(slot_hbm, slot_ref, slot_sem)
    slot_copy.start()
    size = PLANE_BRICKS // CHUNKS
    copies = []
    for chunk in range(CHUNKS):
        bricks = pl.ds(chunk * size, size)
        copies.append(
            (
                pltpu.make_async_copy(accel_hbm.at[bricks], accel_ref.at[bricks], sem.at[0, chunk]),
                pltpu.make_async_copy(weight_hbm.at[bricks], weight_ref.at[bricks], sem.at[1, chunk]),
            )
        )
        for copy in copies[-1]:
            copy.start()
    for o in range(OWNERS):
        count_ref[o] = 0
    for k in range(OWNERS * PER_PAIR):
        held_ref[k] = 0
        number_ref[k] = -1
    slot_copy.wait()

    def assign(s, carry):
        brick = slot_ref[0, s]
        owner = brick >> PLANE_SHIFT
        place = count_ref[owner]
        count_ref[owner] = place + 1
        held_ref[owner * PER_PAIR + place] = s
        number_ref[owner * PER_PAIR + place] = brick & (PLANE_BRICKS - 1)
        return carry

    lax.fori_loop(0, PLANE_BRICKS, assign, 0, unroll=8)
    dims = (GROUP, BR, B)
    lane = lax.broadcasted_iota(jnp.int32, dims, 2)
    row = lax.broadcasted_iota(jnp.int32, dims, 1)
    few_lanes, few_rows = lane[0, :8], row[0, :8]
    edge = jnp.where((few_rows == 0) & (few_lanes == 0), 1.0, 0.0)
    edge = jnp.where((few_rows == 1) & (few_lanes == B - 1), 1.0, edge)

    def inside(group, carry):
        bricks = pl.ds(group * GROUP, GROUP)
        root = jnp.sqrt(weight_ref[bricks])
        weight_ref[bricks] = root
        accel_x = accel_ref[bricks, BR : 2 * BR]
        flux_x = root * pltpu.roll(root, BR - 1, 1) * (accel_x + pltpu.roll(accel_x, BR - 1, 1))
        flux_x = jnp.where(row < BR - 1, flux_x, 0.0)
        inner = pltpu.roll(flux_x, 1, 1) - flux_x
        accel_y = accel_ref[bricks, 2 * BR :]
        flux_y = root * pltpu.roll(root, B - 1, 2) * (accel_y + pltpu.roll(accel_y, B - 1, 2))
        flux_y = jnp.where(lane < B - 1, flux_y, 0.0)
        inner_ref[bricks] = 0.5 * (inner + pltpu.roll(flux_y, 1, 2) - flux_y)
        sides = lax.dot_general(
            edge, accel_y.reshape(GROUP * BR, B), (((1,), (1,)), ((), ())),
            precision=lax.Precision.HIGHEST, preferred_element_type=F32,
        )
        side_ref[group] = jnp.where(few_rows == 1, pltpu.roll(sides, BR, 1), sides)
        return carry

    for chunk in range(CHUNKS):
        for copy in copies[chunk]:
            copy.wait()
        lax.fori_loop(chunk * size // GROUP, (chunk + 1) * size // GROUP, inside, 0, unroll=2)

    def fill(owner, carry):
        ends = jnp.zeros((8, B), F32)
        for place in range(PER_PAIR):
            s = held_ref[owner * PER_PAIR + place]
            number = number_ref[owner * PER_PAIR + place].astype(F32)
            at = place * BRICK_ROWS
            out_ref[owner, at : at + BR] = accel_ref[s, :BR]
            out_ref[owner, at + BR : at + 2 * BR] = inner_ref[s]
            out_ref[owner, at + 2 * BR : at + 3 * BR] = weight_ref[s]
            ends = jnp.where(few_rows == 2 * place, accel_ref[s, BR : BR + 1], ends)
            ends = jnp.where(few_rows == 2 * place + 1, accel_ref[s, 2 * BR - 1 : 2 * BR], ends)
            sides = pltpu.roll(side_ref[s >> GROUP_SHIFT], (2 * BR * place - BR * (s & (GROUP - 1))) & (B - 1), 1)
            sides = jnp.where(few_lanes < 2 * BR * place + BR, sides[0:1], sides[1:2])
            ends = jnp.where((few_rows == SIDE_ROW - END_ROW) & (few_lanes >= 2 * BR * place), sides, ends)
            ends = jnp.where((few_rows == ID_ROW - END_ROW) & (few_lanes == place), number, ends)
        out_ref[owner, END_ROW:] = ends
        return carry

    lax.fori_loop(0, OWNERS, fill, 0, unroll=4)


def place_kernel(
    solid_ref, got_ref, z_ref, source_ref, ends_ref, sides_ref, first_ref, last_ref, ids_ref, from_ref, sem
):
    ids_copy = pltpu.make_async_copy(got_ref.at[:, pl.ds(ID_ROW, 1)], ids_ref, sem)
    ids_copy.start()
    ids_copy.wait()
    lane = lax.broadcasted_iota(jnp.int32, (BR, B), 1)
    row = lax.broadcasted_iota(jnp.int32, (BR, B), 0)

    def find(source, carry):
        for place in range(PER_PAIR):
            brick = ids_ref[source, 0, place].astype(jnp.int32)
            from_ref[jnp.where(brick < 0, PLANE_BRICKS, brick)] = source * 4 + place
        return carry

    lax.fori_loop(0, OWNERS, find, 0, unroll=4)

    def line(x, carry):
        rows = pl.ds(pl.multiple_of(x * BR, BR), BR)
        for y in range(N // B):
            cols = pl.ds(y * B, B)
            held = from_ref[x * (N // B) + y]
            source, place = held >> 2, held & 3
            fluid = (1 - solid_ref[x * (N // B) + y]).astype(F32)
            at = pl.multiple_of(place * BRICK_ROWS, BR)
            z_ref[0, rows, cols] = got_ref[source, pl.ds(at, BR)]
            source_ref[rows, cols] = got_ref[source, pl.ds(at + BR, BR)] * fluid
            z_ref[1, rows, cols] = got_ref[source, pl.ds(at + 2 * BR, BR)] * fluid
            sides = jnp.broadcast_to(got_ref[source, SIDE_ROW : SIDE_ROW + 1], (BR, B))
            own = lane - row - 2 * BR * place
            low = jnp.sum(jnp.where(own == 0, sides, 0.0), axis=1, keepdims=True)
            high = jnp.sum(jnp.where(own == BR, sides, 0.0), axis=1, keepdims=True)
            sides_ref[rows, cols] = jnp.where(lane == 0, low, high)
            first = got_ref[source, pl.ds(END_ROW + 2 * place, 1)]
            last = got_ref[source, pl.ds(END_ROW + 1 + 2 * place, 1)]
            ends_ref[rows, cols] = jnp.where(row < BR // 2, first, last)
        return carry

    lax.fori_loop(0, XL // BR, line, 0)
    for ref, row in ((first_ref, 0), (last_ref, XL - 1)):
        ref[0:1] = z_ref[1, row : row + 1]
        ref[1:2] = ends_ref[row : row + 1]


def prepare_kernel(
    z_ref, inner_ref, x_ends_ref, sides_ref, column_ref, lam_ref, beside_ref, source_ref, inverse_ref, ext_ref
):
    ext_ref[7:8] = jnp.zeros((1, N), F32)
    ext_ref[XL + 8 : XL + 9] = jnp.zeros((1, N), F32)
    ext_ref[8 : XL + 8] = z_ref[1]
    lane = lax.broadcasted_iota(jnp.int32, (8, N), 1)
    brick_end = ((lane & (B - 1)) == B - 1) & (lane < N - 1)
    for i in range(XL // 8):
        rows = pl.ds(8 * i, 8)
        root, side = z_ref[1, rows], sides_ref[rows]
        after = pltpu.roll(root, N - 1, 1)
        beside = SHIFT_RATE * root + ext_ref[pl.ds(8 * i + 9, 8)] + ext_ref[pl.ds(8 * i + 7, 8)]
        beside = beside + jnp.where(lane < N - 1, after, 0.0) + jnp.where(lane > 0, pltpu.roll(root, 1, 1), 0.0)
        beside_ref[rows] = beside
        flux_y = jnp.where(brick_end, 0.5 * root * after * (side + pltpu.roll(side, N - 1, 1)), 0.0)
        source_ref[rows] = inner_ref[rows] + pltpu.roll(flux_y, 1, 1) - flux_y
        inverse_ref[rows] = 1.0 / (column_ref[rows, 0:1] + lam_ref[...])
    for x in range(BR, XL, BR):
        flux = 0.5 * ext_ref[x + 7 : x + 8] * ext_ref[x + 8 : x + 9] * (x_ends_ref[x - 1 : x] + x_ends_ref[x : x + 1])
        source_ref[x - 1 : x] = source_ref[x - 1 : x] - flux
        source_ref[x : x + 1] = source_ref[x : x + 1] + flux


def setup_kernel(
    place_ref, z_ref, beside_ref, inner_ref, x_ends_ref, partner_ref, outer_ref, xlo_ref, xhi_ref,
    even_ref, odd_ref, small_ref, column_ref, inverse_ref,
    diagonal_ref, source_ref, modes_ref, ends_ref, fold_ref,
):
    sign = (2 * place_ref[1] - 1).astype(F32)
    for i in range(XL // 8):
        rows = pl.ds(8 * i, 8)
        accel_z, root = z_ref[0, rows], z_ref[1, rows]
        root_p, root_o = partner_ref[1, rows], outer_ref[1, rows]
        diagonal_ref[rows] = root * (beside_ref[rows] + root_p + root_o) + jnp.where(root > 0.0, 0.0, 1.0)
        flux = root_p * (partner_ref[0, rows] + accel_z) - root_o * (accel_z + outer_ref[0, rows])
        source_ref[rows] = inner_ref[rows] + (0.5 * sign) * (root * flux)
    for at, rim_ref, sign in ((0, xlo_ref, 1.0), (XL - 1, xhi_ref, -1.0)):
        row = pl.ds(at, 1)
        face = z_ref[1, row] * rim_ref[0:1]
        diagonal_ref[row] = diagonal_ref[row] + face
        source_ref[row] = source_ref[row] + (0.5 * sign) * face * (x_ends_ref[row] + rim_ref[1:2])
    to_modes(source_ref, even_ref, odd_ref, small_ref, column_ref, inverse_ref, fold_ref, modes_ref, ends_ref)


def update_kernel(
    place_ref, modes_ref, all_ends_ref, z_ref, xlo_ref, xhi_ref, cut_ref, near_far_ref, even_ref, odd_ref,
    small_t_ref, column_ref, inverse_ref, update_ref, scaled_ref, rim_ref, work_ref,
):
    slab = place_ref[0]

    steps = [all_ends_ref[j, 8:16] - all_ends_ref[j + 1, 0:8] for j in range(SLABS - 1)]

    def jump(cut):
        at = jnp.clip(cut, 0, SLABS - 2)
        total = jnp.zeros((8, 128), F32)
        for j, step in enumerate(steps):
            total = total + cut_ref[at, j] * step
        return jnp.where(at == cut, total, 0.0)

    farther_low, low, high, farther_high = (jump(slab + m) for m in (-2, -1, 0, 1))
    near, far = near_far_ref[0], near_far_ref[1]
    before = all_ends_ref[jnp.maximum(slab - 1, 0), 8:16] - (near * low - far * farther_low)
    after = all_ends_ref[jnp.minimum(slab + 1, SLABS - 1), 0:8] - (far * farther_high - near * high)
    low_row, high_row = as_row(low), as_row(high)
    for i in range(XL // 8):
        rows = pl.ds(8 * i, 8)
        change = column_ref[rows, 2:3] * high_row - column_ref[rows, 1:2] * low_row
        work_ref[rows] = modes_ref[rows] - change * inverse_ref[rows]
    work_ref[0:XL] = of_table(small_t_ref, work_ref[0:XL])
    work_ref[XL : XL + 8] = jnp.concatenate([as_row(before), as_row(after), jnp.zeros((6, N), F32)], axis=0)
    even = by_table(work_ref[:, :H], even_ref, False)
    odd = by_table(work_ref[:, H:], odd_ref, False)
    work_ref[:, :H] = even
    work_ref[:, H:] = odd
    for i in range(XL // 8 + 1):
        rows = pl.ds(8 * i, 8)
        even = work_ref[rows, :H]
        odd = work_ref[rows, H:]
        value = jnp.concatenate([even + odd, mirrored(even - odd)], axis=1)
        if i < XL // 8:
            root = z_ref[1, rows]
            update_ref[rows] = jnp.where(root > 0.0, value, 0.0)
            scaled_ref[rows] = root * value
        else:
            rim_ref[0:1] = value[0:1] * xlo_ref[0:1]
            rim_ref[1:2] = value[1:2] * xhi_ref[0:1]


def own_image(value_ref, scaled_ref, rim_ref, z_ref, diagonal_ref, ext_ref):
    ext_ref[7:8] = rim_ref[0:1]
    ext_ref[XL + 8 : XL + 9] = rim_ref[1:2]
    ext_ref[8 : XL + 8] = scaled_ref[...]
    lane = lax.broadcasted_iota(jnp.int32, (8, N), 1)
    for i in range(XL // 8):
        rows = pl.ds(8 * i, 8)
        scaled = scaled_ref[rows]
        beside = ext_ref[pl.ds(8 * i + 9, 8)] + ext_ref[pl.ds(8 * i + 7, 8)]
        beside = beside + jnp.where(lane < N - 1, pltpu.roll(scaled, N - 1, 1), 0.0)
        beside = beside + jnp.where(lane > 0, pltpu.roll(scaled, 1, 1), 0.0)
        yield rows, diagonal_ref[rows] * value_ref[rows] - z_ref[1, rows] * beside


def own_kernel(value_ref, scaled_ref, rim_ref, z_ref, diagonal_ref, own_ref, ext_ref):
    for rows, image in own_image(value_ref, scaled_ref, rim_ref, z_ref, diagonal_ref, ext_ref):
        own_ref[rows] = image


def image_kernel(
    own_ref, partner_ref, outer_ref, z_ref, even_ref, odd_ref, small_ref, column_ref, inverse_ref,
    image_ref, modes_ref, ends_ref, fold_ref,
):
    for i in range(XL // 8):
        rows = pl.ds(8 * i, 8)
        image_ref[rows] = own_ref[rows] - z_ref[1, rows] * (partner_ref[rows] + outer_ref[rows])
    to_modes(image_ref, even_ref, odd_ref, small_ref, column_ref, inverse_ref, fold_ref, modes_ref, ends_ref)


def one_line(total):
    line = jnp.sum(total, axis=0, keepdims=True)
    return sum(line[:, t * 128 : (t + 1) * 128] for t in range(8))


def own_sums_kernel(
    value_ref, scaled_ref, rim_ref, z_ref, diagonal_ref, source_ref, update_ref, first_image_ref,
    own_ref, lines_ref, ext_ref,
):
    totals = [jnp.zeros((8, N), F32) for _ in range(4)]
    for rows, image in own_image(value_ref, scaled_ref, rim_ref, z_ref, diagonal_ref, ext_ref):
        own_ref[rows] = image
        v, r, u, q = value_ref[rows], source_ref[rows], update_ref[rows], first_image_ref[rows]
        for k, (a, b) in enumerate(((r, u), (u, q), (r, v), (q, v))):
            totals[k] = totals[k] + a * b
    lines_ref[...] = jnp.concatenate([one_line(total) for total in totals] + [jnp.zeros((4, 128), F32)], axis=0)


def sums_kernel(
    value_ref, own_ref, lines_ref, partner_ref, outer_ref, z_ref, update_ref, image_ref, sums_ref
):
    totals = [jnp.zeros((8, N), F32) for _ in range(2)]
    for i in range(XL // 8):
        rows = pl.ds(8 * i, 8)
        t = own_ref[rows] - z_ref[1, rows] * (partner_ref[rows] + outer_ref[rows])
        image_ref[rows] = t
        totals[0] = totals[0] + update_ref[rows] * t
        totals[1] = totals[1] + value_ref[rows] * t
    lines = jnp.concatenate([lines_ref[0:4]] + [one_line(total) for total in totals] + [jnp.zeros((2, 128), F32)], axis=0)
    for j in range(OWNERS):
        sums_ref[j] = lines


def add_kernel(sums_ref, out_ref):
    total = sums_ref[0]
    for j in range(1, OWNERS):
        total = total + sums_ref[j]
    for j in range(SLABS):
        out_ref[j] = total


def final_kernel(
    sums_ref, source_ref, u_ref, q_ref, v_ref, t_ref, solution_hbm, residual_hbm, solution_ref, residual_ref, sem
):
    total = sums_ref[0]
    for j in range(1, SLABS):
        total = total + sums_ref[j]
    total = jnp.sum(total, axis=1, keepdims=True)
    ru, uq, rv, qv, ut, vt = (total[k : k + 1] for k in range(6))
    step = ru / uq
    energy = ru - step * (rv + uq) + step * step * qv
    beta = energy / ru
    cross = uq - step * ut
    curve = cross - step * qv + step * step * vt
    curve = curve + beta * (cross + uq - step * qv) + beta * beta * uq
    second = energy / curve
    spread = lambda s: jnp.broadcast_to(s, (8, N))
    step, beta, second = spread(step), spread(beta), spread(second)
    copies = []
    size = XL // CHUNKS
    for i in range(XL // 8):
        rows = pl.ds(8 * i, 8)
        u, q = u_ref[rows], q_ref[rows]
        direction = u - step * v_ref[rows] + beta * u
        along = q - step * t_ref[rows] + beta * q
        solution_ref[rows] = step * u + second * direction
        residual_ref[rows] = source_ref[rows] - step * q - second * along
        if (8 * i + 8) % size == 0:
            done = pl.ds(8 * i + 8 - size, size)
            for k, (ref, hbm) in enumerate(((solution_ref, solution_hbm), (residual_ref, residual_hbm))):
                copy = pltpu.make_async_copy(ref.at[done], hbm.at[done], sem.at[k, 8 * i // size])
                copy.start()
                copies.append(copy)
    for copy in copies:
        copy.wait()


def shape(*dims):
    return pltpu.VMEM(dims, F32)


def call(kernel, out_shape, in_specs, out_specs, scratch=(), name=None):
    run = pl.pallas_call(
        kernel, out_shape=out_shape, in_specs=in_specs, out_specs=out_specs, scratch_shapes=list(scratch), name=name,
        compiler_params=pltpu.CompilerParams(vmem_limit_bytes=16 * 2**20),
    )

    def with_spaces(*operands):
        assert len(operands) == len(in_specs)
        return run(
            *(
                x if spec is SMEM else pltpu.with_memory_space_constraint(x, spec.memory_space)
                for x, spec in zip(operands, in_specs)
            )
        )

    return with_spaces


PLANE = (XL, N)
EXT = pltpu.VMEM((XL + 16, N), F32)
FOLD = pltpu.VMEM(PLANE, F32)


def on_device(camera_accel, camera_weight, brick_slot, brick_solid):
    constant = {name: jnp.asarray(value) for name, value in tables().items()}
    dct = (constant["even"], constant["odd"])
    place = jnp.stack([lax.axis_index("gx"), lax.axis_index("yz_2")])
    slabs, owners = lax.axis_size("gx"), lax.axis_size(YZ)
    up_x = [(i, i + 1) for i in range(slabs - 1)]
    down_x = [(b, a) for a, b in up_x]
    on_chip = [(0, 1), (1, 0)]
    off_chip = [pair for i in range(1, owners - 1, 2) for pair in ((i, i + 1), (i + 1, i))]

    def neighbours(value):
        outer = lax.ppermute(value, YZ, off_chip)
        return lax.ppermute(value, "yz_2", on_chip), outer

    send = call(
        pack_kernel,
        shape(OWNERS, SEND_ROWS, 128),
        [SMEM, HBM, HBM, HBM],
        VMEM,
        [
            pltpu.SMEM((1, PLANE_BRICKS), jnp.int32),
            pltpu.SMEM((OWNERS,), jnp.int32),
            pltpu.SMEM((OWNERS * PER_PAIR,), jnp.int32),
            pltpu.SMEM((OWNERS * PER_PAIR,), jnp.int32),
            pltpu.VMEM((PLANE_BRICKS, 3 * BR, B), F32),
            pltpu.VMEM((PLANE_BRICKS, BR, B), F32),
            pltpu.VMEM((PLANE_BRICKS, BR, B), F32),
            pltpu.VMEM((PLANE_BRICKS // GROUP, 8, B), F32),
            pltpu.SemaphoreType.DMA((2, CHUNKS)),
            pltpu.SemaphoreType.DMA,
        ],
        name="pack",
    )(place, brick_slot, camera_accel[0].reshape(PLANE_BRICKS, 3 * BR, B), camera_weight[0])
    got = lax.all_to_all(send, YZ, split_axis=0, concat_axis=0, tiled=True)
    z_fields, inner, x_ends, sides, first, last = call(
        place_kernel,
        (shape(2, *PLANE), shape(*PLANE), shape(*PLANE), shape(*PLANE), shape(2, N), shape(2, N)),
        [SMEM, VMEM],
        (VMEM,) * 6,
        [
            pltpu.SMEM((OWNERS, 1, B), F32),
            pltpu.SMEM((PLANE_BRICKS + 1,), jnp.int32),
            pltpu.SemaphoreType.DMA,
        ],
        name="place",
    )(brick_solid[0], got)
    partner, outer = neighbours(z_fields)
    xlo = lax.ppermute(last, "gx", up_x)
    xhi = lax.ppermute(first, "gx", down_x)
    beside, inner, inverse = call(
        prepare_kernel, (shape(*PLANE),) * 3, [VMEM] * 6, (VMEM,) * 3, [EXT], name="prepare"
    )(z_fields, inner, x_ends, sides, constant["column"], constant["lam_y"])
    slab_tables = (constant["column"], inverse)
    forward = dct + (constant["small"],) + slab_tables
    diagonal, source, modes, ends = call(
        setup_kernel,
        (shape(*PLANE), shape(*PLANE), shape(*PLANE), shape(SLABS, 16, 128)),
        [SMEM] + [VMEM] * 13,
        (VMEM,) * 4,
        [FOLD],
        name="setup",
    )(place, z_fields, beside, inner, x_ends, partner, outer, xlo, xhi, *forward)

    def updated(modes, ends):
        all_ends = lax.all_to_all(ends, "gx", split_axis=0, concat_axis=0, tiled=True)
        return call(
            update_kernel,
            (shape(*PLANE), shape(*PLANE), shape(2, N)),
            [SMEM] + [VMEM] * 12,
            (VMEM,) * 3,
            [pltpu.VMEM((XL + 8, N), F32)],
            name="update",
        )(
            place, modes, all_ends, z_fields, xlo, xhi, constant["cut"], constant["ends"],
            *dct, constant["small_t"], *slab_tables,
        )

    u, scaled, rim = updated(modes, ends)
    planes = neighbours(scaled)
    own = call(own_kernel, shape(*PLANE), [VMEM] * 5, VMEM, [EXT], name="own")(u, scaled, rim, z_fields, diagonal)
    q, modes, ends = call(
        image_kernel,
        (shape(*PLANE), shape(*PLANE), shape(SLABS, 16, 128)),
        [VMEM] * 9,
        (VMEM,) * 3,
        [FOLD],
        name="image",
    )(own, *planes, z_fields, *forward)
    v, scaled, rim = updated(modes, ends)
    planes = neighbours(scaled)
    own, lines = call(
        own_sums_kernel, (shape(*PLANE), shape(8, 128)), [VMEM] * 8, (VMEM, VMEM), [EXT], name="own_sums"
    )(v, scaled, rim, z_fields, diagonal, source, u, q)
    t, sums = call(
        sums_kernel,
        (shape(*PLANE), shape(OWNERS, 8, 128)),
        [VMEM] * 7,
        (VMEM, VMEM),
        name="sums",
    )(v, own, lines, *planes, z_fields, u)
    sums = lax.all_to_all(sums, YZ, split_axis=0, concat_axis=0, tiled=True)
    sums = call(add_kernel, shape(SLABS, 8, 128), [VMEM], VMEM, name="add")(sums)
    sums = lax.all_to_all(sums, "gx", split_axis=0, concat_axis=0, tiled=True)
    result, residual = call(
        final_kernel,
        (jax.ShapeDtypeStruct(PLANE, F32),) * 2,
        [VMEM] * 6,
        (HBM, HBM),
        [FOLD, FOLD, pltpu.SemaphoreType.DMA((2, CHUNKS))],
        name="final",
    )(sums, source, u, q, v, t)
    return result[None], residual[None]


def solution(mesh):
    finer = Mesh(mesh.devices.reshape(mesh.shape["gx"], 4, 4, 2), ("gx", "yz_0", "yz_1", "yz_2"))
    in_specs = (P("gx", YZ, None, None, None), P("gx", YZ, None, None), P("gx", YZ), P("gx", YZ))
    out_specs = (P(YZ, "gx", None), P(YZ, "gx", None))
    return jax.shard_map(
        on_device, mesh=finer, in_specs=in_specs, out_specs=out_specs, check_vma=False
    )
```

```python
import functools

import jax
import jax.numpy as jnp
import ml_dtypes
import numpy as np
from jax import lax
from jax.experimental import pallas as pl
from jax.experimental.pallas import tpu as pltpu
from jax.sharding import Mesh
from jax.sharding import PartitionSpec as P

N = 1024
H = N // 2
XL = 128
SLABS = 8
BR = 16
B = 128
PLANE_SHIFT = 6
PLANE_BRICKS = 1 << PLANE_SHIFT
OWNERS = 32
PEERS = 16
PER_PAIR = 3
BRICK_ROWS = 3 * BR
END_ROW = PER_PAIR * BRICK_ROWS
SIDE_ROW = END_ROW + 2 * PER_PAIR
ID_ROW = SIDE_ROW + 1
SEND_ROWS = END_ROW + 8
CHUNKS = 4
GROUP_SHIFT = 3
GROUP = 1 << GROUP_SHIFT
YZ = ("yz_0", "yz_1", "yz_2")
SHIFT_RATE = 0.05
FLOOR = 2.0
F32 = jnp.float32
BF16 = jnp.bfloat16
VMEM = pl.BlockSpec(memory_space=pltpu.VMEM)
SMEM = pl.BlockSpec(memory_space=pltpu.SMEM)
HBM = pl.BlockSpec(memory_space=pltpu.HBM)


def cosine_rows(length):
    k = np.arange(length, dtype=np.int64)[:, None]
    i = np.arange(length, dtype=np.int64)[None, :]
    m = (k * (2 * i + 1)) % (4 * length)
    scale = np.sqrt(np.where(k == 0, 1.0, 2.0) / length)
    return scale * np.cos(np.pi * m / (2.0 * length))


def two_bf16(table):
    high = table.astype(np.float32).astype(ml_dtypes.bfloat16)
    low = (table - high.astype(np.float64)).astype(np.float32).astype(ml_dtypes.bfloat16)
    return high, low


@functools.lru_cache(None)
def tables():
    out = {}
    big = cosine_rows(N)
    out["even"] = np.stack(two_bf16(big[0::2, :H]))
    out["odd"] = np.stack(two_bf16(big[1::2, :H]))
    small = cosine_rows(XL)
    out["small"] = np.concatenate(two_bf16(small), axis=0)
    out["small_t"] = np.concatenate(two_bf16(small.T.copy()), axis=0)
    lam_x = 2.0 - 2.0 * np.cos(np.pi * np.arange(XL) / XL)
    ky = np.concatenate([np.arange(0, N, 2), np.arange(1, N, 2)])
    lam_y = 2.0 - 2.0 * np.cos(np.pi * ky / N)
    column = np.zeros((XL, 128), np.float32)
    column[:, 0] = lam_x + FLOOR
    column[:, 1] = small[:, 0]
    column[:, 2] = small[:, XL - 1]
    out["column"] = column
    out["lam_y"] = lam_y.astype(np.float32)[None]
    denom = lam_x[:, None] + lam_y[None] + FLOOR
    near = np.sum(small[:, :1] ** 2 / denom, axis=0)
    far = np.sum(small[:, :1] * small[:, XL - 1 :] / denom, axis=0)
    cuts = SLABS - 1
    system = np.zeros((N, cuts, cuts))
    for j in range(cuts):
        system[:, j, j] = 1.0 + 2.0 * near
    for j in range(cuts - 1):
        system[:, j, j + 1] = -far
        system[:, j + 1, j] = -far
    inverse = np.linalg.inv(system)
    out["cut"] = inverse.transpose(1, 2, 0).astype(np.float32).reshape(cuts, cuts, 8, 128)
    out["ends"] = np.stack([near, far]).astype(np.float32).reshape(2, 8, 128)
    return out


def split(value):
    high = value.astype(BF16)
    return high, (value - high.astype(F32)).astype(BF16)


def product(a, b, transposed=False):
    dims = (((1,), (1 if transposed else 0,)), ((), ()))
    return lax.dot_general(a, b, dims, preferred_element_type=F32)


def by_table(data, table_ref, transposed):
    high, low = split(data)
    rows = data.shape[0]
    both = product(jnp.concatenate([high, low], axis=0), table_ref[0], transposed)
    return both[:rows] + both[rows:] + product(high, table_ref[1], transposed)


def of_table(table_ref, data):
    high, low = split(data)
    both = product(table_ref[...], high)
    return both[:XL] + both[XL:] + product(table_ref[:XL], low)


def mirrored(value):
    rows, width = value.shape
    index = 127 - lax.broadcasted_iota(jnp.int32, (rows, 128), 1)
    tiles = [
        jnp.take_along_axis(value[:, t * 128 : (t + 1) * 128], index, axis=1)
        for t in range(width // 128)
    ]
    return jnp.concatenate(tiles[::-1], axis=1)


def as_tile(row):
    return jnp.concatenate([row[:, t * 128 : (t + 1) * 128] for t in range(8)], axis=0)


def as_row(tile):
    return jnp.concatenate([tile[t : t + 1] for t in range(8)], axis=1)


def to_modes(field_ref, even_ref, odd_ref, small_ref, column_ref, inverse_ref, fold_ref, modes_ref, ends_ref):
    for i in range(XL // 8):
        rows = pl.ds(8 * i, 8)
        low = field_ref[rows, :H]
        high = mirrored(field_ref[rows, H:])
        fold_ref[rows, :H] = low + high
        fold_ref[rows, H:] = low - high
    spectrum = jnp.concatenate(
        [
            by_table(fold_ref[:, :H], even_ref, True),
            by_table(fold_ref[:, H:], odd_ref, True),
        ],
        axis=1,
    )
    modes_ref[...] = of_table(small_ref, spectrum)
    first = jnp.zeros((8, N), F32)
    last = jnp.zeros((8, N), F32)
    for i in range(XL // 8):
        rows = pl.ds(8 * i, 8)
        modes = modes_ref[rows, :] * inverse_ref[rows]
        modes_ref[rows, :] = modes
        first = first + modes * column_ref[rows, 1:2]
        last = last + modes * column_ref[rows, 2:3]
    first = as_tile(jnp.sum(first, axis=0, keepdims=True))
    last = as_tile(jnp.sum(last, axis=0, keepdims=True))
    for j in range(SLABS):
        ends_ref[j, 0:8] = first
        ends_ref[j, 8:16] = last


def pack_kernel(
    place_ref, slot_hbm, accel_hbm, weight_hbm, out_ref,
    slot_ref, count_ref, held_ref, number_ref, accel_ref, weight_ref, inner_ref, side_ref, sem, slot_sem,
):
    del place_ref
    slot_copy = pltpu.make_async_copy(slot_hbm, slot_ref, slot_sem)
    slot_copy.start()
    size = PLANE_BRICKS // CHUNKS
    copies = []
    for chunk in range(CHUNKS):
        bricks = pl.ds(chunk * size, size)
        copies.append(
            (
                pltpu.make_async_copy(accel_hbm.at[bricks], accel_ref.at[bricks], sem.at[0, chunk]),
                pltpu.make_async_copy(weight_hbm.at[bricks], weight_ref.at[bricks], sem.at[1, chunk]),
            )
        )
        for copy in copies[-1]:
            copy.start()
    for o in range(OWNERS):
        count_ref[o] = 0
    for k in range(OWNERS * PER_PAIR):
        held_ref[k] = 0
        number_ref[k] = -1
    slot_copy.wait()

    def assign(s, carry):
        brick = slot_ref[0, s]
        owner = brick >> PLANE_SHIFT
        place = count_ref[owner]
        count_ref[owner] = place + 1
        held_ref[owner * PER_PAIR + place] = s
        number_ref[owner * PER_PAIR + place] = brick & (PLANE_BRICKS - 1)
        return carry

    lax.fori_loop(0, PLANE_BRICKS, assign, 0, unroll=8)
    dims = (GROUP, BR, B)
    lane = lax.broadcasted_iota(jnp.int32, dims, 2)
    row = lax.broadcasted_iota(jnp.int32, dims, 1)
    few_lanes, few_rows = lane[0, :8], row[0, :8]
    edge = jnp.where((few_rows == 0) & (few_lanes == 0), 1.0, 0.0)
    edge = jnp.where((few_rows == 1) & (few_lanes == B - 1), 1.0, edge)

    def inside(group, carry):
        bricks = pl.ds(group * GROUP, GROUP)
        root = jnp.sqrt(weight_ref[bricks])
        weight_ref[bricks] = root
        accel_x = accel_ref[bricks, BR : 2 * BR]
        flux_x = root * pltpu.roll(root, BR - 1, 1) * (accel_x + pltpu.roll(accel_x, BR - 1, 1))
        flux_x = jnp.where(row < BR - 1, flux_x, 0.0)
        inner = pltpu.roll(flux_x, 1, 1) - flux_x
        accel_y = accel_ref[bricks, 2 * BR :]
        flux_y = root * pltpu.roll(root, B - 1, 2) * (accel_y + pltpu.roll(accel_y, B - 1, 2))
        flux_y = jnp.where(lane < B - 1, flux_y, 0.0)
        inner_ref[bricks] = 0.5 * (inner + pltpu.roll(flux_y, 1, 2) - flux_y)
        sides = lax.dot_general(
            edge, accel_y.reshape(GROUP * BR, B), (((1,), (1,)), ((), ())),
            precision=lax.Precision.HIGHEST, preferred_element_type=F32,
        )
        side_ref[group] = jnp.where(few_rows == 1, pltpu.roll(sides, BR, 1), sides)
        return carry

    for chunk in range(CHUNKS):
        for copy in copies[chunk]:
            copy.wait()
        lax.fori_loop(chunk * size // GROUP, (chunk + 1) * size // GROUP, inside, 0, unroll=2)

    def fill(owner, carry):
        ends = jnp.zeros((8, B), F32)
        for place in range(PER_PAIR):
            s = held_ref[owner * PER_PAIR + place]
            number = number_ref[owner * PER_PAIR + place].astype(F32)
            at = place * BRICK_ROWS
            out_ref[owner, at : at + BR] = accel_ref[s, :BR]
            out_ref[owner, at + BR : at + 2 * BR] = inner_ref[s]
            out_ref[owner, at + 2 * BR : at + 3 * BR] = weight_ref[s]
            ends = jnp.where(few_rows == 2 * place, accel_ref[s, BR : BR + 1], ends)
            ends = jnp.where(few_rows == 2 * place + 1, accel_ref[s, 2 * BR - 1 : 2 * BR], ends)
            sides = pltpu.roll(side_ref[s >> GROUP_SHIFT], (2 * BR * place - BR * (s & (GROUP - 1))) & (B - 1), 1)
            sides = jnp.where(few_lanes < 2 * BR * place + BR, sides[0:1], sides[1:2])
            ends = jnp.where((few_rows == SIDE_ROW - END_ROW) & (few_lanes >= 2 * BR * place), sides, ends)
            ends = jnp.where((few_rows == ID_ROW - END_ROW) & (few_lanes == place), number, ends)
        out_ref[owner, END_ROW:] = ends
        return carry

    lax.fori_loop(0, OWNERS, fill, 0, unroll=4)


def place_kernel(solid_ref, got_ref, z_ref, first_ref, last_ref, from_ref, origin_ref, sem):
    lane = lax.broadcasted_iota(jnp.int32, (OWNERS, B), 1)
    slot = (lax.broadcasted_iota(jnp.int32, (OWNERS, B), 0) << 2).astype(F32)
    numbers = got_ref[:, ID_ROW, :].astype(jnp.int32)
    origin = jnp.zeros((OWNERS, B), F32)
    for place in range(PER_PAIR):
        origin = origin + jnp.where(numbers[:, place : place + 1] == lane, slot + place, 0.0)
    origin_ref[...] = jnp.broadcast_to(jnp.sum(origin, axis=0, keepdims=True), (8, B)).astype(jnp.int32)
    copy = pltpu.make_async_copy(origin_ref.at[pl.ds(0, 1)], from_ref, sem)
    copy.start()
    copy.wait()

    def line(x, carry):
        rows = pl.ds(pl.multiple_of(x * BR, BR), BR)
        for y in range(N // B):
            cols = pl.ds(y * B, B)
            held = from_ref[0, x * (N // B) + y]
            source, place = held >> 2, held & 3
            fluid = (1 - solid_ref[x * (N // B) + y]).astype(F32)
            at = pl.multiple_of(place * BRICK_ROWS, BR)
            z_ref[0, rows, cols] = got_ref[source, pl.ds(at, BR)]
            z_ref[1, rows, cols] = got_ref[source, pl.ds(at + 2 * BR, BR)] * fluid
        return carry

    lax.fori_loop(0, XL // BR, line, 0)
    for ref, row, end in ((first_ref, 0, 0), (last_ref, XL - 1, 1)):
        ref[0:1] = z_ref[1, row : row + 1]
        for y in range(N // B):
            held = from_ref[0, row // BR * (N // B) + y]
            ref[1:2, y * B : (y + 1) * B] = got_ref[held >> 2, pl.ds(END_ROW + end + 2 * (held & 3), 1)]


def place_rest_kernel(solid_ref, from_ref, got_ref, source_ref, ends_ref, sides_ref):
    lane = lax.broadcasted_iota(jnp.int32, (BR, B), 1)
    row = lax.broadcasted_iota(jnp.int32, (BR, B), 0)

    def line(x, carry):
        rows = pl.ds(pl.multiple_of(x * BR, BR), BR)
        for y in range(N // B):
            cols = pl.ds(y * B, B)
            held = from_ref[0, x * (N // B) + y]
            source, place = held >> 2, held & 3
            fluid = (1 - solid_ref[x * (N // B) + y]).astype(F32)
            at = pl.multiple_of(place * BRICK_ROWS, BR)
            source_ref[rows, cols] = got_ref[source, pl.ds(at + BR, BR)] * fluid
            sides = jnp.broadcast_to(got_ref[source, SIDE_ROW : SIDE_ROW + 1], (BR, B))
            own = lane - row - 2 * BR * place
            low = jnp.sum(jnp.where(own == 0, sides, 0.0), axis=1, keepdims=True)
            high = jnp.sum(jnp.where(own == BR, sides, 0.0), axis=1, keepdims=True)
            sides_ref[rows, cols] = jnp.where(lane == 0, low, high)
            first = got_ref[source, pl.ds(END_ROW + 2 * place, 1)]
            last = got_ref[source, pl.ds(END_ROW + 1 + 2 * place, 1)]
            ends_ref[rows, cols] = jnp.where(row < BR // 2, first, last)
        return carry

    lax.fori_loop(0, XL // BR, line, 0)


def prepare_kernel(
    z_ref, inner_ref, x_ends_ref, sides_ref, column_ref, lam_ref, beside_ref, source_ref, inverse_ref, ext_ref
):
    ext_ref[7:8] = jnp.zeros((1, N), F32)
    ext_ref[XL + 8 : XL + 9] = jnp.zeros((1, N), F32)
    ext_ref[8 : XL + 8] = z_ref[1]
    lane = lax.broadcasted_iota(jnp.int32, (8, N), 1)
    brick_end = ((lane & (B - 1)) == B - 1) & (lane < N - 1)
    for i in range(XL // 8):
        rows = pl.ds(8 * i, 8)
        root, side = z_ref[1, rows], sides_ref[rows]
        after = pltpu.roll(root, N - 1, 1)
        beside = SHIFT_RATE * root + ext_ref[pl.ds(8 * i + 9, 8)] + ext_ref[pl.ds(8 * i + 7, 8)]
        beside = beside + jnp.where(lane < N - 1, after, 0.0) + jnp.where(lane > 0, pltpu.roll(root, 1, 1), 0.0)
        beside_ref[rows] = beside
        flux_y = jnp.where(brick_end, 0.5 * root * after * (side + pltpu.roll(side, N - 1, 1)), 0.0)
        source_ref[rows] = inner_ref[rows] + pltpu.roll(flux_y, 1, 1) - flux_y
        inverse_ref[rows] = 1.0 / (column_ref[rows, 0:1] + lam_ref[...])
    for x in range(BR, XL, BR):
        flux = 0.5 * ext_ref[x + 7 : x + 8] * ext_ref[x + 8 : x + 9] * (x_ends_ref[x - 1 : x] + x_ends_ref[x : x + 1])
        source_ref[x - 1 : x] = source_ref[x - 1 : x] - flux
        source_ref[x : x + 1] = source_ref[x : x + 1] + flux


def setup_kernel(
    place_ref, z_ref, beside_ref, inner_ref, x_ends_ref, partner_ref, outer_ref, xlo_ref, xhi_ref,
    even_ref, odd_ref, small_ref, column_ref, inverse_ref,
    diagonal_ref, source_ref, modes_ref, ends_ref, fold_ref,
):
    sign = (2 * place_ref[1] - 1).astype(F32)
    for i in range(XL // 8):
        rows = pl.ds(8 * i, 8)
        accel_z, root = z_ref[0, rows], z_ref[1, rows]
        root_p, root_o = partner_ref[1, rows], outer_ref[1, rows]
        diagonal_ref[rows] = root * (beside_ref[rows] + root_p + root_o) + jnp.where(root > 0.0, 0.0, 1.0)
        flux = root_p * (partner_ref[0, rows] + accel_z) - root_o * (accel_z + outer_ref[0, rows])
        source_ref[rows] = inner_ref[rows] + (0.5 * sign) * (root * flux)
    for at, rim_ref, sign in ((0, xlo_ref, 1.0), (XL - 1, xhi_ref, -1.0)):
        row = pl.ds(at, 1)
        face = z_ref[1, row] * rim_ref[0:1]
        diagonal_ref[row] = diagonal_ref[row] + face
        source_ref[row] = source_ref[row] + (0.5 * sign) * face * (x_ends_ref[row] + rim_ref[1:2])
    to_modes(source_ref, even_ref, odd_ref, small_ref, column_ref, inverse_ref, fold_ref, modes_ref, ends_ref)


def update_kernel(
    place_ref, modes_ref, all_ends_ref, z_ref, xlo_ref, xhi_ref, cut_ref, near_far_ref, even_ref, odd_ref,
    small_t_ref, column_ref, inverse_ref, update_ref, scaled_ref, rim_ref, work_ref,
):
    slab = place_ref[0]

    steps = [all_ends_ref[j, 8:16] - all_ends_ref[j + 1, 0:8] for j in range(SLABS - 1)]

    def jump(cut):
        at = jnp.clip(cut, 0, SLABS - 2)
        total = jnp.zeros((8, 128), F32)
        for j, step in enumerate(steps):
            total = total + cut_ref[at, j] * step
        return jnp.where(at == cut, total, 0.0)

    farther_low, low, high, farther_high = (jump(slab + m) for m in (-2, -1, 0, 1))
    near, far = near_far_ref[0], near_far_ref[1]
    before = all_ends_ref[jnp.maximum(slab - 1, 0), 8:16] - (near * low - far * farther_low)
    after = all_ends_ref[jnp.minimum(slab + 1, SLABS - 1), 0:8] - (far * farther_high - near * high)
    low_row, high_row = as_row(low), as_row(high)
    for i in range(XL // 8):
        rows = pl.ds(8 * i, 8)
        change = column_ref[rows, 2:3] * high_row - column_ref[rows, 1:2] * low_row
        work_ref[rows] = modes_ref[rows] - change * inverse_ref[rows]
    work_ref[0:XL] = of_table(small_t_ref, work_ref[0:XL])
    work_ref[XL : XL + 8] = jnp.concatenate([as_row(before), as_row(after), jnp.zeros((6, N), F32)], axis=0)
    even = by_table(work_ref[:, :H], even_ref, False)
    odd = by_table(work_ref[:, H:], odd_ref, False)
    work_ref[:, :H] = even
    work_ref[:, H:] = odd
    for i in range(XL // 8 + 1):
        rows = pl.ds(8 * i, 8)
        even = work_ref[rows, :H]
        odd = work_ref[rows, H:]
        value = jnp.concatenate([even + odd, mirrored(even - odd)], axis=1)
        if i < XL // 8:
            root = z_ref[1, rows]
            update_ref[rows] = jnp.where(root > 0.0, value, 0.0)
            scaled_ref[rows] = root * value
        else:
            rim_ref[0:1] = value[0:1] * xlo_ref[0:1]
            rim_ref[1:2] = value[1:2] * xhi_ref[0:1]


def own_image(value_ref, scaled_ref, rim_ref, z_ref, diagonal_ref, ext_ref):
    ext_ref[7:8] = rim_ref[0:1]
    ext_ref[XL + 8 : XL + 9] = rim_ref[1:2]
    ext_ref[8 : XL + 8] = scaled_ref[...]
    lane = lax.broadcasted_iota(jnp.int32, (8, N), 1)
    for i in range(XL // 8):
        rows = pl.ds(8 * i, 8)
        scaled = scaled_ref[rows]
        beside = ext_ref[pl.ds(8 * i + 9, 8)] + ext_ref[pl.ds(8 * i + 7, 8)]
        beside = beside + jnp.where(lane < N - 1, pltpu.roll(scaled, N - 1, 1), 0.0)
        beside = beside + jnp.where(lane > 0, pltpu.roll(scaled, 1, 1), 0.0)
        yield rows, diagonal_ref[rows] * value_ref[rows] - z_ref[1, rows] * beside


def own_kernel(value_ref, scaled_ref, rim_ref, z_ref, diagonal_ref, own_ref, ext_ref):
    for rows, image in own_image(value_ref, scaled_ref, rim_ref, z_ref, diagonal_ref, ext_ref):
        own_ref[rows] = image


def image_kernel(
    own_ref, partner_ref, outer_ref, z_ref, even_ref, odd_ref, small_ref, column_ref, inverse_ref,
    image_ref, modes_ref, ends_ref, fold_ref,
):
    for i in range(XL // 8):
        rows = pl.ds(8 * i, 8)
        image_ref[rows] = own_ref[rows] - z_ref[1, rows] * (partner_ref[rows] + outer_ref[rows])
    to_modes(image_ref, even_ref, odd_ref, small_ref, column_ref, inverse_ref, fold_ref, modes_ref, ends_ref)


def one_line(total):
    line = jnp.sum(total, axis=0, keepdims=True)
    return sum(line[:, t * 128 : (t + 1) * 128] for t in range(8))


def own_sums_kernel(
    value_ref, scaled_ref, rim_ref, z_ref, diagonal_ref, source_ref, update_ref, first_image_ref,
    own_ref, lines_ref, ext_ref,
):
    totals = [jnp.zeros((8, N), F32) for _ in range(4)]
    for rows, image in own_image(value_ref, scaled_ref, rim_ref, z_ref, diagonal_ref, ext_ref):
        own_ref[rows] = image
        v, r, u, q = value_ref[rows], source_ref[rows], update_ref[rows], first_image_ref[rows]
        for k, (a, b) in enumerate(((r, u), (u, q), (r, v), (q, v))):
            totals[k] = totals[k] + a * b
    lines_ref[...] = jnp.concatenate([one_line(total) for total in totals] + [jnp.zeros((4, 128), F32)], axis=0)


def sums_kernel(
    value_ref, own_ref, lines_ref, partner_ref, outer_ref, z_ref, update_ref, image_ref, sums_ref
):
    totals = [jnp.zeros((8, N), F32) for _ in range(2)]
    for i in range(XL // 8):
        rows = pl.ds(8 * i, 8)
        t = own_ref[rows] - z_ref[1, rows] * (partner_ref[rows] + outer_ref[rows])
        image_ref[rows] = t
        totals[0] = totals[0] + update_ref[rows] * t
        totals[1] = totals[1] + value_ref[rows] * t
    lines = jnp.concatenate([lines_ref[0:4]] + [one_line(total) for total in totals] + [jnp.zeros((2, 128), F32)], axis=0)
    index = [lax.broadcasted_iota(jnp.int32, (8, 128), k) for k in range(2)]
    line = jnp.where(index[0] == index[1], jnp.sum(lines, axis=1, keepdims=True), 0.0)
    line = jnp.sum(line, axis=0, keepdims=True)
    for j in range(PEERS):
        sums_ref[j] = line


def add_kernel(sums_ref, out_ref):
    total = sums_ref[0]
    for j in range(1, PEERS):
        total = total + sums_ref[j]
    for j in range(PEERS):
        out_ref[j] = total


def final_kernel(
    sums_ref, source_ref, u_ref, q_ref, v_ref, t_ref, solution_hbm, residual_hbm, solution_ref, residual_ref, sem
):
    total = sums_ref[0]
    for j in range(1, PEERS):
        total = total + sums_ref[j]
    index = [lax.broadcasted_iota(jnp.int32, (8, 128), k) for k in range(2)]
    total = jnp.where(index[0] == index[1], jnp.broadcast_to(total, (8, 128)), 0.0)
    total = jnp.sum(total, axis=1, keepdims=True)
    ru, uq, rv, qv, ut, vt = (total[k : k + 1] for k in range(6))
    step = ru / uq
    energy = ru - step * (rv + uq) + step * step * qv
    beta = energy / ru
    cross = uq - step * ut
    curve = cross - step * qv + step * step * vt
    curve = curve + beta * (cross + uq - step * qv) + beta * beta * uq
    second = energy / curve
    spread = lambda s: jnp.broadcast_to(s, (8, N))
    step, beta, second = spread(step), spread(beta), spread(second)
    copies = []
    size = XL // CHUNKS
    for i in range(XL // 8):
        rows = pl.ds(8 * i, 8)
        u, q = u_ref[rows], q_ref[rows]
        direction = u - step * v_ref[rows] + beta * u
        along = q - step * t_ref[rows] + beta * q
        solution_ref[rows] = step * u + second * direction
        residual_ref[rows] = source_ref[rows] - step * q - second * along
        if (8 * i + 8) % size == 0:
            done = pl.ds(8 * i + 8 - size, size)
            for k, (ref, hbm) in enumerate(((solution_ref, solution_hbm), (residual_ref, residual_hbm))):
                copy = pltpu.make_async_copy(ref.at[done], hbm.at[done], sem.at[k, 8 * i // size])
                copy.start()
                copies.append(copy)
    for copy in copies:
        copy.wait()


def shape(*dims):
    return pltpu.VMEM(dims, F32)


def call(kernel, out_shape, in_specs, out_specs, scratch=(), name=None):
    run = pl.pallas_call(
        kernel, out_shape=out_shape, in_specs=in_specs, out_specs=out_specs, scratch_shapes=list(scratch), name=name,
        compiler_params=pltpu.CompilerParams(vmem_limit_bytes=16 * 2**20),
    )

    def with_spaces(*operands):
        assert len(operands) == len(in_specs)
        return run(
            *(
                x if spec is SMEM else pltpu.with_memory_space_constraint(x, spec.memory_space)
                for x, spec in zip(operands, in_specs)
            )
        )

    return with_spaces


PLANE = (XL, N)
EXT = pltpu.VMEM((XL + 16, N), F32)
FOLD = pltpu.VMEM(PLANE, F32)


def on_device(camera_accel, camera_weight, brick_slot, brick_solid):
    constant = {name: jnp.asarray(value) for name, value in tables().items()}
    dct = (constant["even"], constant["odd"])
    place = jnp.stack([lax.axis_index("gx"), lax.axis_index("yz_2")])
    slabs, owners = lax.axis_size("gx"), lax.axis_size(YZ)
    up_x = [(i, i + 1) for i in range(slabs - 1)]
    down_x = [(b, a) for a, b in up_x]
    on_chip = [(0, 1), (1, 0)]
    off_chip = [pair for i in range(1, owners - 1, 2) for pair in ((i, i + 1), (i + 1, i))]

    def neighbours(value):
        outer = lax.ppermute(value, YZ, off_chip)
        return lax.ppermute(value, "yz_2", on_chip), outer

    send = call(
        pack_kernel,
        shape(OWNERS, SEND_ROWS, 128),
        [SMEM, HBM, HBM, HBM],
        VMEM,
        [
            pltpu.SMEM((1, PLANE_BRICKS), jnp.int32),
            pltpu.SMEM((OWNERS,), jnp.int32),
            pltpu.SMEM((OWNERS * PER_PAIR,), jnp.int32),
            pltpu.SMEM((OWNERS * PER_PAIR,), jnp.int32),
            pltpu.VMEM((PLANE_BRICKS, 3 * BR, B), F32),
            pltpu.VMEM((PLANE_BRICKS, BR, B), F32),
            pltpu.VMEM((PLANE_BRICKS, BR, B), F32),
            pltpu.VMEM((PLANE_BRICKS // GROUP, 8, B), F32),
            pltpu.SemaphoreType.DMA((2, CHUNKS)),
            pltpu.SemaphoreType.DMA,
        ],
        name="pack",
    )(place, brick_slot, camera_accel[0].reshape(PLANE_BRICKS, 3 * BR, B), camera_weight[0])
    got = lax.all_to_all(send, YZ, split_axis=0, concat_axis=0, tiled=True)
    z_fields, first, last, origin = call(
        place_kernel,
        (shape(2, *PLANE), shape(2, N), shape(2, N), jax.ShapeDtypeStruct((1, B), jnp.int32)),
        [SMEM, VMEM],
        (VMEM,) * 3 + (SMEM,),
        [pltpu.VMEM((8, B), jnp.int32), pltpu.SemaphoreType.DMA],
        name="place",
    )(brick_solid[0], got)
    partner, outer = neighbours(z_fields)
    xlo = lax.ppermute(last, "gx", up_x)
    xhi = lax.ppermute(first, "gx", down_x)
    inner, x_ends, sides = call(
        place_rest_kernel, (shape(*PLANE),) * 3, [SMEM, SMEM, VMEM], (VMEM,) * 3, name="place_rest"
    )(brick_solid[0], origin, got)
    beside, inner, inverse = call(
        prepare_kernel, (shape(*PLANE),) * 3, [VMEM] * 6, (VMEM,) * 3, [EXT], name="prepare"
    )(z_fields, inner, x_ends, sides, constant["column"], constant["lam_y"])
    slab_tables = (constant["column"], inverse)
    forward = dct + (constant["small"],) + slab_tables
    diagonal, source, modes, ends = call(
        setup_kernel,
        (shape(*PLANE), shape(*PLANE), shape(*PLANE), shape(SLABS, 16, 128)),
        [SMEM] + [VMEM] * 13,
        (VMEM,) * 4,
        [FOLD],
        name="setup",
    )(place, z_fields, beside, inner, x_ends, partner, outer, xlo, xhi, *forward)

    def updated(modes, ends):
        all_ends = lax.all_to_all(ends, "gx", split_axis=0, concat_axis=0, tiled=True)
        return call(
            update_kernel,
            (shape(*PLANE), shape(*PLANE), shape(2, N)),
            [SMEM] + [VMEM] * 12,
            (VMEM,) * 3,
            [pltpu.VMEM((XL + 8, N), F32)],
            name="update",
        )(
            place, modes, all_ends, z_fields, xlo, xhi, constant["cut"], constant["ends"],
            *dct, constant["small_t"], *slab_tables,
        )

    u, scaled, rim = updated(modes, ends)
    planes = neighbours(scaled)
    own = call(own_kernel, shape(*PLANE), [VMEM] * 5, VMEM, [EXT], name="own")(u, scaled, rim, z_fields, diagonal)
    q, modes, ends = call(
        image_kernel,
        (shape(*PLANE), shape(*PLANE), shape(SLABS, 16, 128)),
        [VMEM] * 9,
        (VMEM,) * 3,
        [FOLD],
        name="image",
    )(own, *planes, z_fields, *forward)
    v, scaled, rim = updated(modes, ends)
    planes = neighbours(scaled)
    own, lines = call(
        own_sums_kernel, (shape(*PLANE), shape(8, 128)), [VMEM] * 8, (VMEM, VMEM), [EXT], name="own_sums"
    )(v, scaled, rim, z_fields, diagonal, source, u, q)
    t, sums = call(
        sums_kernel,
        (shape(*PLANE), shape(PEERS, 1, 128)),
        [VMEM] * 7,
        (VMEM, VMEM),
        name="sums",
    )(v, own, lines, *planes, z_fields, u)
    sums = lax.all_to_all(sums, ("gx", "yz_2"), split_axis=0, concat_axis=0, tiled=True)
    sums = call(add_kernel, shape(PEERS, 1, 128), [VMEM], VMEM, name="add")(sums)
    sums = lax.all_to_all(sums, ("yz_0", "yz_1"), split_axis=0, concat_axis=0, tiled=True)
    result, residual = call(
        final_kernel,
        (jax.ShapeDtypeStruct(PLANE, F32),) * 2,
        [VMEM] * 6,
        (HBM, HBM),
        [FOLD, FOLD, pltpu.SemaphoreType.DMA((2, CHUNKS))],
        name="final",
    )(sums, source, u, q, v, t)
    return result[None], residual[None]


def solution(mesh):
    finer = Mesh(mesh.devices.reshape(mesh.shape["gx"], 4, 4, 2), ("gx", "yz_0", "yz_1", "yz_2"))
    in_specs = (P("gx", YZ, None, None, None), P("gx", YZ, None, None), P("gx", YZ), P("gx", YZ))
    out_specs = (P(YZ, "gx", None), P(YZ, "gx", None))
    return jax.shard_map(
        on_device, mesh=finer, in_specs=in_specs, out_specs=out_specs, check_vma=False
    )
```

```python
import functools

import jax
import jax.numpy as jnp
import ml_dtypes
import numpy as np
from jax import lax
from jax.experimental import pallas as pl
from jax.experimental.pallas import tpu as pltpu
from jax.sharding import Mesh
from jax.sharding import PartitionSpec as P

N = 1024
H = N // 2
XL = 128
SLABS = 8
BR = 16
B = 128
PLANE_SHIFT = 6
PLANE_BRICKS = 1 << PLANE_SHIFT
OWNERS = 32
PEERS = 16
PER_PAIR = 3
BRICK_ROWS = 3 * BR
END_ROW = PER_PAIR * BRICK_ROWS
SIDE_ROW = END_ROW + 2 * PER_PAIR
ID_ROW = SIDE_ROW + 1
SEND_ROWS = END_ROW + 8
CHUNKS = 4
GROUP_SHIFT = 3
GROUP = 1 << GROUP_SHIFT
YZ = ("yz_0", "yz_1", "yz_2")
SHIFT_RATE = 0.05
FLOOR = 2.0
F32 = jnp.float32
BF16 = jnp.bfloat16
VMEM = pl.BlockSpec(memory_space=pltpu.VMEM)
SMEM = pl.BlockSpec(memory_space=pltpu.SMEM)
HBM = pl.BlockSpec(memory_space=pltpu.HBM)


def cosine_rows(length):
    k = np.arange(length, dtype=np.int64)[:, None]
    i = np.arange(length, dtype=np.int64)[None, :]
    m = (k * (2 * i + 1)) % (4 * length)
    scale = np.sqrt(np.where(k == 0, 1.0, 2.0) / length)
    return scale * np.cos(np.pi * m / (2.0 * length))


def two_bf16(table):
    high = table.astype(np.float32).astype(ml_dtypes.bfloat16)
    low = (table - high.astype(np.float64)).astype(np.float32).astype(ml_dtypes.bfloat16)
    return high, low


@functools.lru_cache(None)
def tables():
    out = {}
    big = cosine_rows(N)
    out["even"] = np.stack(two_bf16(big[0::2, :H]))
    out["odd"] = np.stack(two_bf16(big[1::2, :H]))
    small = cosine_rows(XL)
    out["small"] = np.concatenate(two_bf16(small), axis=0)
    out["small_t"] = np.concatenate(two_bf16(small.T.copy()), axis=0)
    lam_x = 2.0 - 2.0 * np.cos(np.pi * np.arange(XL) / XL)
    ky = np.concatenate([np.arange(0, N, 2), np.arange(1, N, 2)])
    lam_y = 2.0 - 2.0 * np.cos(np.pi * ky / N)
    column = np.zeros((XL, 128), np.float32)
    column[:, 0] = lam_x + FLOOR
    column[:, 1] = small[:, 0]
    out["column"] = column
    out["lam_y"] = lam_y.astype(np.float32)[None]
    denom = lam_x[:, None] + lam_y[None] + FLOOR
    near = np.sum(small[:, :1] ** 2 / denom, axis=0)
    far = np.sum(small[:, :1] * small[:, XL - 1 :] / denom, axis=0)
    cuts = SLABS - 1
    system = np.zeros((N, cuts, cuts))
    for j in range(cuts):
        system[:, j, j] = 1.0 + 2.0 * near
    for j in range(cuts - 1):
        system[:, j, j + 1] = -far
        system[:, j + 1, j] = -far
    inverse = np.linalg.inv(system)
    out["cut"] = inverse.transpose(1, 2, 0).astype(np.float32).reshape(cuts, cuts, 8, 128)
    out["ends"] = np.stack([near, far]).astype(np.float32).reshape(2, 8, 128)
    return out


def split(value):
    high = value.astype(BF16)
    return high, (value - high.astype(F32)).astype(BF16)


def product(a, b, transposed=False):
    dims = (((1,), (1 if transposed else 0,)), ((), ()))
    return lax.dot_general(a, b, dims, preferred_element_type=F32)


def by_table(data, table_ref, transposed):
    high, low = split(data)
    rows = data.shape[0]
    both = product(jnp.concatenate([high, low], axis=0), table_ref[0], transposed)
    return both[:rows] + both[rows:] + product(high, table_ref[1], transposed)


def of_table(table_ref, data):
    high, low = split(data)
    both = product(table_ref[...], high)
    return both[:XL] + both[XL:] + product(table_ref[:XL], low)


def mirrored(value):
    rows, width = value.shape
    index = 127 - lax.broadcasted_iota(jnp.int32, (rows, 128), 1)
    tiles = [
        jnp.take_along_axis(value[:, t * 128 : (t + 1) * 128], index, axis=1)
        for t in range(width // 128)
    ]
    return jnp.concatenate(tiles[::-1], axis=1)


def as_tile(row):
    return jnp.concatenate([row[:, t * 128 : (t + 1) * 128] for t in range(8)], axis=0)


def as_row(tile):
    return jnp.concatenate([tile[t : t + 1] for t in range(8)], axis=1)


def to_modes(field_ref, even_ref, odd_ref, small_ref, column_ref, inverse_ref, fold_ref, modes_ref, ends_ref):
    for i in range(XL // 8):
        rows = pl.ds(8 * i, 8)
        low = field_ref[rows, :H]
        high = mirrored(field_ref[rows, H:])
        fold_ref[rows, :H] = low + high
        fold_ref[rows, H:] = low - high
    spectrum = jnp.concatenate(
        [
            by_table(fold_ref[:, :H], even_ref, True),
            by_table(fold_ref[:, H:], odd_ref, True),
        ],
        axis=1,
    )
    modes_ref[...] = of_table(small_ref, spectrum)
    total = jnp.zeros((8, N), F32)
    for i in range(XL // 8):
        rows = pl.ds(8 * i, 8)
        modes = modes_ref[rows, :] * inverse_ref[rows]
        modes_ref[rows, :] = modes
        total = total + modes * column_ref[rows, 1:2]
    odd = (lax.broadcasted_iota(jnp.int32, (8, N), 0) & 1) == 1
    first = as_tile(jnp.sum(total, axis=0, keepdims=True))
    last = as_tile(jnp.sum(jnp.where(odd, -total, total), axis=0, keepdims=True))
    for j in range(SLABS):
        ends_ref[j, 0:8] = first
        ends_ref[j, 8:16] = last


def pack_kernel(
    place_ref, slot_hbm, accel_hbm, weight_hbm, out_ref,
    slot_ref, count_ref, held_ref, number_ref, accel_ref, weight_ref, inner_ref, side_ref, sem, slot_sem,
):
    del place_ref
    slot_copy = pltpu.make_async_copy(slot_hbm, slot_ref, slot_sem)
    slot_copy.start()
    size = PLANE_BRICKS // CHUNKS
    copies = []
    for chunk in range(CHUNKS):
        bricks = pl.ds(chunk * size, size)
        copies.append(
            (
                pltpu.make_async_copy(accel_hbm.at[bricks], accel_ref.at[bricks], sem.at[0, chunk]),
                pltpu.make_async_copy(weight_hbm.at[bricks], weight_ref.at[bricks], sem.at[1, chunk]),
            )
        )
        for copy in copies[-1]:
            copy.start()
    for o in range(OWNERS):
        count_ref[o] = 0
    for k in range(OWNERS * PER_PAIR):
        held_ref[k] = 0
        number_ref[k] = -1
    slot_copy.wait()

    def assign(s, carry):
        brick = slot_ref[0, s]
        owner = brick >> PLANE_SHIFT
        place = count_ref[owner]
        count_ref[owner] = place + 1
        held_ref[owner * PER_PAIR + place] = s
        number_ref[owner * PER_PAIR + place] = brick & (PLANE_BRICKS - 1)
        return carry

    lax.fori_loop(0, PLANE_BRICKS, assign, 0, unroll=8)
    dims = (GROUP, BR, B)
    lane = lax.broadcasted_iota(jnp.int32, dims, 2)
    row = lax.broadcasted_iota(jnp.int32, dims, 1)
    few_lanes, few_rows = lane[0, :8], row[0, :8]
    edge = jnp.where((few_rows == 0) & (few_lanes == 0), 1.0, 0.0)
    edge = jnp.where((few_rows == 1) & (few_lanes == B - 1), 1.0, edge).astype(BF16)

    def inside(group, carry):
        bricks = pl.ds(group * GROUP, GROUP)
        root = jnp.sqrt(weight_ref[bricks])
        weight_ref[bricks] = root
        accel_x = accel_ref[bricks, BR : 2 * BR]
        flux_x = root * pltpu.roll(root, BR - 1, 1) * (accel_x + pltpu.roll(accel_x, BR - 1, 1))
        flux_x = jnp.where(row < BR - 1, flux_x, 0.0)
        inner = pltpu.roll(flux_x, 1, 1) - flux_x
        accel_y = accel_ref[bricks, 2 * BR :]
        flux_y = root * pltpu.roll(root, B - 1, 2) * (accel_y + pltpu.roll(accel_y, B - 1, 2))
        flux_y = jnp.where(lane < B - 1, flux_y, 0.0)
        inner_ref[bricks] = 0.5 * (inner + pltpu.roll(flux_y, 1, 2) - flux_y)
        flat = accel_y.reshape(GROUP * BR, B)
        high, middle = split(flat)
        low = (flat - high.astype(F32) - middle.astype(F32)).astype(BF16)
        sides = product(edge, high, True) + product(edge, middle, True) + product(edge, low, True)
        side_ref[group] = jnp.where(few_rows == 1, pltpu.roll(sides, BR, 1), sides)
        return carry

    for chunk in range(CHUNKS):
        for copy in copies[chunk]:
            copy.wait()
        lax.fori_loop(chunk * size // GROUP, (chunk + 1) * size // GROUP, inside, 0, unroll=2)

    def fill(owner, carry):
        ends = jnp.zeros((8, B), F32)
        for place in range(PER_PAIR):
            s = held_ref[owner * PER_PAIR + place]
            number = number_ref[owner * PER_PAIR + place].astype(F32)
            at = place * BRICK_ROWS
            out_ref[owner, at : at + BR] = accel_ref[s, :BR]
            out_ref[owner, at + BR : at + 2 * BR] = inner_ref[s]
            out_ref[owner, at + 2 * BR : at + 3 * BR] = weight_ref[s]
            ends = jnp.where(few_rows == 2 * place, accel_ref[s, BR : BR + 1], ends)
            ends = jnp.where(few_rows == 2 * place + 1, accel_ref[s, 2 * BR - 1 : 2 * BR], ends)
            sides = pltpu.roll(side_ref[s >> GROUP_SHIFT], (2 * BR * place - BR * (s & (GROUP - 1))) & (B - 1), 1)
            sides = jnp.where(few_lanes < 2 * BR * place + BR, sides[0:1], sides[1:2])
            ends = jnp.where((few_rows == SIDE_ROW - END_ROW) & (few_lanes >= 2 * BR * place), sides, ends)
            ends = jnp.where((few_rows == ID_ROW - END_ROW) & (few_lanes == place), number, ends)
        out_ref[owner, END_ROW:] = ends
        return carry

    lax.fori_loop(0, OWNERS, fill, 0, unroll=8)


def place_kernel(solid_ref, got_ref, z_ref, first_ref, last_ref, from_ref, origin_ref, sem):
    lane = lax.broadcasted_iota(jnp.int32, (OWNERS, B), 1)
    slot = (lax.broadcasted_iota(jnp.int32, (OWNERS, B), 0) << 2).astype(F32)
    numbers = got_ref[:, ID_ROW, :].astype(jnp.int32)
    origin = jnp.zeros((OWNERS, B), F32)
    for place in range(PER_PAIR):
        origin = origin + jnp.where(numbers[:, place : place + 1] == lane, slot + place, 0.0)
    origin_ref[...] = jnp.broadcast_to(jnp.sum(origin, axis=0, keepdims=True), (8, B)).astype(jnp.int32)
    copy = pltpu.make_async_copy(origin_ref.at[pl.ds(0, 1)], from_ref, sem)
    copy.start()
    copy.wait()

    def line(x, carry):
        rows = pl.ds(pl.multiple_of(x * BR, BR), BR)
        for y in range(N // B):
            cols = pl.ds(y * B, B)
            held = from_ref[0, x * (N // B) + y]
            source, place = held >> 2, held & 3
            fluid = (1 - solid_ref[x * (N // B) + y]).astype(F32)
            at = pl.multiple_of(place * BRICK_ROWS, BR)
            z_ref[0, rows, cols] = got_ref[source, pl.ds(at, BR)]
            z_ref[1, rows, cols] = got_ref[source, pl.ds(at + 2 * BR, BR)] * fluid
        return carry

    lax.fori_loop(0, XL // BR, line, 0)
    for ref, row, end in ((first_ref, 0, 0), (last_ref, XL - 1, 1)):
        ref[0:1] = z_ref[1, row : row + 1]
        for y in range(N // B):
            held = from_ref[0, row // BR * (N // B) + y]
            ref[1:2, y * B : (y + 1) * B] = got_ref[held >> 2, pl.ds(END_ROW + end + 2 * (held & 3), 1)]


def place_rest_kernel(solid_ref, from_ref, got_ref, source_ref, ends_ref, sides_ref):
    lane = lax.broadcasted_iota(jnp.int32, (BR, B), 1)
    row = lax.broadcasted_iota(jnp.int32, (BR, B), 0)

    def line(x, carry):
        rows = pl.ds(pl.multiple_of(x * BR, BR), BR)
        for y in range(N // B):
            cols = pl.ds(y * B, B)
            held = from_ref[0, x * (N // B) + y]
            source, place = held >> 2, held & 3
            fluid = (1 - solid_ref[x * (N // B) + y]).astype(F32)
            at = pl.multiple_of(place * BRICK_ROWS, BR)
            source_ref[rows, cols] = got_ref[source, pl.ds(at + BR, BR)] * fluid
            sides = jnp.broadcast_to(got_ref[source, SIDE_ROW : SIDE_ROW + 1], (BR, B))
            own = lane - row - 2 * BR * place
            low = jnp.sum(jnp.where(own == 0, sides, 0.0), axis=1, keepdims=True)
            high = jnp.sum(jnp.where(own == BR, sides, 0.0), axis=1, keepdims=True)
            sides_ref[rows, cols] = jnp.where(lane == 0, low, high)
            first = got_ref[source, pl.ds(END_ROW + 2 * place, 1)]
            last = got_ref[source, pl.ds(END_ROW + 1 + 2 * place, 1)]
            ends_ref[rows, cols] = jnp.where(row < BR // 2, first, last)
        return carry

    lax.fori_loop(0, XL // BR, line, 0)


def prepare_kernel(
    z_ref, inner_ref, x_ends_ref, sides_ref, column_ref, lam_ref, beside_ref, source_ref, inverse_ref, ext_ref
):
    ext_ref[7:8] = jnp.zeros((1, N), F32)
    ext_ref[XL + 8 : XL + 9] = jnp.zeros((1, N), F32)
    ext_ref[8 : XL + 8] = z_ref[1]
    lane = lax.broadcasted_iota(jnp.int32, (8, N), 1)
    brick_end = ((lane & (B - 1)) == B - 1) & (lane < N - 1)
    for i in range(XL // 8):
        rows = pl.ds(8 * i, 8)
        root, side = z_ref[1, rows], sides_ref[rows]
        after = pltpu.roll(root, N - 1, 1)
        beside = SHIFT_RATE * root + ext_ref[pl.ds(8 * i + 9, 8)] + ext_ref[pl.ds(8 * i + 7, 8)]
        beside = beside + jnp.where(lane < N - 1, after, 0.0) + jnp.where(lane > 0, pltpu.roll(root, 1, 1), 0.0)
        beside_ref[rows] = beside
        flux_y = jnp.where(brick_end, 0.5 * root * after * (side + pltpu.roll(side, N - 1, 1)), 0.0)
        source_ref[rows] = inner_ref[rows] + pltpu.roll(flux_y, 1, 1) - flux_y
        inverse_ref[rows] = 1.0 / (column_ref[rows, 0:1] + lam_ref[...])
    for x in range(BR, XL, BR):
        flux = 0.5 * ext_ref[x + 7 : x + 8] * ext_ref[x + 8 : x + 9] * (x_ends_ref[x - 1 : x] + x_ends_ref[x : x + 1])
        source_ref[x - 1 : x] = source_ref[x - 1 : x] - flux
        source_ref[x : x + 1] = source_ref[x : x + 1] + flux


def setup_kernel(
    place_ref, z_ref, beside_ref, inner_ref, x_ends_ref, partner_ref, outer_ref, xlo_ref, xhi_ref,
    even_ref, odd_ref, small_ref, column_ref, inverse_ref,
    diagonal_ref, source_ref, modes_ref, ends_ref, fold_ref,
):
    sign = (2 * place_ref[1] - 1).astype(F32)
    for i in range(XL // 8):
        rows = pl.ds(8 * i, 8)
        accel_z, root = z_ref[0, rows], z_ref[1, rows]
        root_p, root_o = partner_ref[1, rows], outer_ref[1, rows]
        diagonal_ref[rows] = root * (beside_ref[rows] + root_p + root_o) + jnp.where(root > 0.0, 0.0, 1.0)
        flux = root_p * (partner_ref[0, rows] + accel_z) - root_o * (accel_z + outer_ref[0, rows])
        source_ref[rows] = inner_ref[rows] + (0.5 * sign) * (root * flux)
    for at, rim_ref, sign in ((0, xlo_ref, 1.0), (XL - 1, xhi_ref, -1.0)):
        row = pl.ds(at, 1)
        face = z_ref[1, row] * rim_ref[0:1]
        diagonal_ref[row] = diagonal_ref[row] + face
        source_ref[row] = source_ref[row] + (0.5 * sign) * face * (x_ends_ref[row] + rim_ref[1:2])
    to_modes(source_ref, even_ref, odd_ref, small_ref, column_ref, inverse_ref, fold_ref, modes_ref, ends_ref)


def update_kernel(
    place_ref, modes_ref, all_ends_ref, z_ref, xlo_ref, xhi_ref, cut_ref, near_far_ref, even_ref, odd_ref,
    small_t_ref, column_ref, inverse_ref, update_ref, scaled_ref, rim_ref, work_ref,
):
    slab = place_ref[0]

    steps = [all_ends_ref[j, 8:16] - all_ends_ref[j + 1, 0:8] for j in range(SLABS - 1)]

    def jump(cut):
        at = jnp.clip(cut, 0, SLABS - 2)
        total = jnp.zeros((8, 128), F32)
        for j, step in enumerate(steps):
            total = total + cut_ref[at, j] * step
        return jnp.where(at == cut, total, 0.0)

    farther_low, low, high, farther_high = (jump(slab + m) for m in (-2, -1, 0, 1))
    near, far = near_far_ref[0], near_far_ref[1]
    before = all_ends_ref[jnp.maximum(slab - 1, 0), 8:16] - (near * low - far * farther_low)
    after = all_ends_ref[jnp.minimum(slab + 1, SLABS - 1), 0:8] - (far * farther_high - near * high)
    low_row, high_row = as_row(low), as_row(high)
    odd = (lax.broadcasted_iota(jnp.int32, (8, N), 0) & 1) == 1
    jumps = jnp.where(odd, -high_row, high_row) - low_row
    for i in range(XL // 8):
        rows = pl.ds(8 * i, 8)
        work_ref[rows] = modes_ref[rows] - column_ref[rows, 1:2] * jumps * inverse_ref[rows]
    work_ref[0:XL] = of_table(small_t_ref, work_ref[0:XL])
    work_ref[XL : XL + 8] = jnp.concatenate([as_row(before), as_row(after), jnp.zeros((6, N), F32)], axis=0)
    even = by_table(work_ref[:, :H], even_ref, False)
    odd = by_table(work_ref[:, H:], odd_ref, False)
    work_ref[:, :H] = even
    work_ref[:, H:] = odd
    for i in range(XL // 8 + 1):
        rows = pl.ds(8 * i, 8)
        even = work_ref[rows, :H]
        odd = work_ref[rows, H:]
        value = jnp.concatenate([even + odd, mirrored(even - odd)], axis=1)
        if i < XL // 8:
            root = z_ref[1, rows]
            update_ref[rows] = jnp.where(root > 0.0, value, 0.0)
            scaled_ref[rows] = root * value
        else:
            rim_ref[0:1] = value[0:1] * xlo_ref[0:1]
            rim_ref[1:2] = value[1:2] * xhi_ref[0:1]


def own_image(value_ref, scaled_ref, rim_ref, z_ref, diagonal_ref, ext_ref):
    ext_ref[7:8] = rim_ref[0:1]
    ext_ref[XL + 8 : XL + 9] = rim_ref[1:2]
    ext_ref[8 : XL + 8] = scaled_ref[...]
    lane = lax.broadcasted_iota(jnp.int32, (8, N), 1)
    for i in range(XL // 8):
        rows = pl.ds(8 * i, 8)
        scaled = scaled_ref[rows]
        beside = ext_ref[pl.ds(8 * i + 9, 8)] + ext_ref[pl.ds(8 * i + 7, 8)]
        beside = beside + jnp.where(lane < N - 1, pltpu.roll(scaled, N - 1, 1), 0.0)
        beside = beside + jnp.where(lane > 0, pltpu.roll(scaled, 1, 1), 0.0)
        yield rows, diagonal_ref[rows] * value_ref[rows] - z_ref[1, rows] * beside


def own_kernel(value_ref, scaled_ref, rim_ref, z_ref, diagonal_ref, own_ref, ext_ref):
    for rows, image in own_image(value_ref, scaled_ref, rim_ref, z_ref, diagonal_ref, ext_ref):
        own_ref[rows] = image


def image_kernel(
    own_ref, partner_ref, outer_ref, z_ref, even_ref, odd_ref, small_ref, column_ref, inverse_ref,
    image_ref, modes_ref, ends_ref, fold_ref,
):
    for i in range(XL // 8):
        rows = pl.ds(8 * i, 8)
        image_ref[rows] = own_ref[rows] - z_ref[1, rows] * (partner_ref[rows] + outer_ref[rows])
    to_modes(image_ref, even_ref, odd_ref, small_ref, column_ref, inverse_ref, fold_ref, modes_ref, ends_ref)


def one_line(total):
    line = jnp.sum(total, axis=0, keepdims=True)
    return sum(line[:, t * 128 : (t + 1) * 128] for t in range(8))


def own_sums_kernel(
    value_ref, scaled_ref, rim_ref, z_ref, diagonal_ref, source_ref, update_ref, first_image_ref,
    own_ref, lines_ref, ext_ref,
):
    totals = [jnp.zeros((8, N), F32) for _ in range(4)]
    for rows, image in own_image(value_ref, scaled_ref, rim_ref, z_ref, diagonal_ref, ext_ref):
        own_ref[rows] = image
        v, r, u, q = value_ref[rows], source_ref[rows], update_ref[rows], first_image_ref[rows]
        for k, (a, b) in enumerate(((r, u), (u, q), (r, v), (q, v))):
            totals[k] = totals[k] + a * b
    lines_ref[...] = jnp.concatenate([one_line(total) for total in totals] + [jnp.zeros((4, 128), F32)], axis=0)


def sums_kernel(
    value_ref, own_ref, lines_ref, partner_ref, outer_ref, z_ref, update_ref, image_ref, sums_ref
):
    totals = [jnp.zeros((8, N), F32) for _ in range(2)]
    for i in range(XL // 8):
        rows = pl.ds(8 * i, 8)
        t = own_ref[rows] - z_ref[1, rows] * (partner_ref[rows] + outer_ref[rows])
        image_ref[rows] = t
        totals[0] = totals[0] + update_ref[rows] * t
        totals[1] = totals[1] + value_ref[rows] * t
    lines = jnp.concatenate([lines_ref[0:4]] + [one_line(total) for total in totals] + [jnp.zeros((2, 128), F32)], axis=0)
    index = [lax.broadcasted_iota(jnp.int32, (8, 128), k) for k in range(2)]
    line = jnp.where(index[0] == index[1], jnp.sum(lines, axis=1, keepdims=True), 0.0)
    line = jnp.sum(line, axis=0, keepdims=True)
    for j in range(PEERS):
        sums_ref[j] = line


def add_kernel(sums_ref, out_ref):
    total = sums_ref[0]
    for j in range(1, PEERS):
        total = total + sums_ref[j]
    for j in range(PEERS):
        out_ref[j] = total


def final_kernel(
    sums_ref, source_ref, u_ref, q_ref, v_ref, t_ref, solution_hbm, residual_hbm, solution_ref, residual_ref, sem
):
    total = sums_ref[0]
    for j in range(1, PEERS):
        total = total + sums_ref[j]
    index = [lax.broadcasted_iota(jnp.int32, (8, 128), k) for k in range(2)]
    total = jnp.where(index[0] == index[1], jnp.broadcast_to(total, (8, 128)), 0.0)
    total = jnp.sum(total, axis=1, keepdims=True)
    ru, uq, rv, qv, ut, vt = (total[k : k + 1] for k in range(6))
    step = ru / uq
    energy = ru - step * (rv + uq) + step * step * qv
    beta = energy / ru
    cross = uq - step * ut
    curve = cross - step * qv + step * step * vt
    curve = curve + beta * (cross + uq - step * qv) + beta * beta * uq
    second = energy / curve
    spread = lambda s: jnp.broadcast_to(s, (8, N))
    step, beta, second = spread(step), spread(beta), spread(second)
    copies = []
    size = XL // CHUNKS
    for i in range(XL // 8):
        rows = pl.ds(8 * i, 8)
        u, q = u_ref[rows], q_ref[rows]
        direction = u - step * v_ref[rows] + beta * u
        along = q - step * t_ref[rows] + beta * q
        solution_ref[rows] = step * u + second * direction
        residual_ref[rows] = source_ref[rows] - step * q - second * along
        if (8 * i + 8) % size == 0:
            done = pl.ds(8 * i + 8 - size, size)
            for k, (ref, hbm) in enumerate(((solution_ref, solution_hbm), (residual_ref, residual_hbm))):
                copy = pltpu.make_async_copy(ref.at[done], hbm.at[done], sem.at[k, 8 * i // size])
                copy.start()
                copies.append(copy)
    for copy in copies:
        copy.wait()


def shape(*dims):
    return pltpu.VMEM(dims, F32)


def call(kernel, out_shape, in_specs, out_specs, scratch=(), name=None):
    run = pl.pallas_call(
        kernel, out_shape=out_shape, in_specs=in_specs, out_specs=out_specs, scratch_shapes=list(scratch), name=name,
        compiler_params=pltpu.CompilerParams(vmem_limit_bytes=16 * 2**20),
    )

    def with_spaces(*operands):
        assert len(operands) == len(in_specs)
        return run(
            *(
                x if spec is SMEM else pltpu.with_memory_space_constraint(x, spec.memory_space)
                for x, spec in zip(operands, in_specs)
            )
        )

    return with_spaces


PLANE = (XL, N)
EXT = pltpu.VMEM((XL + 16, N), F32)
FOLD = pltpu.VMEM(PLANE, F32)


def on_device(camera_accel, camera_weight, brick_slot, brick_solid):
    constant = {name: jnp.asarray(value) for name, value in tables().items()}
    dct = (constant["even"], constant["odd"])
    place = jnp.stack([lax.axis_index("gx"), lax.axis_index("yz_2")])
    slabs, owners = lax.axis_size("gx"), lax.axis_size(YZ)
    up_x = [(i, i + 1) for i in range(slabs - 1)]
    down_x = [(b, a) for a, b in up_x]
    on_chip = [(0, 1), (1, 0)]
    off_chip = [pair for i in range(1, owners - 1, 2) for pair in ((i, i + 1), (i + 1, i))]

    def neighbours(value):
        outer = lax.ppermute(value, YZ, off_chip)
        return lax.ppermute(value, "yz_2", on_chip), outer

    send = call(
        pack_kernel,
        shape(OWNERS, SEND_ROWS, 128),
        [SMEM, HBM, HBM, HBM],
        VMEM,
        [
            pltpu.SMEM((1, PLANE_BRICKS), jnp.int32),
            pltpu.SMEM((OWNERS,), jnp.int32),
            pltpu.SMEM((OWNERS * PER_PAIR,), jnp.int32),
            pltpu.SMEM((OWNERS * PER_PAIR,), jnp.int32),
            pltpu.VMEM((PLANE_BRICKS, 3 * BR, B), F32),
            pltpu.VMEM((PLANE_BRICKS, BR, B), F32),
            pltpu.VMEM((PLANE_BRICKS, BR, B), F32),
            pltpu.VMEM((PLANE_BRICKS // GROUP, 8, B), F32),
            pltpu.SemaphoreType.DMA((2, CHUNKS)),
            pltpu.SemaphoreType.DMA,
        ],
        name="pack",
    )(place, brick_slot, camera_accel[0].reshape(PLANE_BRICKS, 3 * BR, B), camera_weight[0])
    got = lax.all_to_all(send, YZ, split_axis=0, concat_axis=0, tiled=True)
    z_fields, first, last, origin = call(
        place_kernel,
        (shape(2, *PLANE), shape(2, N), shape(2, N), jax.ShapeDtypeStruct((1, B), jnp.int32)),
        [SMEM, VMEM],
        (VMEM,) * 3 + (SMEM,),
        [pltpu.VMEM((8, B), jnp.int32), pltpu.SemaphoreType.DMA],
        name="place",
    )(brick_solid[0], got)
    partner, outer = neighbours(z_fields)
    xlo = lax.ppermute(last, "gx", up_x)
    xhi = lax.ppermute(first, "gx", down_x)
    inner, x_ends, sides = call(
        place_rest_kernel, (shape(*PLANE),) * 3, [SMEM, SMEM, VMEM], (VMEM,) * 3, name="place_rest"
    )(brick_solid[0], origin, got)
    beside, inner, inverse = call(
        prepare_kernel, (shape(*PLANE),) * 3, [VMEM] * 6, (VMEM,) * 3, [EXT], name="prepare"
    )(z_fields, inner, x_ends, sides, constant["column"], constant["lam_y"])
    slab_tables = (constant["column"], inverse)
    forward = dct + (constant["small"],) + slab_tables
    diagonal, source, modes, ends = call(
        setup_kernel,
        (shape(*PLANE), shape(*PLANE), shape(*PLANE), shape(SLABS, 16, 128)),
        [SMEM] + [VMEM] * 13,
        (VMEM,) * 4,
        [FOLD],
        name="setup",
    )(place, z_fields, beside, inner, x_ends, partner, outer, xlo, xhi, *forward)

    def updated(modes, ends):
        all_ends = lax.all_to_all(ends, "gx", split_axis=0, concat_axis=0, tiled=True)
        return call(
            update_kernel,
            (shape(*PLANE), shape(*PLANE), shape(2, N)),
            [SMEM] + [VMEM] * 12,
            (VMEM,) * 3,
            [pltpu.VMEM((XL + 8, N), F32)],
            name="update",
        )(
            place, modes, all_ends, z_fields, xlo, xhi, constant["cut"], constant["ends"],
            *dct, constant["small_t"], *slab_tables,
        )

    u, scaled, rim = updated(modes, ends)
    planes = neighbours(scaled)
    own = call(own_kernel, shape(*PLANE), [VMEM] * 5, VMEM, [EXT], name="own")(u, scaled, rim, z_fields, diagonal)
    q, modes, ends = call(
        image_kernel,
        (shape(*PLANE), shape(*PLANE), shape(SLABS, 16, 128)),
        [VMEM] * 9,
        (VMEM,) * 3,
        [FOLD],
        name="image",
    )(own, *planes, z_fields, *forward)
    v, scaled, rim = updated(modes, ends)
    planes = neighbours(scaled)
    own, lines = call(
        own_sums_kernel, (shape(*PLANE), shape(8, 128)), [VMEM] * 8, (VMEM, VMEM), [EXT], name="own_sums"
    )(v, scaled, rim, z_fields, diagonal, source, u, q)
    t, sums = call(
        sums_kernel,
        (shape(*PLANE), shape(PEERS, 1, 128)),
        [VMEM] * 7,
        (VMEM, VMEM),
        name="sums",
    )(v, own, lines, *planes, z_fields, u)
    sums = lax.all_to_all(sums, ("gx", "yz_2"), split_axis=0, concat_axis=0, tiled=True)
    sums = call(add_kernel, shape(PEERS, 1, 128), [VMEM], VMEM, name="add")(sums)
    sums = lax.all_to_all(sums, ("yz_0", "yz_1"), split_axis=0, concat_axis=0, tiled=True)
    result, residual = call(
        final_kernel,
        (jax.ShapeDtypeStruct(PLANE, F32),) * 2,
        [VMEM] * 6,
        (HBM, HBM),
        [FOLD, FOLD, pltpu.SemaphoreType.DMA((2, CHUNKS))],
        name="final",
    )(sums, source, u, q, v, t)
    return result[None], residual[None]


def solution(mesh):
    finer = Mesh(mesh.devices.reshape(mesh.shape["gx"], 4, 4, 2), ("gx", "yz_0", "yz_1", "yz_2"))
    in_specs = (P("gx", YZ, None, None, None), P("gx", YZ, None, None), P("gx", YZ), P("gx", YZ))
    out_specs = (P(YZ, "gx", None), P(YZ, "gx", None))
    return jax.shard_map(
        on_device, mesh=finer, in_specs=in_specs, out_specs=out_specs, check_vma=False
    )
```

```python
import functools

import jax
import jax.numpy as jnp
import ml_dtypes
import numpy as np
from jax import lax
from jax.experimental import pallas as pl
from jax.experimental.pallas import tpu as pltpu
from jax.sharding import Mesh
from jax.sharding import PartitionSpec as P

N = 1024
H = N // 2
XL = 128
SLABS = 8
BR = 16
B = 128
PLANE_SHIFT = 6
PLANE_BRICKS = 1 << PLANE_SHIFT
OWNERS = 32
PEERS = 16
PER_PAIR = 3
BRICK_ROWS = 3 * BR
END_ROW = PER_PAIR * BRICK_ROWS
SIDE_ROW = END_ROW + 2 * PER_PAIR
ID_ROW = SIDE_ROW + 1
SEND_ROWS = END_ROW + 8
CHUNKS = 4
GROUP_SHIFT = 3
GROUP = 1 << GROUP_SHIFT
YZ = ("yz_0", "yz_1", "yz_2")
SHIFT_RATE = 0.05
FLOOR = 2.0
F32 = jnp.float32
BF16 = jnp.bfloat16
VMEM = pl.BlockSpec(memory_space=pltpu.VMEM)
SMEM = pl.BlockSpec(memory_space=pltpu.SMEM)
HBM = pl.BlockSpec(memory_space=pltpu.HBM)


def cosine_rows(length):
    k = np.arange(length, dtype=np.int64)[:, None]
    i = np.arange(length, dtype=np.int64)[None, :]
    m = (k * (2 * i + 1)) % (4 * length)
    scale = np.sqrt(np.where(k == 0, 1.0, 2.0) / length)
    return scale * np.cos(np.pi * m / (2.0 * length))


def two_bf16(table):
    high = table.astype(np.float32).astype(ml_dtypes.bfloat16)
    low = (table - high.astype(np.float64)).astype(np.float32).astype(ml_dtypes.bfloat16)
    return high, low


@functools.lru_cache(None)
def tables():
    out = {}
    big = cosine_rows(N)
    out["even"] = np.stack(two_bf16(big[0::2, :H]))
    out["odd"] = np.stack(two_bf16(big[1::2, :H]))
    small = cosine_rows(XL)
    out["small"] = np.concatenate(two_bf16(small), axis=0)
    out["small_t"] = np.concatenate(two_bf16(small.T.copy()), axis=0)
    lam_x = 2.0 - 2.0 * np.cos(np.pi * np.arange(XL) / XL)
    ky = np.concatenate([np.arange(0, N, 2), np.arange(1, N, 2)])
    lam_y = 2.0 - 2.0 * np.cos(np.pi * ky / N)
    column = np.zeros((XL, 128), np.float32)
    column[:, 0] = lam_x + FLOOR
    column[:, 1] = small[:, 0]
    out["column"] = column
    out["lam_y"] = lam_y.astype(np.float32)[None]
    denom = lam_x[:, None] + lam_y[None] + FLOOR
    near = np.sum(small[:, :1] ** 2 / denom, axis=0)
    far = np.sum(small[:, :1] * small[:, XL - 1 :] / denom, axis=0)
    cuts = SLABS - 1
    system = np.zeros((N, cuts, cuts))
    for j in range(cuts):
        system[:, j, j] = 1.0 + 2.0 * near
    for j in range(cuts - 1):
        system[:, j, j + 1] = -far
        system[:, j + 1, j] = -far
    inverse = np.linalg.inv(system)
    out["cut"] = inverse.transpose(1, 2, 0).astype(np.float32).reshape(cuts, cuts, 8, 128)
    out["ends"] = np.stack([near, far]).astype(np.float32).reshape(2, 8, 128)
    return out


def split(value):
    high = value.astype(BF16)
    return high, (value - high.astype(F32)).astype(BF16)


def product(a, b, transposed=False):
    dims = (((1,), (1 if transposed else 0,)), ((), ()))
    return lax.dot_general(a, b, dims, preferred_element_type=F32)


def by_table(data, table_ref, transposed):
    high, low = split(data)
    rows = data.shape[0]
    both = product(jnp.concatenate([high, low], axis=0), table_ref[0], transposed)
    return both[:rows] + both[rows:] + product(high, table_ref[1], transposed)


def of_table(table_ref, data):
    high, low = split(data)
    both = product(table_ref[...], high)
    return both[:XL] + both[XL:] + product(table_ref[:XL], low)


def mirrored(value):
    rows, width = value.shape
    index = 127 - lax.broadcasted_iota(jnp.int32, (rows, 128), 1)
    tiles = [
        jnp.take_along_axis(value[:, t * 128 : (t + 1) * 128], index, axis=1)
        for t in range(width // 128)
    ]
    return jnp.concatenate(tiles[::-1], axis=1)


def as_tile(row):
    return jnp.concatenate([row[:, t * 128 : (t + 1) * 128] for t in range(8)], axis=0)


def as_row(tile):
    return jnp.concatenate([tile[t : t + 1] for t in range(8)], axis=1)


def to_modes(field_ref, even_ref, odd_ref, small_ref, column_ref, inverse_ref, fold_ref, modes_ref, ends_ref):
    for i in range(XL // 8):
        rows = pl.ds(8 * i, 8)
        low = field_ref[rows, :H]
        high = mirrored(field_ref[rows, H:])
        fold_ref[rows, :H] = low + high
        fold_ref[rows, H:] = low - high
    spectrum = jnp.concatenate(
        [
            by_table(fold_ref[:, :H], even_ref, True),
            by_table(fold_ref[:, H:], odd_ref, True),
        ],
        axis=1,
    )
    modes_ref[...] = of_table(small_ref, spectrum)
    total = jnp.zeros((8, N), F32)
    for i in range(XL // 8):
        rows = pl.ds(8 * i, 8)
        modes = modes_ref[rows, :] * inverse_ref[rows]
        modes_ref[rows, :] = modes
        total = total + modes * column_ref[rows, 1:2]
    odd = (lax.broadcasted_iota(jnp.int32, (8, N), 0) & 1) == 1
    first = as_tile(jnp.sum(total, axis=0, keepdims=True))
    last = as_tile(jnp.sum(jnp.where(odd, -total, total), axis=0, keepdims=True))
    for j in range(SLABS):
        ends_ref[j, 0:8] = first
        ends_ref[j, 8:16] = last


def pack_kernel(
    place_ref, slot_hbm, accel_hbm, weight_hbm, out_ref,
    slot_ref, count_ref, held_ref, number_ref, accel_ref, weight_ref, inner_ref, side_ref, sem, slot_sem,
):
    del place_ref
    slot_copy = pltpu.make_async_copy(slot_hbm, slot_ref, slot_sem)
    slot_copy.start()
    size = PLANE_BRICKS // CHUNKS
    copies = []
    for chunk in range(CHUNKS):
        bricks = pl.ds(chunk * size, size)
        copies.append(
            (
                pltpu.make_async_copy(accel_hbm.at[bricks], accel_ref.at[bricks], sem.at[0, chunk]),
                pltpu.make_async_copy(weight_hbm.at[bricks], weight_ref.at[bricks], sem.at[1, chunk]),
            )
        )
        for copy in copies[-1]:
            copy.start()
    for o in range(OWNERS):
        count_ref[o] = 0
    for k in range(OWNERS * PER_PAIR):
        held_ref[k] = 0
        number_ref[k] = -1
    slot_copy.wait()

    def assign(s, carry):
        brick = slot_ref[0, s]
        owner = brick >> PLANE_SHIFT
        place = count_ref[owner]
        count_ref[owner] = place + 1
        held_ref[owner * PER_PAIR + place] = s
        number_ref[owner * PER_PAIR + place] = brick & (PLANE_BRICKS - 1)
        return carry

    lax.fori_loop(0, PLANE_BRICKS, assign, 0, unroll=8)
    dims = (GROUP, BR, B)
    lane = lax.broadcasted_iota(jnp.int32, dims, 2)
    row = lax.broadcasted_iota(jnp.int32, dims, 1)
    few_lanes, few_rows = lane[0, :8], row[0, :8]
    edge = jnp.where((few_rows == 0) & (few_lanes == 0), 1.0, 0.0)
    edge = jnp.where((few_rows == 1) & (few_lanes == B - 1), 1.0, edge).astype(BF16)

    def inside(group, carry):
        bricks = pl.ds(group * GROUP, GROUP)
        root = jnp.sqrt(weight_ref[bricks])
        weight_ref[bricks] = root
        accel_x = accel_ref[bricks, BR : 2 * BR]
        flux_x = root * pltpu.roll(root, BR - 1, 1) * (accel_x + pltpu.roll(accel_x, BR - 1, 1))
        flux_x = jnp.where(row < BR - 1, flux_x, 0.0)
        inner = pltpu.roll(flux_x, 1, 1) - flux_x
        accel_y = accel_ref[bricks, 2 * BR :]
        flux_y = root * pltpu.roll(root, B - 1, 2) * (accel_y + pltpu.roll(accel_y, B - 1, 2))
        flux_y = jnp.where(lane < B - 1, flux_y, 0.0)
        inner_ref[bricks] = 0.5 * (inner + pltpu.roll(flux_y, 1, 2) - flux_y)
        flat = accel_y.reshape(GROUP * BR, B)
        high, middle = split(flat)
        low = (flat - high.astype(F32) - middle.astype(F32)).astype(BF16)
        sides = product(edge, high, True) + product(edge, middle, True) + product(edge, low, True)
        side_ref[group] = jnp.where(few_rows == 1, pltpu.roll(sides, BR, 1), sides)
        return carry

    for chunk in range(CHUNKS):
        for copy in copies[chunk]:
            copy.wait()
        lax.fori_loop(chunk * size // GROUP, (chunk + 1) * size // GROUP, inside, 0, unroll=2)

    def fill(owner, carry):
        ends = jnp.zeros((8, B), F32)
        for place in range(PER_PAIR):
            s = held_ref[owner * PER_PAIR + place]
            number = number_ref[owner * PER_PAIR + place].astype(F32)
            at = place * BRICK_ROWS
            out_ref[owner, at : at + BR] = accel_ref[s, :BR]
            out_ref[owner, at + BR : at + 2 * BR] = inner_ref[s]
            out_ref[owner, at + 2 * BR : at + 3 * BR] = weight_ref[s]
            ends = jnp.where(few_rows == 2 * place, accel_ref[s, BR : BR + 1], ends)
            ends = jnp.where(few_rows == 2 * place + 1, accel_ref[s, 2 * BR - 1 : 2 * BR], ends)
            sides = pltpu.roll(side_ref[s >> GROUP_SHIFT], (2 * BR * place - BR * (s & (GROUP - 1))) & (B - 1), 1)
            sides = jnp.where(few_lanes < 2 * BR * place + BR, sides[0:1], sides[1:2])
            ends = jnp.where((few_rows == SIDE_ROW - END_ROW) & (few_lanes >= 2 * BR * place), sides, ends)
            ends = jnp.where((few_rows == ID_ROW - END_ROW) & (few_lanes == place), number, ends)
        out_ref[owner, END_ROW:] = ends
        return carry

    lax.fori_loop(0, OWNERS, fill, 0, unroll=8)


def place_kernel(solid_ref, got_ref, z_ref, first_ref, last_ref, from_ref, origin_ref, sem):
    lane = lax.broadcasted_iota(jnp.int32, (OWNERS, B), 1)
    slot = (lax.broadcasted_iota(jnp.int32, (OWNERS, B), 0) << 2).astype(F32)
    numbers = got_ref[:, ID_ROW, :].astype(jnp.int32)
    origin = jnp.zeros((OWNERS, B), F32)
    for place in range(PER_PAIR):
        origin = origin + jnp.where(numbers[:, place : place + 1] == lane, slot + place, 0.0)
    origin_ref[...] = jnp.broadcast_to(jnp.sum(origin, axis=0, keepdims=True), (8, B)).astype(jnp.int32)
    copy = pltpu.make_async_copy(origin_ref.at[pl.ds(0, 1)], from_ref, sem)
    copy.start()
    copy.wait()

    def line(x, carry):
        rows = pl.ds(pl.multiple_of(x * BR, BR), BR)
        for y in range(N // B):
            cols = pl.ds(y * B, B)
            held = from_ref[0, x * (N // B) + y]
            source, place = held >> 2, held & 3
            fluid = (1 - solid_ref[x * (N // B) + y]).astype(F32)
            at = pl.multiple_of(place * BRICK_ROWS, BR)
            z_ref[0, rows, cols] = got_ref[source, pl.ds(at, BR)]
            z_ref[1, rows, cols] = got_ref[source, pl.ds(at + 2 * BR, BR)] * fluid
        return carry

    lax.fori_loop(0, XL // BR, line, 0, unroll=4)
    for ref, row, end in ((first_ref, 0, 0), (last_ref, XL - 1, 1)):
        ref[0:1] = z_ref[1, row : row + 1]
        for y in range(N // B):
            held = from_ref[0, row // BR * (N // B) + y]
            ref[1:2, y * B : (y + 1) * B] = got_ref[held >> 2, pl.ds(END_ROW + end + 2 * (held & 3), 1)]


def place_rest_kernel(solid_ref, from_ref, got_ref, source_ref, ends_ref, sides_ref):
    lane = lax.broadcasted_iota(jnp.int32, (BR, B), 1)
    row = lax.broadcasted_iota(jnp.int32, (BR, B), 0)

    def line(x, carry):
        rows = pl.ds(pl.multiple_of(x * BR, BR), BR)
        for y in range(N // B):
            cols = pl.ds(y * B, B)
            held = from_ref[0, x * (N // B) + y]
            source, place = held >> 2, held & 3
            fluid = (1 - solid_ref[x * (N // B) + y]).astype(F32)
            at = pl.multiple_of(place * BRICK_ROWS, BR)
            source_ref[rows, cols] = got_ref[source, pl.ds(at + BR, BR)] * fluid
            sides = jnp.broadcast_to(got_ref[source, SIDE_ROW : SIDE_ROW + 1], (BR, B))
            own = lane - row - 2 * BR * place
            low = jnp.sum(jnp.where(own == 0, sides, 0.0), axis=1, keepdims=True)
            high = jnp.sum(jnp.where(own == BR, sides, 0.0), axis=1, keepdims=True)
            sides_ref[rows, cols] = jnp.where(lane == 0, low, high)
            first = got_ref[source, pl.ds(END_ROW + 2 * place, 1)]
            last = got_ref[source, pl.ds(END_ROW + 1 + 2 * place, 1)]
            ends_ref[rows, cols] = jnp.where(row < BR // 2, first, last)
        return carry

    lax.fori_loop(0, XL // BR, line, 0)


def prepare_kernel(
    z_ref, inner_ref, x_ends_ref, sides_ref, column_ref, lam_ref, beside_ref, source_ref, inverse_ref, ext_ref
):
    ext_ref[7:8] = jnp.zeros((1, N), F32)
    ext_ref[XL + 8 : XL + 9] = jnp.zeros((1, N), F32)
    ext_ref[8 : XL + 8] = z_ref[1]
    lane = lax.broadcasted_iota(jnp.int32, (8, N), 1)
    brick_end = ((lane & (B - 1)) == B - 1) & (lane < N - 1)
    for i in range(XL // 8):
        rows = pl.ds(8 * i, 8)
        root, side = z_ref[1, rows], sides_ref[rows]
        after = pltpu.roll(root, N - 1, 1)
        beside = SHIFT_RATE * root + ext_ref[pl.ds(8 * i + 9, 8)] + ext_ref[pl.ds(8 * i + 7, 8)]
        beside = beside + jnp.where(lane < N - 1, after, 0.0) + jnp.where(lane > 0, pltpu.roll(root, 1, 1), 0.0)
        beside_ref[rows] = beside
        flux_y = jnp.where(brick_end, 0.5 * root * after * (side + pltpu.roll(side, N - 1, 1)), 0.0)
        source_ref[rows] = inner_ref[rows] + pltpu.roll(flux_y, 1, 1) - flux_y
        inverse_ref[rows] = 1.0 / (column_ref[rows, 0:1] + lam_ref[...])
    for x in range(BR, XL, BR):
        flux = 0.5 * ext_ref[x + 7 : x + 8] * ext_ref[x + 8 : x + 9] * (x_ends_ref[x - 1 : x] + x_ends_ref[x : x + 1])
        source_ref[x - 1 : x] = source_ref[x - 1 : x] - flux
        source_ref[x : x + 1] = source_ref[x : x + 1] + flux


def setup_kernel(
    place_ref, z_ref, beside_ref, inner_ref, x_ends_ref, partner_ref, outer_ref, xlo_ref, xhi_ref,
    even_ref, odd_ref, small_ref, column_ref, inverse_ref,
    diagonal_ref, source_ref, modes_ref, ends_ref, fold_ref,
):
    sign = (2 * place_ref[1] - 1).astype(F32)
    for i in range(XL // 8):
        rows = pl.ds(8 * i, 8)
        accel_z, root = z_ref[0, rows], z_ref[1, rows]
        root_p, root_o = partner_ref[1, rows], outer_ref[1, rows]
        diagonal_ref[rows] = root * (beside_ref[rows] + root_p + root_o) + jnp.where(root > 0.0, 0.0, 1.0)
        flux = root_p * (partner_ref[0, rows] + accel_z) - root_o * (accel_z + outer_ref[0, rows])
        source_ref[rows] = inner_ref[rows] + (0.5 * sign) * (root * flux)
    for at, rim_ref, sign in ((0, xlo_ref, 1.0), (XL - 1, xhi_ref, -1.0)):
        row = pl.ds(at, 1)
        face = z_ref[1, row] * rim_ref[0:1]
        diagonal_ref[row] = diagonal_ref[row] + face
        source_ref[row] = source_ref[row] + (0.5 * sign) * face * (x_ends_ref[row] + rim_ref[1:2])
    to_modes(source_ref, even_ref, odd_ref, small_ref, column_ref, inverse_ref, fold_ref, modes_ref, ends_ref)


def update_kernel(
    place_ref, modes_ref, all_ends_ref, z_ref, xlo_ref, xhi_ref, cut_ref, near_far_ref, even_ref, odd_ref,
    small_t_ref, column_ref, inverse_ref, update_ref, scaled_ref, rim_ref, work_ref,
):
    slab = place_ref[0]

    steps = [all_ends_ref[j, 8:16] - all_ends_ref[j + 1, 0:8] for j in range(SLABS - 1)]

    def jump(cut):
        at = jnp.clip(cut, 0, SLABS - 2)
        total = jnp.zeros((8, 128), F32)
        for j, step in enumerate(steps):
            total = total + cut_ref[at, j] * step
        return jnp.where(at == cut, total, 0.0)

    farther_low, low, high, farther_high = (jump(slab + m) for m in (-2, -1, 0, 1))
    near, far = near_far_ref[0], near_far_ref[1]
    before = all_ends_ref[jnp.maximum(slab - 1, 0), 8:16] - (near * low - far * farther_low)
    after = all_ends_ref[jnp.minimum(slab + 1, SLABS - 1), 0:8] - (far * farther_high - near * high)
    low_row, high_row = as_row(low), as_row(high)
    odd = (lax.broadcasted_iota(jnp.int32, (8, N), 0) & 1) == 1
    jumps = jnp.where(odd, -high_row, high_row) - low_row
    for i in range(XL // 8):
        rows = pl.ds(8 * i, 8)
        work_ref[rows] = modes_ref[rows] - column_ref[rows, 1:2] * jumps * inverse_ref[rows]
    work_ref[0:XL] = of_table(small_t_ref, work_ref[0:XL])
    work_ref[XL : XL + 8] = jnp.concatenate([as_row(before), as_row(after), jnp.zeros((6, N), F32)], axis=0)
    even = by_table(work_ref[:, :H], even_ref, False)
    odd = by_table(work_ref[:, H:], odd_ref, False)
    work_ref[:, :H] = even
    work_ref[:, H:] = odd
    for i in range(XL // 8 + 1):
        rows = pl.ds(8 * i, 8)
        even = work_ref[rows, :H]
        odd = work_ref[rows, H:]
        value = jnp.concatenate([even + odd, mirrored(even - odd)], axis=1)
        if i < XL // 8:
            root = z_ref[1, rows]
            update_ref[rows] = jnp.where(root > 0.0, value, 0.0)
            scaled_ref[rows] = root * value
        else:
            rim_ref[0:1] = value[0:1] * xlo_ref[0:1]
            rim_ref[1:2] = value[1:2] * xhi_ref[0:1]


def own_image(value_ref, scaled_ref, rim_ref, z_ref, diagonal_ref, ext_ref):
    ext_ref[7:8] = rim_ref[0:1]
    ext_ref[XL + 8 : XL + 9] = rim_ref[1:2]
    ext_ref[8 : XL + 8] = scaled_ref[...]
    lane = lax.broadcasted_iota(jnp.int32, (8, N), 1)
    for i in range(XL // 8):
        rows = pl.ds(8 * i, 8)
        scaled = scaled_ref[rows]
        beside = ext_ref[pl.ds(8 * i + 9, 8)] + ext_ref[pl.ds(8 * i + 7, 8)]
        beside = beside + jnp.where(lane < N - 1, pltpu.roll(scaled, N - 1, 1), 0.0)
        beside = beside + jnp.where(lane > 0, pltpu.roll(scaled, 1, 1), 0.0)
        yield rows, diagonal_ref[rows] * value_ref[rows] - z_ref[1, rows] * beside


def own_kernel(value_ref, scaled_ref, rim_ref, z_ref, diagonal_ref, own_ref, ext_ref):
    for rows, image in own_image(value_ref, scaled_ref, rim_ref, z_ref, diagonal_ref, ext_ref):
        own_ref[rows] = image


def image_kernel(
    own_ref, partner_ref, outer_ref, z_ref, even_ref, odd_ref, small_ref, column_ref, inverse_ref,
    image_ref, modes_ref, ends_ref, fold_ref,
):
    for i in range(XL // 8):
        rows = pl.ds(8 * i, 8)
        image_ref[rows] = own_ref[rows] - z_ref[1, rows] * (partner_ref[rows] + outer_ref[rows])
    to_modes(image_ref, even_ref, odd_ref, small_ref, column_ref, inverse_ref, fold_ref, modes_ref, ends_ref)


def one_line(total):
    line = jnp.sum(total, axis=0, keepdims=True)
    return sum(line[:, t * 128 : (t + 1) * 128] for t in range(8))


def own_sums_kernel(
    value_ref, scaled_ref, rim_ref, z_ref, diagonal_ref, source_ref, update_ref, first_image_ref,
    own_ref, lines_ref, ext_ref,
):
    totals = [jnp.zeros((8, N), F32) for _ in range(4)]
    for rows, image in own_image(value_ref, scaled_ref, rim_ref, z_ref, diagonal_ref, ext_ref):
        own_ref[rows] = image
        v, r, u, q = value_ref[rows], source_ref[rows], update_ref[rows], first_image_ref[rows]
        for k, (a, b) in enumerate(((r, u), (u, q), (r, v), (q, v))):
            totals[k] = totals[k] + a * b
    lines_ref[...] = jnp.concatenate([one_line(total) for total in totals] + [jnp.zeros((4, 128), F32)], axis=0)


def sums_kernel(
    value_ref, own_ref, lines_ref, partner_ref, outer_ref, z_ref, update_ref, image_ref, sums_ref
):
    totals = [jnp.zeros((8, N), F32) for _ in range(2)]
    for i in range(XL // 8):
        rows = pl.ds(8 * i, 8)
        t = own_ref[rows] - z_ref[1, rows] * (partner_ref[rows] + outer_ref[rows])
        image_ref[rows] = t
        totals[0] = totals[0] + update_ref[rows] * t
        totals[1] = totals[1] + value_ref[rows] * t
    lines = jnp.concatenate([lines_ref[0:4]] + [one_line(total) for total in totals] + [jnp.zeros((2, 128), F32)], axis=0)
    index = [lax.broadcasted_iota(jnp.int32, (8, 128), k) for k in range(2)]
    line = jnp.where(index[0] == index[1], jnp.sum(lines, axis=1, keepdims=True), 0.0)
    line = jnp.sum(line, axis=0, keepdims=True)
    for j in range(PEERS):
        sums_ref[j] = line


def add_kernel(sums_ref, out_ref):
    total = sums_ref[0]
    for j in range(1, PEERS):
        total = total + sums_ref[j]
    for j in range(PEERS):
        out_ref[j] = total


def final_kernel(
    sums_ref, source_ref, u_ref, q_ref, v_ref, t_ref, solution_hbm, residual_hbm, solution_ref, residual_ref, sem
):
    total = sums_ref[0]
    for j in range(1, PEERS):
        total = total + sums_ref[j]
    index = [lax.broadcasted_iota(jnp.int32, (8, 128), k) for k in range(2)]
    total = jnp.where(index[0] == index[1], jnp.broadcast_to(total, (8, 128)), 0.0)
    total = jnp.sum(total, axis=1, keepdims=True)
    ru, uq, rv, qv, ut, vt = (total[k : k + 1] for k in range(6))
    step = ru / uq
    energy = ru - step * (rv + uq) + step * step * qv
    beta = energy / ru
    cross = uq - step * ut
    curve = cross - step * qv + step * step * vt
    curve = curve + beta * (cross + uq - step * qv) + beta * beta * uq
    second = energy / curve
    spread = lambda s: jnp.broadcast_to(s, (8, N))
    step, beta, second = spread(step), spread(beta), spread(second)
    copies = []
    size = XL // CHUNKS
    for i in range(XL // 8):
        rows = pl.ds(8 * i, 8)
        u, q = u_ref[rows], q_ref[rows]
        direction = u - step * v_ref[rows] + beta * u
        along = q - step * t_ref[rows] + beta * q
        solution_ref[rows] = step * u + second * direction
        residual_ref[rows] = source_ref[rows] - step * q - second * along
        if (8 * i + 8) % size == 0:
            done = pl.ds(8 * i + 8 - size, size)
            for k, (ref, hbm) in enumerate(((solution_ref, solution_hbm), (residual_ref, residual_hbm))):
                copy = pltpu.make_async_copy(ref.at[done], hbm.at[done], sem.at[k, 8 * i // size])
                copy.start()
                copies.append(copy)
    for copy in copies:
        copy.wait()


def shape(*dims):
    return pltpu.VMEM(dims, F32)


def call(kernel, out_shape, in_specs, out_specs, scratch=(), name=None):
    run = pl.pallas_call(
        kernel, out_shape=out_shape, in_specs=in_specs, out_specs=out_specs, scratch_shapes=list(scratch), name=name,
        compiler_params=pltpu.CompilerParams(vmem_limit_bytes=16 * 2**20),
    )

    def with_spaces(*operands):
        assert len(operands) == len(in_specs)
        return run(
            *(
                x if spec is SMEM else pltpu.with_memory_space_constraint(x, spec.memory_space)
                for x, spec in zip(operands, in_specs)
            )
        )

    return with_spaces


PLANE = (XL, N)
EXT = pltpu.VMEM((XL + 16, N), F32)
FOLD = pltpu.VMEM(PLANE, F32)


def on_device(camera_accel, camera_weight, brick_slot, brick_solid):
    constant = {name: jnp.asarray(value) for name, value in tables().items()}
    dct = (constant["even"], constant["odd"])
    place = jnp.stack([lax.axis_index("gx"), lax.axis_index("yz_2")])
    slabs, owners = lax.axis_size("gx"), lax.axis_size(YZ)
    up_x = [(i, i + 1) for i in range(slabs - 1)]
    down_x = [(b, a) for a, b in up_x]
    on_chip = [(0, 1), (1, 0)]
    off_chip = [pair for i in range(1, owners - 1, 2) for pair in ((i, i + 1), (i + 1, i))]

    def neighbours(value):
        outer = lax.ppermute(value, YZ, off_chip)
        return lax.ppermute(value, "yz_2", on_chip), outer

    send = call(
        pack_kernel,
        shape(OWNERS, SEND_ROWS, 128),
        [SMEM, HBM, HBM, HBM],
        VMEM,
        [
            pltpu.SMEM((1, PLANE_BRICKS), jnp.int32),
            pltpu.SMEM((OWNERS,), jnp.int32),
            pltpu.SMEM((OWNERS * PER_PAIR,), jnp.int32),
            pltpu.SMEM((OWNERS * PER_PAIR,), jnp.int32),
            pltpu.VMEM((PLANE_BRICKS, 3 * BR, B), F32),
            pltpu.VMEM((PLANE_BRICKS, BR, B), F32),
            pltpu.VMEM((PLANE_BRICKS, BR, B), F32),
            pltpu.VMEM((PLANE_BRICKS // GROUP, 8, B), F32),
            pltpu.SemaphoreType.DMA((2, CHUNKS)),
            pltpu.SemaphoreType.DMA,
        ],
        name="pack",
    )(place, brick_slot, camera_accel[0].reshape(PLANE_BRICKS, 3 * BR, B), camera_weight[0])
    got = lax.all_to_all(send, YZ, split_axis=0, concat_axis=0, tiled=True)
    z_fields, first, last, origin = call(
        place_kernel,
        (shape(2, *PLANE), shape(2, N), shape(2, N), jax.ShapeDtypeStruct((1, B), jnp.int32)),
        [SMEM, VMEM],
        (VMEM,) * 3 + (SMEM,),
        [pltpu.VMEM((8, B), jnp.int32), pltpu.SemaphoreType.DMA],
        name="place",
    )(brick_solid[0], got)
    partner, outer = neighbours(z_fields)
    xlo = lax.ppermute(last, "gx", up_x)
    xhi = lax.ppermute(first, "gx", down_x)
    inner, x_ends, sides = call(
        place_rest_kernel, (shape(*PLANE),) * 3, [SMEM, SMEM, VMEM], (VMEM,) * 3, name="place_rest"
    )(brick_solid[0], origin, got)
    beside, inner, inverse = call(
        prepare_kernel, (shape(*PLANE),) * 3, [VMEM] * 6, (VMEM,) * 3, [EXT], name="prepare"
    )(z_fields, inner, x_ends, sides, constant["column"], constant["lam_y"])
    slab_tables = (constant["column"], inverse)
    forward = dct + (constant["small"],) + slab_tables
    diagonal, source, modes, ends = call(
        setup_kernel,
        (shape(*PLANE), shape(*PLANE), shape(*PLANE), shape(SLABS, 16, 128)),
        [SMEM] + [VMEM] * 13,
        (VMEM,) * 4,
        [FOLD],
        name="setup",
    )(place, z_fields, beside, inner, x_ends, partner, outer, xlo, xhi, *forward)

    def updated(modes, ends):
        all_ends = lax.all_to_all(ends, "gx", split_axis=0, concat_axis=0, tiled=True)
        return call(
            update_kernel,
            (shape(*PLANE), shape(*PLANE), shape(2, N)),
            [SMEM] + [VMEM] * 12,
            (VMEM,) * 3,
            [pltpu.VMEM((XL + 8, N), F32)],
            name="update",
        )(
            place, modes, all_ends, z_fields, xlo, xhi, constant["cut"], constant["ends"],
            *dct, constant["small_t"], *slab_tables,
        )

    u, scaled, rim = updated(modes, ends)
    planes = neighbours(scaled)
    own = call(own_kernel, shape(*PLANE), [VMEM] * 5, VMEM, [EXT], name="own")(u, scaled, rim, z_fields, diagonal)
    q, modes, ends = call(
        image_kernel,
        (shape(*PLANE), shape(*PLANE), shape(SLABS, 16, 128)),
        [VMEM] * 9,
        (VMEM,) * 3,
        [FOLD],
        name="image",
    )(own, *planes, z_fields, *forward)
    v, scaled, rim = updated(modes, ends)
    planes = neighbours(scaled)
    own, lines = call(
        own_sums_kernel, (shape(*PLANE), shape(8, 128)), [VMEM] * 8, (VMEM, VMEM), [EXT], name="own_sums"
    )(v, scaled, rim, z_fields, diagonal, source, u, q)
    t, sums = call(
        sums_kernel,
        (shape(*PLANE), shape(PEERS, 1, 128)),
        [VMEM] * 7,
        (VMEM, VMEM),
        name="sums",
    )(v, own, lines, *planes, z_fields, u)
    sums = lax.all_to_all(sums, ("gx", "yz_2"), split_axis=0, concat_axis=0, tiled=True)
    sums = call(add_kernel, shape(PEERS, 1, 128), [VMEM], VMEM, name="add")(sums)
    sums = lax.all_to_all(sums, ("yz_0", "yz_1"), split_axis=0, concat_axis=0, tiled=True)
    result, residual = call(
        final_kernel,
        (jax.ShapeDtypeStruct(PLANE, F32),) * 2,
        [VMEM] * 6,
        (HBM, HBM),
        [FOLD, FOLD, pltpu.SemaphoreType.DMA((2, CHUNKS))],
        name="final",
    )(sums, source, u, q, v, t)
    return result[None], residual[None]


def solution(mesh):
    finer = Mesh(mesh.devices.reshape(mesh.shape["gx"], 4, 4, 2), ("gx", "yz_0", "yz_1", "yz_2"))
    in_specs = (P("gx", YZ, None, None, None), P("gx", YZ, None, None), P("gx", YZ), P("gx", YZ))
    out_specs = (P(YZ, "gx", None), P(YZ, "gx", None))
    return jax.shard_map(
        on_device, mesh=finer, in_specs=in_specs, out_specs=out_specs, check_vma=False
    )
```
